32 devices in a mesh: batch: 8 (over y, x, core), grp: 4 (over z).
Axes of the slice: x: 2, y: 2, z: 4, core: 2. Of those that a mesh axis runs over, the one named last changes fastest.
Arguments:
- latents: bfloat16 [16, 32, 32, 768], P('batch', 'grp'), may hold values from -6 to 6
- cotangent: bfloat16 [16, 32, 32, 768], P('batch', 'grp'), may hold values from -6 to 6
- timesteps: int32 [16], P('batch'), may hold values from 0 to 999, as said below
- labels: int32 [16], P('batch'), may hold values from 0 to 999
- time_weight: bfloat16 [256, 768], replicated, may hold values from -0.375 to 0.375
- time_bias: bfloat16 [1, 768], replicated, may hold values from -3 to 3
- label_table: bfloat16 [1000, 768], replicated, may hold values from -6 to 6
- ada_weight: bfloat16 [768, 4608], replicated, may hold values from -0.21875 to 0.21875
- ada_bias: bfloat16 [1, 4608], replicated, may hold values from -3 to 3
- conv_a: bfloat16 [9, 768], replicated, may hold values from -2 to 2
- conv_a_bias: bfloat16 [1, 768], replicated, may hold values from -3 to 3
- qkv_weight: bfloat16 [768, 2304], replicated, may hold values from -0.21875 to 0.21875
- qv_bias: bfloat16 [2, 768], replicated, may hold values from -3 to 3
- proj_weight: bfloat16 [768, 768], replicated, may hold values from -0.875 to 0.875
- proj_bias: bfloat16 [1, 768], replicated, may hold values from -3 to 3
- fc1_weight: bfloat16 [768, 3072], replicated, may hold values from -0.21875 to 0.21875
- fc1_bias: bfloat16 [1, 3072], replicated, may hold values from -3 to 3
- conv_f: bfloat16 [9, 3072], replicated, may hold values from -2 to 2
- conv_f_bias: bfloat16 [1, 3072], replicated, may hold values from -3 to 3
- fc2_weight: bfloat16 [3072, 768], replicated, may hold values from -0.109375 to 0.109375
- fc2_bias: bfloat16 [1, 768], replicated, may hold values from -3 to 3
Outputs:
- output: bfloat16 [16, 32, 32, 768], P('batch', 'grp')
- latents_grad: bfloat16 [16, 32, 32, 768], P('batch', 'grp')
- time_weight_grad: float32 [256, 768], P(None, ('batch', 'grp'))
- time_bias_grad: float32 [1, 768], P(None, ('batch', 'grp'))
- label_table_grad: float32 [1000, 768], P(None, ('batch', 'grp'))
- ada_weight_grad: float32 [768, 4608], P(None, ('batch', 'grp'))
- ada_bias_grad: float32 [1, 4608], P(None, ('batch', 'grp'))
- conv_a_grad: float32 [9, 768], P(None, ('batch', 'grp'))
- conv_a_bias_grad: float32 [1, 768], P(None, ('batch', 'grp'))
- qkv_weight_grad: float32 [768, 2304], P(None, ('batch', 'grp'))
- qv_bias_grad: float32 [2, 768], P(None, ('batch', 'grp'))
- proj_weight_grad: float32 [768, 768], P(None, ('batch', 'grp'))
- proj_bias_grad: float32 [1, 768], P(None, ('batch', 'grp'))
- fc1_weight_grad: float32 [768, 3072], P(None, ('batch', 'grp'))
- fc1_bias_grad: float32 [1, 3072], P(None, ('batch', 'grp'))
- conv_f_grad: float32 [9, 3072], P(None, ('batch', 'grp'))
- conv_f_bias_grad: float32 [1, 3072], P(None, ('batch', 'grp'))
- fc2_weight_grad: float32 [3072, 768], P(None, ('batch', 'grp'))
- fc2_bias_grad: float32 [1, 768], P(None, ('batch', 'grp'))
The draws below stay inside these ranges and needn't reach their ends.
Inputs may be any that keep to these rules, and one draw needn't show every extreme that they name: `timesteps`: diffusion timestep of each latent, more often low than high; some latent has timestep 999 and some has 0.
All inputs are finite; a program needn't handle non-finite values.
Results may differ from the reference program's by a relative error of at most 0.018.
The reference program's roundings to bfloat16 on the way count: a program that leaves them out, or rounds other values in their place, can miss the bound.
Values may be sent and summed in bfloat16 or wider, within the bound.
No kernel may reach another device: no remote copies, remote signals or barrier semaphores. Data moves between devices by JAX's collectives and lax.ppermute only.
A program may use at most 192 MiB of HBM per device.

```python
import math
import jax
import jax.numpy as jnp
from jax import lax

D = 768
HEADS = 12
HEAD = 64
FF = 3072
CLASSES = 1000
FREQS = 256
SIDE = 32
LATENTS = 16


def draw_timesteps(key, part):
    first_key, second_key, third_key = jax.random.split(jax.random.fold_in(key, 7), 3)
    earlier = jax.random.randint(first_key, (LATENTS,), 0, 1000)
    later = jax.random.randint(second_key, (LATENTS,), 0, 1000)
    drawn = jnp.minimum(earlier, later).astype(jnp.int32)
    order = jax.random.permutation(third_key, LATENTS)
    places = jnp.arange(LATENTS, dtype=jnp.int32)
    drawn = jnp.where(places == order[0], 999, drawn)
    drawn = jnp.where(places == order[1], 0, drawn)
    return drawn.astype(jnp.int32)


def place_ends(values, key, least, high):
    spot = [jax.random.randint(jax.random.fold_in(key, axis), (), 0, length) for axis, length in enumerate(values.shape)]
    widest = values.shape.index(max(values.shape))
    neighbour = spot[:widest] + [(spot[widest] + 1) % values.shape[widest]] + spot[widest + 1:]
    return values.at[tuple(spot)].set(least).at[tuple(neighbour)].set(high)


def spiked(array, key, source, target, shards_of, factor):
    def block_of(axis_at):
        return (jnp.arange(array.shape[axis_at]) // (array.shape[axis_at] // shards_of)).reshape((-1,) + (1,) * (array.ndim - 1 - axis_at))

    first = jax.random.permutation(key, shards_of)[block_of(target)]
    second = (block_of(target) + shards_of // 2) % shards_of
    return jnp.where((block_of(source) == first) | (block_of(source) == second), factor * array, array)


def shard_levels(key, extent, cuts, low, top_value):
    loudness = 1.0
    for axis_at, parts in cuts:
        steps = jax.random.uniform(jax.random.fold_in(jax.random.fold_in(key, 6), axis_at), (parts,), jnp.float32, low / len(cuts), top_value / len(cuts))
        loudness = loudness * jnp.repeat(jnp.exp(steps), extent[axis_at] // parts).reshape((-1,) + (1,) * (len(extent) - 1 - axis_at))
    return loudness


def gaussian(stream_key, shape, deviation, most, cuts=(), kind=jnp.bfloat16):
    array = deviation * jax.random.normal(stream_key, shape, jnp.float32)
    if cuts:
        array = array * shard_levels(stream_key, shape, cuts, -0.22, 0.18)
    return jnp.clip(array, -most, most).astype(kind)


def bell_draw_with(stream_key, dims, scale, limit, shards, heavy, kind=jnp.bfloat16):
    values = scale * jax.random.normal(stream_key, dims, jnp.float32)
    if shards:
        values = values * shard_levels(stream_key, dims, shards, -0.22, 0.18)
    return jnp.clip(spiked(values, jax.random.fold_in(stream_key, 3), *heavy), -limit, limit).astype(kind)


def setup_inputs(seed: int = 0) -> dict:
    key_of = jax.random.split(jax.random.key(seed), 22)
    latents = gaussian(key_of[0], (LATENTS, SIDE, SIDE, D), 1.0, 6.0, ((0, 8), (1, 4)))
    cotangent = bell_draw_with(key_of[1], (LATENTS, SIDE, SIDE, D), 1.0, 6.0, ((0, 8), (1, 4)), (0, 3, 8, 2.0))
    timesteps = draw_timesteps(jax.random.fold_in(key_of[21], 71), 0)
    labels = place_ends(jax.random.randint(key_of[3], (LATENTS,), 0, CLASSES), jax.random.fold_in(key_of[3], 1), 0, CLASSES - 1).astype(jnp.int32)
    time_weight = gaussian(key_of[4], (FREQS, D), FREQS ** -0.5, 0.375)
    time_bias = gaussian(key_of[5], (1, D), 0.5, 3.0)
    label_table = gaussian(key_of[6], (CLASSES, D), 1.0, 6.0)
    ada_weight = gaussian(key_of[7], (D, 6 * D), D ** -0.5, 0.21875)
    ada_bias = gaussian(key_of[8], (1, 6 * D), 0.5, 3.0)
    conv_a = gaussian(key_of[9], (9, D), 9 ** -0.5, 2.0)
    conv_a_bias = gaussian(key_of[10], (1, D), 0.5, 3.0)
    qkv_weight = gaussian(key_of[11], (D, 3 * D), D ** -0.5, 0.21875)
    qv_bias = gaussian(key_of[12], (2, D), 0.5, 3.0)
    proj_weight = gaussian(key_of[13], (D, D), (D // 16) ** -0.5, 0.875)
    proj_bias = gaussian(key_of[14], (1, D), 0.5, 3.0)
    fc1_weight = gaussian(key_of[15], (D, FF), D ** -0.5, 0.21875)
    fc1_bias = gaussian(key_of[16], (1, FF), 0.5, 3.0)
    conv_f = gaussian(key_of[17], (9, FF), 9 ** -0.5, 2.0)
    conv_f_bias = gaussian(key_of[18], (1, FF), 0.5, 3.0)
    fc2_weight = gaussian(key_of[19], (FF, D), FF ** -0.5, 0.109375)
    fc2_bias = gaussian(key_of[20], (1, D), 0.5, 3.0)
    return {"latents": latents, "cotangent": cotangent, "timesteps": timesteps, "labels": labels, "time_weight": time_weight, "time_bias": time_bias, "label_table": label_table, "ada_weight": ada_weight, "ada_bias": ada_bias, "conv_a": conv_a, "conv_a_bias": conv_a_bias, "qkv_weight": qkv_weight, "qv_bias": qv_bias, "proj_weight": proj_weight, "proj_bias": proj_bias, "fc1_weight": fc1_weight, "fc1_bias": fc1_bias, "conv_f": conv_f, "conv_f_bias": conv_f_bias, "fc2_weight": fc2_weight, "fc2_bias": fc2_bias}


HIGHEST = lax.Precision.HIGHEST

@jax.custom_vjp
def low(v):
    return lax.optimization_barrier(v.astype(jnp.bfloat16)).astype(jnp.float32)

@jax.custom_vjp
def low_back(v):
    return v

def low_keep(v):
    return (low(v), None)

def low_pass(kept, grad):
    return (grad,)

def back_keep(v):
    return (v, None)

def back_low(kept, grad):
    return (low(grad),)
low.defvjp(low_keep, low_pass)
low_back.defvjp(back_keep, back_low)

def sinusoid(timestep, length):
    halfway = length // 2
    frequency = jnp.exp(-math.log(10000.0) * jnp.arange(halfway, dtype=jnp.float32) / halfway)
    angles = timestep.astype(jnp.float32)[:, None] * frequency[None, :]
    return jnp.concatenate([jnp.cos(angles), jnp.sin(angles)], axis=1)

def normalize(values, offset, scaling):
    centre = lax.optimization_barrier(jnp.mean(values, axis=-1, keepdims=True))
    centred = values - centre
    spread = lax.optimization_barrier(jnp.mean(centred * centred, axis=-1, keepdims=True))
    return centred * lax.rsqrt(spread + 1e-06) * (1.0 + scaling) + offset

def depthwise(values, tap_weights, biases):
    height = values.shape[1]
    breadth = values.shape[2]
    padded = jnp.pad(values, ((0, 0), (1, 1), (1, 1), (0, 0)))
    summed = biases
    for row_tap in range(3):
        for col_tap in range(3):
            window = padded[:, row_tap:row_tap + height, col_tap:col_tap + breadth]
            summed = summed + tap_weights[3 * row_tap + col_tap] * window
    return summed

def unshuffle(values):
    latent_count, height, breadth, channels = values.shape
    parted = values.reshape(latent_count, height // 2, 2, breadth // 2, 2, channels)
    return parted.transpose(0, 2, 4, 1, 3, 5).reshape(latent_count, 4, height // 2 * (breadth // 2), channels)

def shuffle(values, height, breadth):
    latent_count, groups, tokens, channels = values.shape
    parted = values.reshape(latent_count, 2, 2, height // 2, breadth // 2, channels)
    return parted.transpose(0, 3, 1, 4, 2, 5).reshape(latent_count, height, breadth, channels)

def attend(query_rows, key_rows, value_rows):
    latent_count, groups, tokens, channels = query_rows.shape
    shaped = (latent_count, groups, tokens, HEADS, HEAD)
    scores = jnp.einsum('lgqhe,lgkhe->lghqk', query_rows.reshape(shaped), key_rows.reshape(shaped), precision=HIGHEST)
    scores = low_back(scores * HEAD ** (-0.5))
    weights = low(jax.nn.softmax(scores, axis=-1))
    mixed = jnp.einsum('lghqk,lgkhe->lgqhe', weights, value_rows.reshape(shaped), precision=HIGHEST)
    return low_back(low(mixed.reshape(latent_count, groups, tokens, channels)))

def forward(latent_rows, frequency_rows, onehot, time_weight, time_bias, label_table, ada_weight, ada_bias, conv_a, conv_a_bias, qkv_weight, qv_bias, proj_weight, proj_bias, fc1_weight, fc1_bias, conv_f, conv_f_bias, fc2_weight, fc2_bias):
    condition = jnp.dot(frequency_rows, time_weight, precision=HIGHEST) + time_bias
    condition = condition + jnp.dot(onehot, label_table, precision=HIGHEST)
    modulation = jnp.dot(jax.nn.silu(condition), ada_weight, precision=HIGHEST) + ada_bias
    pieces = [modulation[:, None, None, slot * D:(slot + 1) * D] for slot in range(6)]
    offset_one, scaling_one, gate_one, offset_two, scaling_two, gate_two = pieces
    normed_one = low(normalize(latent_rows, offset_one, scaling_one))
    mixed_input = low_back(low(depthwise(normed_one, conv_a, conv_a_bias)))
    query_rows = low_back(low(jnp.dot(mixed_input, qkv_weight[:, :D], precision=HIGHEST) + qv_bias[0]))
    key_rows = low_back(low(jnp.dot(mixed_input, qkv_weight[:, D:2 * D], precision=HIGHEST)))
    value_rows = low_back(low(jnp.dot(mixed_input, qkv_weight[:, 2 * D:], precision=HIGHEST) + qv_bias[1]))
    grouped = attend(unshuffle(query_rows), unshuffle(key_rows), unshuffle(value_rows))
    attended = shuffle(grouped, SIDE, SIDE)
    branch_one = low_back(jnp.dot(attended, proj_weight, precision=HIGHEST) + proj_bias)
    middle = latent_rows + gate_one * branch_one
    normed_two = low(normalize(middle, offset_two, scaling_two))
    hidden = low_back(low(jnp.dot(normed_two, fc1_weight, precision=HIGHEST) + fc1_bias))
    convolved = low_back(depthwise(hidden, conv_f, conv_f_bias))
    activated = low(jax.nn.gelu(convolved, approximate=True))
    branch_two = low_back(jnp.dot(activated, fc2_weight, precision=HIGHEST) + fc2_bias)
    return middle + gate_two * branch_two

def reference(latents, cotangent, timesteps, labels, time_weight, time_bias, label_table, ada_weight, ada_bias, conv_a, conv_a_bias, qkv_weight, qv_bias, proj_weight, proj_bias, fc1_weight, fc1_bias, conv_f, conv_f_bias, fc2_weight, fc2_bias):
    parameters = tuple((weight_array.astype(jnp.float32) for weight_array in (time_weight, time_bias, label_table, ada_weight, ada_bias, conv_a, conv_a_bias, qkv_weight, qv_bias, proj_weight, proj_bias, fc1_weight, fc1_bias, conv_f, conv_f_bias, fc2_weight, fc2_bias)))
    blocks = latents.shape[0] // 4
    inputs = latents.astype(jnp.float32).reshape(blocks, 4, SIDE, SIDE, D)
    upstream = cotangent.astype(jnp.float32).reshape(blocks, 4, SIDE, SIDE, D)
    step_rows = timesteps.reshape(blocks, 4)
    label_rows = labels.reshape(blocks, 4)

    def one_block(totals, entries):
        latent_rows, cot_rows, steps_block, labels_block = entries
        frequency_rows = sinusoid(steps_block, FREQS)
        onehot = (labels_block[:, None] == jnp.arange(CLASSES, dtype=jnp.int32)[None, :]).astype(jnp.float32)

        def forward_block(values, *weight_list):
            return forward(values, frequency_rows, onehot, *weight_list)
        result, pullback = jax.vjp(forward_block, latent_rows, *parameters)
        gradients = pullback(cot_rows)
        totals = tuple((total_grad + new_grad for total_grad, new_grad in zip(totals, gradients[1:])))
        return (totals, (result.astype(jnp.bfloat16), gradients[0].astype(jnp.bfloat16)))
    starting = tuple((jnp.zeros_like(weight_array) for weight_array in parameters))
    totals, (outputs, input_grads) = lax.scan(one_block, starting, (inputs, upstream, step_rows, label_rows))
    return (outputs.reshape(latents.shape), input_grads.reshape(latents.shape), totals[0], totals[1], totals[2], totals[3], totals[4], totals[5], totals[6], totals[7], totals[8], totals[9], totals[10], totals[11], totals[12], totals[13], totals[14], totals[15], totals[16])
```

```python
import math

import jax
import jax.numpy as jnp
from jax import lax
from jax.sharding import PartitionSpec as P

HEADS = 12
HEAD = 64
BATCH, GRP = "batch", "grp"
HIGHEST = lax.Precision.HIGHEST
F32 = jnp.float32
BF16 = jnp.bfloat16
GELU_C = math.sqrt(2.0 / math.pi)


def swap_bit(value, axis, bit):
    count = lax.axis_size(axis)
    return lax.ppermute(value, axis, [(i, i ^ (1 << bit)) for i in range(count)])


def edge_rows(block, width):
    count = lax.axis_size(GRP)
    up = [(i, i + 1) for i in range(count - 1)]
    down = [(i + 1, i) for i in range(count - 1)]
    rows = block.shape[1]
    above = lax.ppermute(block[:, rows - width :], GRP, up)
    below = lax.ppermute(block[:, :width], GRP, down)
    return above, below


def with_edges(block, width):
    above, below = edge_rows(block, width)
    return jnp.concatenate([above, block, below], axis=1)


def row_mask(rows, width):
    strip = lax.axis_index(GRP)
    place = jnp.arange(rows) + strip * (rows - 2 * width) - width
    total = lax.axis_size(GRP) * (rows - 2 * width)
    return ((place >= 0) & (place < total))[None, :, None, None]


def halve_steps(swapped):
    batch_bits = lax.axis_size(BATCH).bit_length() - 1
    grp_bits = lax.axis_size(GRP).bit_length() - 1
    high = list(range(1, batch_bits))
    if swapped:
        high = high[::-1]
    return [(BATCH, bit) for bit in [0] + high] + [(GRP, bit) for bit in range(grp_bits)][::-1]


def split_bits(block):
    bits = (lax.axis_size(BATCH) * lax.axis_size(GRP)).bit_length() - 1
    return block.reshape((2,) * bits + block.shape[1:])


def scatter_sum(block, swapped):
    batch_bits = lax.axis_size(BATCH).bit_length() - 1
    grp_bits = lax.axis_size(GRP).bit_length() - 1
    order = [(BATCH, b) for b in range(batch_bits)][::-1] + [(GRP, b) for b in range(grp_bits)][::-1]
    block = split_bits(block)
    for axis, bit in halve_steps(swapped):
        place = order.index((axis, bit))
        order.remove((axis, bit))
        mine = (lax.axis_index(axis) >> bit) & 1
        away = lax.dynamic_index_in_dim(block, 1 - mine, place, keepdims=False)
        here = lax.dynamic_index_in_dim(block, mine, place, keepdims=False)
        arrived = swap_bit(away, axis, bit)
        block = here.astype(F32) + arrived.astype(F32)
        if order:
            block = block.astype(BF16)
    return block


def all_sum_grp(value):
    for bit in range(lax.axis_size(GRP).bit_length() - 1):
        value = value + swap_bit(value, GRP, bit)
    return value


def gather_batch(value):
    for bit in range(lax.axis_size(BATCH).bit_length() - 1):
        other = swap_bit(value, BATCH, bit)
        mine = (lax.axis_index(BATCH) >> bit) & 1
        value = jnp.where(
            mine == 0,
            jnp.concatenate([value, other], axis=0),
            jnp.concatenate([other, value], axis=0),
        )
    return value


def exact_dot(left, right):
    high = lax.reduce_precision(left, 8, 7)
    rest = left - high
    middle = lax.reduce_precision(rest, 8, 7)
    low = rest - middle
    rows = jnp.concatenate([high, middle, low], axis=0).astype(BF16)
    out = jnp.dot(rows, right, preferred_element_type=F32)
    count = left.shape[0]
    return out[:count] + (out[count : 2 * count] + out[2 * count :])


def sinusoid(timestep, length):
    halfway = length // 2
    frequency = jnp.exp(-math.log(10000.0) * jnp.arange(halfway, dtype=F32) / halfway)
    angles = timestep.astype(F32)[:, None] * frequency[None, :]
    return jnp.concatenate([jnp.cos(angles), jnp.sin(angles)], axis=1)


def centred_unit(values):
    centre = jnp.mean(values, axis=-1, keepdims=True)
    centred = values - centre
    spread = jnp.mean(centred * centred, axis=-1, keepdims=True)
    inverse = lax.rsqrt(spread + 1e-06)
    return centred * inverse, inverse


def unit_pull(unit, inverse, grad):
    first = jnp.mean(grad, axis=-1, keepdims=True)
    second = jnp.mean(grad * unit, axis=-1, keepdims=True)
    return inverse * (grad - first - unit * second)


def shift_cols(values, step):
    pad = jnp.zeros_like(values[:, :, :1])
    if step == 1:
        return jnp.concatenate([pad, values[:, :, :-1]], axis=2)
    return jnp.concatenate([values[:, :, 1:], pad], axis=2)


def depthwise(rimmed, taps):
    rows = rimmed.shape[1] - 2
    full = rimmed.astype(F32)
    parts = []
    for col_tap in range(3):
        part = sum(taps[3 * row_tap + col_tap] * full[:, row_tap : row_tap + rows] for row_tap in range(3))
        parts.append(part)
    return shift_cols(parts[0], 1) + parts[1] + shift_cols(parts[2], -1)


def depthwise_back(rimmed_grad, taps, values):
    rows = rimmed_grad.shape[1] - 2
    full = values.astype(F32)
    total = 0.0
    tap_grads = []
    moved = [shift_cols(rimmed_grad, -1), rimmed_grad, shift_cols(rimmed_grad, 1)]
    for row_tap in range(3):
        for col_tap in range(3):
            window = moved[col_tap][:, 2 - row_tap : 2 - row_tap + rows].astype(F32)
            total = total + taps[3 * row_tap + col_tap] * window
            tap_grads.append(jnp.sum(full * window, axis=(0, 1, 2)))
    bias_grad = jnp.sum(rimmed_grad[:, 1:-1].astype(F32), axis=(0, 1, 2))
    return total, tap_grads, bias_grad


def to_groups(values):
    count, rows, cols, channels = values.shape
    parted = values.reshape(count, rows // 2, 2, cols // 2, 2, channels)
    return parted.transpose(2, 4, 0, 1, 3, 5).reshape(4, count, rows // 2 * (cols // 2), channels)


def from_groups(blocks, rows, cols):
    groups, count, tokens, channels = blocks.shape
    parted = blocks.reshape(2, 2, count, rows // 2, cols // 2, channels)
    return parted.transpose(2, 3, 0, 4, 1, 5).reshape(count, rows, cols, channels)


def strips_to_group(values):
    blocks = to_groups(values)
    me = lax.axis_index(GRP)
    parts = [lax.dynamic_index_in_dim(blocks, me, 0, keepdims=False)]
    for step in range(1, lax.axis_size(GRP)):
        away = lax.dynamic_index_in_dim(blocks, me ^ step, 0, keepdims=False)
        parts.append(lax.ppermute(away, GRP, [(i, i ^ step) for i in range(lax.axis_size(GRP))]))
    return jnp.stack(parts, axis=1)


def group_to_strips(values, rows, cols):
    me = lax.axis_index(GRP)
    parts = [values[:, 0]]
    for step in range(1, lax.axis_size(GRP)):
        parts.append(
            lax.ppermute(values[:, step], GRP, [(i, i ^ step) for i in range(lax.axis_size(GRP))])
        )
    stacked = jnp.stack(parts)
    ordered = [lax.dynamic_index_in_dim(stacked, me ^ group, 0, keepdims=False) for group in range(4)]
    return from_groups(jnp.stack(ordered), rows, cols)


def attention_forward(query_rows, key_rows, value_rows):
    count, tokens, channels = query_rows.shape
    shaped = (count, tokens, HEADS, HEAD)
    scores = jnp.einsum(
        "lqhe,lkhe->lhqk",
        query_rows.reshape(shaped),
        key_rows.reshape(shaped),
        preferred_element_type=F32,
    ) * HEAD ** (-0.5)
    highest = jnp.max(scores, axis=-1, keepdims=True)
    raised = jnp.exp(scores - highest)
    totals = jnp.sum(raised, axis=-1, keepdims=True)
    weights = (raised / totals).astype(BF16)
    mixed = jnp.einsum("lhqk,lkhe->lqhe", weights, value_rows.reshape(shaped), preferred_element_type=F32)
    return mixed.reshape(count, tokens, channels).astype(BF16), highest + jnp.log(totals)


def attention_backward(query_rows, key_rows, value_rows, log_totals, upstream):
    count, tokens, channels = query_rows.shape
    shaped = (count, tokens, HEADS, HEAD)
    query_heads = query_rows.reshape(shaped)
    key_heads = key_rows.reshape(shaped)
    upstream_heads = upstream.reshape(shaped)
    scores = jnp.einsum("lqhe,lkhe->lhqk", query_heads, key_heads, preferred_element_type=F32) * HEAD ** (
        -0.5
    )
    weights = jnp.exp(scores - log_totals)
    rounded = weights.astype(BF16)
    value_grad = jnp.einsum("lhqk,lqhe->lkhe", rounded, upstream_heads, preferred_element_type=F32)
    weight_grad = jnp.einsum(
        "lqhe,lkhe->lhqk", upstream_heads, value_rows.reshape(shaped), preferred_element_type=F32
    )
    weighted = jnp.sum(weights * weight_grad, axis=-1, keepdims=True)
    score_grad = (weights * (weight_grad - weighted)).astype(BF16)
    query_grad = jnp.einsum("lhqk,lkhe->lqhe", score_grad, key_heads, preferred_element_type=F32) * HEAD ** (
        -0.5
    )
    key_grad = jnp.einsum("lhqk,lqhe->lkhe", score_grad, query_heads, preferred_element_type=F32) * HEAD ** (
        -0.5
    )
    flat = (count, tokens, channels)
    return jnp.concatenate(
        [query_grad.reshape(flat), key_grad.reshape(flat), value_grad.reshape(flat)], axis=-1
    ).astype(BF16)


def on_device(
    latents,
    cotangent,
    timesteps,
    labels,
    time_weight,
    time_bias,
    label_table,
    ada_weight,
    ada_bias,
    conv_a,
    conv_a_bias,
    qkv_weight,
    qv_bias,
    proj_weight,
    proj_bias,
    fc1_weight,
    fc1_bias,
    conv_f,
    conv_f_bias,
    fc2_weight,
    fc2_bias,
):
    count, rows, cols, width = latents.shape
    hidden_width = fc1_weight.shape[1]
    devices = lax.axis_size(BATCH) * lax.axis_size(GRP)
    slot = lax.axis_index(BATCH) * lax.axis_size(GRP) + lax.axis_index(GRP)
    tokens = rows * cols

    latents_rim = with_edges(latents, 1)
    cotangent_rim = with_edges(cotangent, 1)

    frequency_rows = sinusoid(timesteps, time_weight.shape[0])
    condition = exact_dot(frequency_rows, time_weight) + time_bias.astype(F32)
    picked = jnp.concatenate(
        [lax.dynamic_slice_in_dim(label_table, labels[i], 1, axis=0) for i in range(count)], axis=0
    )
    condition = condition + picked.astype(F32)
    active = condition * jax.nn.sigmoid(condition)
    modulation = exact_dot(active, ada_weight) + ada_bias.astype(F32)
    pieces = [modulation[:, None, None, i * width : (i + 1) * width] for i in range(6)]
    offset_one, scaling_one, gate_one, offset_two, scaling_two, gate_two = pieces

    inputs_full = latents_rim.astype(F32)
    unit_one, inverse_one = centred_unit(inputs_full)
    rimmed_one = jnp.where(
        row_mask(rows + 2, 1), unit_one * (1.0 + scaling_one) + offset_one, 0.0
    ).astype(BF16)
    unit_one, inverse_one, inputs_full = unit_one[:, 1:-1], inverse_one[:, 1:-1], inputs_full[:, 1:-1]
    taps_a = conv_a.astype(F32)
    mixed_strip = (depthwise(rimmed_one, taps_a) + conv_a_bias.astype(F32)).astype(BF16)
    mixed_input = strips_to_group(mixed_strip).reshape(count, -1, width)
    qkv_bias = jnp.concatenate([qv_bias[0:1], jnp.zeros_like(qv_bias[0:1]), qv_bias[1:2]], axis=1)
    projected = (
        jnp.dot(mixed_input, qkv_weight, preferred_element_type=F32) + qkv_bias.astype(F32)
    ).astype(BF16)
    query_rows, key_rows, value_rows = (projected[:, :, i * width : (i + 1) * width] for i in range(3))
    attended_group, log_totals = attention_forward(query_rows, key_rows, value_rows)
    attended = group_to_strips(attended_group.reshape(count, 4, -1, width), rows, cols)
    branch_one = jnp.dot(attended, proj_weight, preferred_element_type=F32) + proj_bias.astype(F32)
    middle = inputs_full + gate_one * branch_one

    unit_two, inverse_two = centred_unit(middle)
    normed_two = (unit_two * (1.0 + scaling_two) + offset_two).astype(BF16)
    normed_rim = with_edges(normed_two, 2)
    hidden = jnp.dot(normed_rim, fc1_weight, preferred_element_type=F32) + fc1_bias.astype(F32)
    hidden = jnp.where(row_mask(rows + 4, 2), hidden, 0.0).astype(BF16)
    taps_f = conv_f.astype(F32)
    convolved = depthwise(hidden, taps_f) + conv_f_bias.astype(F32)
    bent = jnp.tanh(GELU_C * (convolved + 0.044715 * convolved * convolved * convolved))
    activated = (0.5 * convolved * (1.0 + bent))[:, 1:-1].astype(BF16)
    slope = 0.5 * (1.0 + bent) + 0.5 * convolved * (1.0 - bent * bent) * GELU_C * (
        1.0 + 3.0 * 0.044715 * convolved * convolved
    )
    branch_two = jnp.dot(activated, fc2_weight, preferred_element_type=F32) + fc2_bias.astype(F32)
    output = (middle + gate_two * branch_two).astype(BF16)

    upstream = cotangent.astype(F32)
    gate_two_grad = jnp.sum(upstream * branch_two, axis=(1, 2))
    branch_two_rim = (gate_two * cotangent_rim.astype(F32)).astype(BF16)
    branch_two_grad = branch_two_rim[:, 1:-1]
    fc2_grad = jnp.einsum("lrcd,lrcf->df", branch_two_grad, activated, preferred_element_type=F32)
    fc2_bias_grad = jnp.sum(branch_two_grad.astype(F32), axis=(0, 1, 2))
    activated_grad = jnp.einsum("lrcd,fd->lrcf", branch_two_rim, fc2_weight, preferred_element_type=F32)
    convolved_grad = (activated_grad * slope).astype(BF16)
    hidden_grad, conv_f_grads, conv_f_bias_grad = depthwise_back(convolved_grad, taps_f, hidden[:, 2:-2])
    hidden_grad = hidden_grad.astype(BF16)
    fc1_grad = jnp.einsum("lrcf,lrcd->fd", hidden_grad, normed_two, preferred_element_type=F32)
    fc1_bias_grad = jnp.sum(hidden_grad.astype(F32), axis=(0, 1, 2))
    normed_two_grad = jnp.einsum("lrcf,df->lrcd", hidden_grad, fc1_weight, preferred_element_type=F32)
    fc1_sum = scatter_sum(fc1_grad.astype(BF16).reshape(devices, -1, width), False)
    fc2_sum = scatter_sum(fc2_grad.astype(BF16).reshape(devices, -1, hidden_width), True)
    offset_two_grad = jnp.sum(normed_two_grad, axis=(1, 2))
    scaling_two_grad = jnp.sum(normed_two_grad * unit_two, axis=(1, 2))
    middle_grad = upstream + unit_pull(unit_two, inverse_two, normed_two_grad * (1.0 + scaling_two))
    gate_one_grad = jnp.sum(middle_grad * branch_one, axis=(1, 2))
    branch_one_grad = (gate_one * middle_grad).astype(BF16)
    proj_grad = jnp.einsum("lrce,lrcd->ed", branch_one_grad, attended, preferred_element_type=F32)
    proj_bias_grad = jnp.sum(branch_one_grad.astype(F32), axis=(0, 1, 2))
    attended_grad = jnp.einsum(
        "lrce,de->lrcd", branch_one_grad, proj_weight, preferred_element_type=F32
    ).astype(BF16)
    proj_sum = scatter_sum(proj_grad.astype(BF16).reshape(devices, -1, width), False)
    group_upstream = strips_to_group(attended_grad).reshape(count, -1, width)
    group_grad = attention_backward(query_rows, key_rows, value_rows, log_totals, group_upstream)
    input_grad_group = jnp.einsum(
        "lte,de->ltd", group_grad, qkv_weight, preferred_element_type=F32
    ).astype(BF16)
    input_grad = group_to_strips(input_grad_group.reshape(count, 4, -1, width), rows, cols)
    qkv_grad = jnp.einsum("lte,ltd->ed", group_grad, mixed_input, preferred_element_type=F32)
    qkv_sum = scatter_sum(qkv_grad.astype(BF16).reshape(devices, -1, width), True)
    bias_sums = jnp.sum(group_grad.astype(F32), axis=(0, 1))
    input_grad_rim = with_edges(input_grad, 1)
    normed_one_grad, conv_a_grads, conv_a_bias_grad = depthwise_back(
        input_grad_rim, taps_a, rimmed_one[:, 1:-1]
    )
    offset_one_grad = jnp.sum(normed_one_grad, axis=(1, 2))
    scaling_one_grad = jnp.sum(normed_one_grad * unit_one, axis=(1, 2))
    latents_grad = (
        middle_grad + unit_pull(unit_one, inverse_one, normed_one_grad * (1.0 + scaling_one))
    ).astype(BF16)

    def slots(vectors):
        return jnp.stack(vectors).reshape(len(vectors), devices, -1).transpose(1, 0, 2).reshape(devices, -1)

    wide = [*conv_f_grads, conv_f_bias_grad, fc1_bias_grad]
    narrow = [
        *conv_a_grads,
        conv_a_bias_grad,
        bias_sums[:width],
        bias_sums[2 * width :],
        proj_bias_grad,
        fc2_bias_grad,
    ]
    small = jnp.concatenate([slots(wide), slots(narrow)], axis=1)
    small_sum = scatter_sum(small.astype(BF16), False)
    wide_sum = small_sum[: len(wide) * (hidden_width // devices)].reshape(len(wide), -1)
    narrow_sum = small_sum[len(wide) * (hidden_width // devices) :].reshape(len(narrow), -1)

    modulation_grad = jnp.concatenate(
        [offset_one_grad, scaling_one_grad, gate_one_grad, offset_two_grad, scaling_two_grad, gate_two_grad],
        axis=1,
    )
    every_grad = gather_batch(all_sum_grp(modulation_grad))
    every_condition = gather_batch(condition)
    every_frequency = gather_batch(frequency_rows)
    every_label = gather_batch(labels.astype(F32)[:, None])[:, 0].astype(jnp.int32)
    sigmoid = jax.nn.sigmoid(every_condition)
    every_active = every_condition * sigmoid
    narrow_width = width // devices
    ada_width = 6 * width // devices
    ada_part = lax.dynamic_slice_in_dim(every_grad, slot * ada_width, ada_width, axis=1)
    ada_grad = lax.dot_general(
        every_active, ada_part, (((0,), (0,)), ((), ())), precision=HIGHEST, preferred_element_type=F32
    )
    ada_bias_grad = jnp.sum(ada_part, axis=0)[None, :]
    ada_rows = lax.dynamic_slice_in_dim(ada_weight, slot * narrow_width, narrow_width, axis=0)
    active_grad = lax.dot_general(
        every_grad, ada_rows.astype(F32), (((1,), (1,)), ((), ())), precision=HIGHEST
    )
    slope_silu = lax.dynamic_slice_in_dim(
        sigmoid * (1.0 + every_condition * (1.0 - sigmoid)), slot * narrow_width, narrow_width, axis=1
    )
    condition_grad = active_grad * slope_silu
    onehot = (every_label[:, None] == jnp.arange(label_table.shape[0], dtype=jnp.int32)[None, :]).astype(F32)
    table_grad = lax.dot_general(onehot, condition_grad, (((0,), (0,)), ((), ())), precision=HIGHEST)
    time_grad = lax.dot_general(
        every_frequency, condition_grad, (((0,), (0,)), ((), ())), precision=HIGHEST
    )
    time_bias_grad = jnp.sum(condition_grad, axis=0)[None, :]

    return (
        output,
        latents_grad,
        time_grad,
        time_bias_grad,
        table_grad,
        ada_grad,
        ada_bias_grad,
        narrow_sum[0:9],
        narrow_sum[9:10],
        qkv_sum.T,
        narrow_sum[10:12],
        proj_sum.T,
        narrow_sum[12:13],
        fc1_sum.T,
        wide_sum[10:11],
        wide_sum[0:9],
        wide_sum[9:10],
        fc2_sum.T,
        narrow_sum[13:14],
    )


def solution(mesh):
    columns = P(None, (BATCH, GRP))
    return jax.shard_map(
        on_device,
        mesh=mesh,
        in_specs=(P(BATCH, GRP, None, None), P(BATCH, GRP, None, None), P(BATCH), P(BATCH)) + (P(),) * 17,
        out_specs=(P(BATCH, GRP, None, None), P(BATCH, GRP, None, None)) + (columns,) * 17,
        check_vma=False,
    )
```

```python
import math

import jax
import jax.numpy as jnp
from jax import lax
from jax.experimental import pallas as pl
from jax.experimental.pallas import tpu as pltpu
from jax.sharding import PartitionSpec as P

HEADS = 12
HEAD = 64
BATCH, GRP = "batch", "grp"
HIGHEST = lax.Precision.HIGHEST
F32 = jnp.float32
BF16 = jnp.bfloat16
GELU_C = math.sqrt(2.0 / math.pi)


def swap_bit(value, axis, bit):
    count = lax.axis_size(axis)
    return lax.ppermute(value, axis, [(i, i ^ (1 << bit)) for i in range(count)])


def edge_rows(block, width):
    count = lax.axis_size(GRP)
    up = [(i, i + 1) for i in range(count - 1)]
    down = [(i + 1, i) for i in range(count - 1)]
    rows = block.shape[1]
    above = lax.ppermute(block[:, rows - width :], GRP, up)
    below = lax.ppermute(block[:, :width], GRP, down)
    return above, below


def with_edges(block, width):
    above, below = edge_rows(block, width)
    return jnp.concatenate([above, block, below], axis=1)


def halve_steps(swapped):
    batch_bits = lax.axis_size(BATCH).bit_length() - 1
    grp_bits = lax.axis_size(GRP).bit_length() - 1
    high = list(range(1, batch_bits))
    if swapped:
        high = high[::-1]
    return [(BATCH, bit) for bit in [0] + high] + [(GRP, bit) for bit in range(grp_bits)][::-1]


def split_bits(block):
    bits = (lax.axis_size(BATCH) * lax.axis_size(GRP)).bit_length() - 1
    return block.reshape((2,) * bits + block.shape[1:])


def scatter_sum(block, swapped):
    batch_bits = lax.axis_size(BATCH).bit_length() - 1
    grp_bits = lax.axis_size(GRP).bit_length() - 1
    order = [(BATCH, b) for b in range(batch_bits)][::-1] + [(GRP, b) for b in range(grp_bits)][::-1]
    block = split_bits(block)
    for axis, bit in halve_steps(swapped):
        place = order.index((axis, bit))
        order.remove((axis, bit))
        mine = (lax.axis_index(axis) >> bit) & 1
        away = lax.dynamic_index_in_dim(block, 1 - mine, place, keepdims=False)
        here = lax.dynamic_index_in_dim(block, mine, place, keepdims=False)
        arrived = swap_bit(away, axis, bit)
        block = here.astype(F32) + arrived.astype(F32)
        if order:
            block = block.astype(BF16)
    return block


def all_sum_grp(*values):
    for bit in range(lax.axis_size(GRP).bit_length() - 1):
        values = tuple(value + swap_bit(value, GRP, bit) for value in values)
    return values


def gather_batch(value, summed):
    for bit in range(lax.axis_size(BATCH).bit_length() - 1):
        other = swap_bit(value, BATCH, bit)
        mine = (lax.axis_index(BATCH) >> bit) & 1
        value = jnp.where(
            mine == 0,
            jnp.concatenate([value, other], axis=0),
            jnp.concatenate([other, value], axis=0),
        )
        if summed is not None:
            summed = summed + swap_bit(summed, BATCH, bit)
    return value, summed


def exact_dot(left, right):
    high = lax.reduce_precision(left, 8, 7)
    rest = left - high
    middle = lax.reduce_precision(rest, 8, 7)
    low = rest - middle
    rows = jnp.concatenate([high, middle, low], axis=0).astype(BF16)
    out = jnp.dot(rows, right, preferred_element_type=F32)
    count = left.shape[0]
    return out[:count] + (out[count : 2 * count] + out[2 * count :])


def sinusoid(timestep, length):
    halfway = length // 2
    frequency = jnp.exp(-math.log(10000.0) * jnp.arange(halfway, dtype=F32) / halfway)
    angles = timestep.astype(F32)[:, None] * frequency[None, :]
    return jnp.concatenate([jnp.cos(angles), jnp.sin(angles)], axis=1)


def unit_pull(unit, inverse, grad):
    first = jnp.mean(grad, axis=-1, keepdims=True)
    second = jnp.mean(grad * unit, axis=-1, keepdims=True)
    return inverse * (grad - first - unit * second)


def row_shift(values, step):
    cols = values.shape[0]
    place = lax.broadcasted_iota(jnp.int32, values.shape, 0)
    rolled = pltpu.roll(values, step % cols, 0)
    return jnp.where(place == (0 if step == 1 else cols - 1), 0.0, rolled)


def fold_rows(values):
    total = values[0:8]
    for start in range(8, values.shape[0], 8):
        total = total + values[start : start + 8]
    return total


def feed_forward_body(
    flags, normed, upstream, fc1, fc1_bias, taps, conv_bias, fc2,
    branch_out, normed_grad_out, fc1_grad_out, fc2_grad_out, small_out,
    hidden, lifted, activated, convolved_grad, hidden_grad,
):
    count, rim_rows, cols, width = normed.shape
    rows = rim_rows - 4
    tile = fc1.shape[1]
    lanes = 128
    raw = jnp.dot(
        normed[...].reshape(count * rim_rows * cols, width), fc1[...], preferred_element_type=F32
    ) + fc1_bias[...].astype(F32)
    hidden[...] = raw.astype(BF16).astype(F32).reshape(count, rim_rows, cols, tile)
    hidden[:, 0:2] = hidden[:, 0:2] * flags[0]
    hidden[:, rows + 2 :] = hidden[:, rows + 2 :] * flags[1]
    lifted[...] = lax.dot_general(
        upstream[...].reshape(count * (rows + 2) * cols, width),
        fc2[...],
        (((1,), (1,)), ((), ())),
        preferred_element_type=F32,
    ).reshape(count, rows + 2, cols, tile)
    for start in range(0, tile, lanes):
        here = slice(start, start + lanes)
        tap = [taps[k : k + 1, here].astype(F32) for k in range(9)]
        bias = conv_bias[:, here].astype(F32)

        def forward_row(l, r, sums):
            near = [hidden[l, r + a, :, here] for a in range(3)]
            parts = [sum(tap[3 * a + e] * near[a] for a in range(3)) for e in range(3)]
            value = row_shift(parts[0], 1) + parts[1] + row_shift(parts[2], -1) + bias
            square = value * value
            bent = jnp.tanh(value * (GELU_C + GELU_C * 0.044715 * square))
            half = 0.5 * (1.0 + bent)
            activated[l, r, :, here] = (value * half).astype(BF16)
            slope = half + value * half * (1.0 - bent) * (GELU_C + 3.0 * 0.044715 * GELU_C * square)
            grad = (lifted[l, r, :, here] * slope).astype(BF16).astype(F32)
            convolved_grad[l, r, :, here] = grad
            if sums is None:
                return None
            moved = [row_shift(grad, -1), grad, row_shift(grad, 1)]
            added = [sums[3 * a + e] + fold_rows(near[a] * moved[e]) for a in range(3) for e in range(3)]
            return tuple(added) + (sums[9] + fold_rows(grad),)

        sums = tuple(jnp.zeros((8, lanes), F32) for _ in range(10))
        bias_sum = jnp.zeros((8, lanes), F32)
        for l in range(count):
            forward_row(l, 0, None)
            forward_row(l, rows + 1, None)
            sums = lax.fori_loop(1, rows + 1, lambda r, sums, l=l: forward_row(l, r, sums), sums)

            def backward_row(r, bias_sum, l=l):
                near = [convolved_grad[l, r + 2 - a, :, here] for a in range(3)]
                parts = [sum(tap[3 * a + e] * near[a] for a in range(3)) for e in range(3)]
                value = row_shift(parts[0], -1) + parts[1] + row_shift(parts[2], 1)
                rounded = value.astype(BF16)
                hidden_grad[l, r, :, here] = rounded
                return bias_sum + fold_rows(rounded.astype(F32))

            bias_sum = lax.fori_loop(0, rows, backward_row, bias_sum)
        for k in range(10):
            small_out[k : k + 1, here] = jnp.sum(sums[k], axis=0, keepdims=True)
        small_out[10:11, here] = jnp.sum(bias_sum, axis=0, keepdims=True)
    tokens = count * rows * cols
    active = activated[:, 1 : rows + 1].reshape(tokens, tile)
    back = hidden_grad[...].reshape(tokens, tile)
    inner = normed[:, 2 : rows + 2].reshape(tokens, width)
    above = upstream[:, 1 : rows + 1].reshape(tokens, width)

    @pl.when(pl.program_id(0) == 0)
    def _():
        branch_out[...] = jnp.zeros_like(branch_out)
        normed_grad_out[...] = jnp.zeros_like(normed_grad_out)

    branch_out[...] += jnp.dot(active, fc2[...], preferred_element_type=F32)
    normed_grad_out[...] += lax.dot_general(
        back, fc1[...], (((1,), (1,)), ((), ())), preferred_element_type=F32
    )
    fc1_grad_out[...] = lax.dot_general(
        back, inner, (((0,), (0,)), ((), ())), preferred_element_type=F32
    ).astype(BF16)
    fc2_grad_out[...] = lax.dot_general(
        above, active, (((0,), (0,)), ((), ())), preferred_element_type=F32
    ).astype(BF16)


def feed_forward(flags, normed, upstream, fc1, fc1_bias, taps, conv_bias, fc2):
    count, rim_rows, cols, width = normed.shape
    rows = rim_rows - 4
    tokens = count * rows * cols
    units = fc1.shape[1]
    tile = 256
    return pl.pallas_call(
        feed_forward_body,
        grid=(units // tile,),
        in_specs=[
            pl.BlockSpec(memory_space=pltpu.SMEM),
            pl.BlockSpec(normed.shape, lambda i: (0, 0, 0, 0)),
            pl.BlockSpec(upstream.shape, lambda i: (0, 0, 0, 0)),
            pl.BlockSpec((width, tile), lambda i: (0, i)),
            pl.BlockSpec((1, tile), lambda i: (0, i)),
            pl.BlockSpec((9, tile), lambda i: (0, i)),
            pl.BlockSpec((1, tile), lambda i: (0, i)),
            pl.BlockSpec((tile, width), lambda i: (i, 0)),
        ],
        out_specs=[
            pl.BlockSpec((tokens, width), lambda i: (0, 0)),
            pl.BlockSpec((tokens, width), lambda i: (0, 0)),
            pl.BlockSpec((tile, width), lambda i: (i, 0)),
            pl.BlockSpec((width, tile), lambda i: (0, i)),
            pl.BlockSpec((16, tile), lambda i: (0, i)),
        ],
        out_shape=[
            jax.ShapeDtypeStruct((tokens, width), F32),
            jax.ShapeDtypeStruct((tokens, width), F32),
            jax.ShapeDtypeStruct((units, width), BF16),
            jax.ShapeDtypeStruct((width, units), BF16),
            jax.ShapeDtypeStruct((16, units), F32),
        ],
        scratch_shapes=[
            pltpu.VMEM((count, rim_rows, cols, tile), F32),
            pltpu.VMEM((count, rows + 2, cols, tile), F32),
            pltpu.VMEM((count, rows + 2, cols, tile), BF16),
            pltpu.VMEM((count, rows + 2, cols, tile), F32),
            pltpu.VMEM((count, rows, cols, tile), BF16),
        ],
        compiler_params=pltpu.CompilerParams(
            dimension_semantics=("arbitrary",), vmem_limit_bytes=48 * 1024 * 1024
        ),
        name="feed_forward",
    )(flags, normed, upstream, fc1, fc1_bias, taps, conv_bias, fc2)


def layer_unit(values):
    centre = jnp.mean(values, axis=-1, keepdims=True)
    centred = values - centre
    inverse = lax.rsqrt(jnp.mean(centred * centred, axis=-1, keepdims=True) + 1e-06)
    return centred * inverse, inverse


def chunked(count, rows, cols, width):
    return (count, rows, width // 128, cols, 128)


def half_rows(start):
    return pl.ds(start, 16, stride=2)


def pack_strips(values, outs, me):
    count, rows, chunks, _, lanes = values.shape
    for l in range(count):

        def one(i, carry, l=l):
            for s, out in enumerate(outs):
                group = me ^ s
                row = 2 * i + (group >> 1)
                for c in range(chunks):
                    even = values[l, row, c, half_rows(0), :]
                    odd = values[l, row, c, half_rows(1), :]
                    picked = jnp.where((group & 1) == 0, even, odd).astype(BF16)
                    out[l, i, :, c * lanes : (c + 1) * lanes] = picked
            return carry

        lax.fori_loop(0, rows // 2, one, 0)


def pick_slot(parts, slot, l, i):
    picked = parts[0][l, i].astype(F32)
    for s in range(1, len(parts)):
        picked = jnp.where(slot == s, parts[s][l, i].astype(F32), picked)
    return picked


def unpack_strips(parts, values, me, first):
    count, halves = parts[0].shape[:2]
    chunks, _, lanes = values.shape[2:]
    for l in range(count):

        def one(i, carry, l=l):
            for p in range(2):
                for q in range(2):
                    picked = pick_slot(parts, (2 * p + q) ^ me, l, i)
                    for c in range(chunks):
                        piece = picked[:, c * lanes : (c + 1) * lanes]
                        values[l, 2 * i + (p ^ first), c, half_rows(q), :] = piece
            return carry

        lax.fori_loop(0, halves, one, 0)


def stem_body(place, latents, modulation, taps, conv_bias, out0, out1, out2, out3, normed, mixed):
    count, rim_rows, cols, width = normed.shape
    rows = rim_rows - 2
    lanes = 128
    for l in range(count):
        offset = modulation[l : l + 1, 0:width]
        scaling = 1.0 + modulation[l : l + 1, width : 2 * width]

        def norm_row(r, carry, l=l, offset=offset, scaling=scaling):
            for h in range(0, cols, 16):
                unit, _ = layer_unit(latents[l, r + 1, h : h + 16].astype(F32))
                normed[l, r, h : h + 16] = (unit * scaling + offset).astype(BF16).astype(F32)
            return carry

        lax.fori_loop(0, rim_rows, norm_row, 0)
        normed[l, 0] = normed[l, 0] * place[1].astype(F32)
        normed[l, rows + 1] = normed[l, rows + 1] * place[2].astype(F32)
    for start in range(0, width, lanes):
        here = slice(start, start + lanes)
        tap = [taps[k : k + 1, here].astype(F32) for k in range(9)]
        bias = conv_bias[:, here].astype(F32)
        for l in range(count):

            def conv_row(r, carry, l=l, here=here, tap=tap, bias=bias):
                near = [normed[l, r + a, :, here] for a in range(3)]
                parts = [sum(tap[3 * a + e] * near[a] for a in range(3)) for e in range(3)]
                total = row_shift(parts[0], 1) + parts[1] + row_shift(parts[2], -1) + bias
                mixed[l, r, here.start // lanes] = total
                return carry

            lax.fori_loop(0, rows, conv_row, 0)
    pack_strips(mixed, (out0, out1, out2, out3), place[0])


WHOLE = pl.BlockSpec(memory_space=pltpu.VMEM)
SCALARS = pl.BlockSpec(memory_space=pltpu.SMEM)


def call_whole(body, name, inputs, outputs, scratch):
    return pl.pallas_call(
        body,
        in_specs=[SCALARS] + [WHOLE] * (len(inputs) - 1),
        out_specs=[WHOLE] * len(outputs),
        out_shape=[jax.ShapeDtypeStruct(shape, kind) for shape, kind in outputs],
        scratch_shapes=[pltpu.VMEM(shape, kind) for shape, kind in scratch],
        compiler_params=pltpu.CompilerParams(vmem_limit_bytes=56 * 1024 * 1024),
        name=name,
    )(*inputs)


def stem(place, latents_rim, modulation, taps, conv_bias):
    count, rim_rows, cols, width = latents_rim.shape
    rows = rim_rows - 4
    return call_whole(
        stem_body,
        "stem",
        (place, latents_rim, modulation, taps, conv_bias),
        [((count, rows // 2, cols // 2, width), BF16)] * 4,
        [((count, rows + 2, cols, width), F32), (chunked(count, rows, cols, width), F32)],
    )


def head_mask(lanes, h):
    lane = lax.broadcasted_iota(jnp.int32, (1, lanes), 1)
    return (lane >= h * HEAD) & (lane < (h + 1) * HEAD)


def attend_body(place, part0, part1, part2, part3, weight, bias, out0, out1, out2, out3, projected, log_totals, gathered, attended):
    parts = (part0, part1, part2, part3)
    count, halves, cols, width = part0.shape
    block = halves * cols
    tokens = len(parts) * block
    me = place[0]
    for l in range(count):
        for s, part in enumerate(parts):
            gathered[l, s * block : (s + 1) * block] = part[l].reshape(block, width)
    raw = jnp.dot(gathered[...].reshape(count * tokens, width), weight[...], preferred_element_type=F32)
    projected[...] = (raw + bias[...].astype(F32)).astype(BF16).reshape(count, tokens, 3 * width)
    log_totals[...] = jnp.zeros_like(log_totals)
    lanes = 2 * HEAD
    lane = lax.broadcasted_iota(jnp.int32, (1, lanes), 1)
    for l in range(count):

        def pair(n, carry, l=l):
            start = pl.multiple_of(n * lanes, lanes)
            query = projected[l, :, pl.ds(start, lanes)].astype(F32) * HEAD ** (-0.5)
            key = projected[l, :, pl.ds(pl.multiple_of(width + n * lanes, lanes), lanes)]
            value = projected[l, :, pl.ds(pl.multiple_of(2 * width + n * lanes, lanes), lanes)]
            total_rows = log_totals[l]
            mixed = []
            for h in range(2):
                masked = jnp.where(head_mask(lanes, h), query, 0.0).astype(BF16)
                scores = lax.dot_general(masked, key, (((1,), (1,)), ((), ())), preferred_element_type=F32)
                highest = jnp.max(scores, axis=-1, keepdims=True)
                raised = jnp.exp(scores - highest)
                totals = jnp.sum(raised, axis=-1, keepdims=True)
                weights = (raised * (1.0 / totals)).astype(BF16)
                mixed.append(jnp.dot(weights, value, preferred_element_type=F32))
                total_rows = jnp.where(lane == 2 * n + h, highest + jnp.log(totals), total_rows)
            log_totals[l] = total_rows
            both = jnp.where(head_mask(lanes, 0), mixed[0], mixed[1]).astype(BF16)
            attended[l, :, :, pl.ds(start, lanes)] = both.reshape(len(parts) * halves, cols, lanes)
            return carry

        lax.fori_loop(0, width // lanes, pair, 0)
    send_rows(attended, (out0, out1, out2, out3), me, halves, 1, 0)


def send_rows(values, outs, me, halves, before, shift):
    count, total = values.shape[:2]
    for s, out in enumerate(outs):
        strip = me ^ s
        for k in range(out.shape[1]):
            row = strip * halves - before + shift + k
            inside = ((row >= 0) & (row < total)).astype(F32)
            kept = jnp.clip(row, 0, total - 1)
            source = (me ^ (kept // halves)) * halves + kept % halves
            for l in range(count):
                out[l, k] = (values[l, source].astype(F32) * inside).astype(BF16)


def attend(place, parts, weight, bias):
    count, halves, cols, width = parts[0].shape
    tokens = 4 * halves * cols
    return call_whole(
        attend_body,
        "attend",
        (place, *parts, weight, bias),
        [((count, halves + 2, cols, width), BF16)] * 4
        + [((count, tokens, 3 * width), BF16), ((count, tokens, 2 * HEAD), F32)],
        [((count, tokens, width), BF16), ((count, 4 * halves, cols, width), BF16)],
    )


def middle_body(place, part0, part1, part2, part3, latents, modulation, weight, bias, normed, attended, branch, spread, rimmed, raw):
    count, rim_rows, cols, width = latents.shape
    rows = rim_rows - 4
    unpack_strips((part0, part1, part2, part3), spread, place[0], 0)
    for c in range(width // 128):
        rimmed[:, :, :, c * 128 : (c + 1) * 128] = spread[:, :, c].astype(BF16)
    attended[...] = rimmed[:, 2 : rows + 2]
    every = rimmed[...].reshape(count * rim_rows * cols, width)
    dotted = jnp.dot(every, weight[...], preferred_element_type=F32) + bias[...].astype(F32)
    raw[...] = dotted.reshape(count, rim_rows, cols, width)
    branch[...] = raw[:, 2 : rows + 2]
    for l in range(count):
        gate = modulation[l : l + 1, 2 * width : 3 * width]
        offset = modulation[l : l + 1, 3 * width : 4 * width]
        scaling = 1.0 + modulation[l : l + 1, 4 * width : 5 * width]

        def norm_row(r, carry, l=l, gate=gate, offset=offset, scaling=scaling):
            for h in range(0, cols, 16):
                middle = latents[l, r, h : h + 16].astype(F32) + gate * raw[l, r, h : h + 16]
                unit, _ = layer_unit(middle)
                normed[l, r, h : h + 16] = (unit * scaling + offset).astype(BF16)
            return carry

        lax.fori_loop(0, rim_rows, norm_row, 0)


def middle_part(place, parts, latents_rim, modulation, weight, bias):
    count, rim_rows, cols, width = latents_rim.shape
    rows = rim_rows - 4
    return call_whole(
        middle_body,
        "middle",
        (place, *parts, latents_rim, modulation, weight, bias),
        [
            (latents_rim.shape, BF16),
            ((count, rows, cols, width), BF16),
            ((count, rows, cols, width), F32),
        ],
        [(chunked(*latents_rim.shape), F32), (latents_rim.shape, BF16), (latents_rim.shape, F32)],
    )


def turn_body(
    place, branch_two, normed_grad, branch_one, attended, latents, cotangent, modulation, fc2_bias, weight,
    output, middle_grad, weight_grad, sums, bias_sums, out0, out1, out2, out3, branch_grad, spread,
):
    count, rows, cols, width = cotangent.shape
    bias_sums[...] = jnp.zeros_like(bias_sums)
    sums[...] = jnp.zeros_like(sums)
    for l in range(count):
        gate_one, _, scaling, gate_two = (
            modulation[l : l + 1, k * width : (k + 1) * width] for k in range(2, 6)
        )
        scaling = 1.0 + scaling

        def one_row(r, carry, l=l, gate_one=gate_one, scaling=scaling, gate_two=gate_two):
            for h in range(0, cols, 16):
                here = slice(h, h + 16)
                first = branch_one[l, r, here]
                second = branch_two[l, r, here] + fc2_bias[...].astype(F32)
                upstream = cotangent[l, r, here].astype(F32)
                middle = latents[l, r + 2, here].astype(F32) + gate_one * first
                output[l, r, here] = (middle + gate_two * second).astype(BF16)
                unit, inverse = layer_unit(middle)
                grad = normed_grad[l, r, here]
                pulled = upstream + unit_pull(unit, inverse, grad * scaling)
                middle_grad[l, r, here] = pulled
                rounded = (gate_one * pulled).astype(BF16)
                branch_grad[l, r, here] = rounded
                sums[l, 0] += fold_rows(pulled * first)
                sums[l, 1] += fold_rows(grad)
                sums[l, 2] += fold_rows(grad * unit)
                sums[l, 3] += fold_rows(upstream * second)
                bias_sums[0] += fold_rows(rounded.astype(F32))
                bias_sums[1] += fold_rows((gate_two * upstream).astype(BF16).astype(F32))
            return carry

        lax.fori_loop(0, rows, one_row, 0)
    tokens = count * rows * cols
    back = branch_grad[...].reshape(tokens, width)
    weight_grad[...] = lax.dot_general(
        back, attended[...].reshape(tokens, width), (((0,), (0,)), ((), ())), preferred_element_type=F32
    ).astype(BF16)
    raw = lax.dot_general(back, weight[...], (((1,), (1,)), ((), ())), preferred_element_type=F32)
    for c in range(width // 128):
        spread[:, :, c] = raw[:, c * 128 : (c + 1) * 128].reshape(count, rows, cols, 128)
    pack_strips(spread, (out0, out1, out2, out3), place[0])


def turn(place, branch_two, normed_grad, branch_one, attended, latents_rim, cotangent, modulation, fc2_bias, weight):
    count, rows, cols, width = cotangent.shape
    return call_whole(
        turn_body,
        "turn",
        (place, branch_two, normed_grad, branch_one, attended, latents_rim, cotangent, modulation, fc2_bias, weight),
        [
            (cotangent.shape, BF16),
            (cotangent.shape, F32),
            ((width, width), BF16),
            ((count, 4, 8, width), F32),
            ((2, 8, width), F32),
        ]
        + [((count, rows // 2, cols // 2, width), BF16)] * 4,
        [(cotangent.shape, BF16), (chunked(*cotangent.shape), F32)],
    )


def attend_back_body(
    place, up0, up1, up2, up3, part0, part1, part2, part3, projected, log_totals, weight,
    weight_grad, bias_sums, out0, out1, out2, out3, gathered, upstream, grads, spread,
):
    parts = (part0, part1, part2, part3)
    count, halves, cols, width = part0.shape
    block = halves * cols
    tokens = len(parts) * block
    me = place[0]
    for l in range(count):
        for s, (part, up) in enumerate(zip(parts, (up0, up1, up2, up3))):
            gathered[l, s * block : (s + 1) * block] = part[l].reshape(block, width)
            upstream[l, s * block : (s + 1) * block] = up[l].reshape(block, width)
    bias_sums[...] = jnp.zeros_like(bias_sums)
    lanes = 2 * HEAD
    lane = lax.broadcasted_iota(jnp.int32, (1, lanes), 1)
    turned = (((0,), (0,)), ((), ()))
    inner = (((1,), (1,)), ((), ()))
    for l in range(count):

        def pair(n, carry, l=l):
            here = [pl.ds(pl.multiple_of(k * width + n * lanes, lanes), lanes) for k in range(3)]
            query = projected[l, :, here[0]]
            key = projected[l, :, here[1]]
            value = projected[l, :, here[2]]
            up = upstream[l, :, here[0]]
            query_full = query.astype(F32) * HEAD ** (-0.5)
            up_full = up.astype(F32)
            found = []
            for h in range(2):
                mask = head_mask(lanes, h)
                total = jnp.sum(jnp.where(lane == 2 * n + h, log_totals[l], 0.0), axis=-1, keepdims=True)
                masked = jnp.where(mask, query_full, 0.0).astype(BF16)
                scores = lax.dot_general(masked, key, inner, preferred_element_type=F32)
                weights = jnp.exp(scores - total)
                value_grad = lax.dot_general(weights.astype(BF16), up, turned, preferred_element_type=F32)
                weight_side = lax.dot_general(
                    jnp.where(mask, up_full, 0.0).astype(BF16), value, inner, preferred_element_type=F32
                )
                weighted = jnp.sum(weights * weight_side, axis=-1, keepdims=True)
                score_grad = (weights * (weight_side - weighted)).astype(BF16)
                query_grad = jnp.dot(score_grad, key, preferred_element_type=F32) * HEAD ** (-0.5)
                key_grad = lax.dot_general(score_grad, query, turned, preferred_element_type=F32) * HEAD ** (-0.5)
                found.append((query_grad, key_grad, value_grad))
            mask = head_mask(lanes, 0)
            for k in range(3):
                both = jnp.where(mask, found[0][k], found[1][k]).astype(BF16)
                grads[l, :, here[k]] = both
                if k != 1:
                    bias_sums[k // 2, :, here[0]] += fold_rows(both.astype(F32))
            return carry

        lax.fori_loop(0, width // lanes, pair, 0)
    every = grads[...].reshape(count * tokens, 3 * width)
    weight_grad[...] = lax.dot_general(
        every, gathered[...].reshape(count * tokens, width), turned, preferred_element_type=F32
    ).astype(BF16)
    raw = lax.dot_general(every, weight[...], inner, preferred_element_type=F32)
    spread[...] = raw.astype(BF16).reshape(count, len(parts) * halves, cols, width)
    send_rows(spread, (out0, out1, out2, out3), me, halves, me >> 1, 0)


def attend_back(place, ups, parts, projected, log_totals, weight):
    count, halves, cols, width = parts[0].shape
    tokens = 4 * halves * cols
    return call_whole(
        attend_back_body,
        "attend_back",
        (place, *ups, *parts, projected, log_totals, weight),
        [((3 * width, width), BF16), ((2, 8, width), F32)] + [((count, halves + 1, cols, width), BF16)] * 4,
        [
            ((count, tokens, width), BF16),
            ((count, tokens, width), BF16),
            ((count, tokens, 3 * width), BF16),
            ((count, 4 * halves, cols, width), BF16),
        ],
    )


def finish_body(
    place, part0, part1, part2, part3, latents, modulation, taps, middle_grad, latents_grad, sums, small,
    rimmed, normed, normed_grad,
):
    count, rows, cols, width = middle_grad.shape
    lanes = 128
    unpack_strips((part0, part1, part2, part3), rimmed, place[0], 1)
    for l in range(count):
        offset = modulation[l : l + 1, 0:width]
        scaling = 1.0 + modulation[l : l + 1, width : 2 * width]

        def norm_row(r, carry, l=l, offset=offset, scaling=scaling):
            for h in range(0, cols, 16):
                unit, _ = layer_unit(latents[l, r + 2, h : h + 16].astype(F32))
                normed[l, r, h : h + 16] = (unit * scaling + offset).astype(BF16).astype(F32)
            return carry

        lax.fori_loop(0, rows, norm_row, 0)
    for start in range(0, width, lanes):
        here = slice(start, start + lanes)
        tap = [taps[k : k + 1, here].astype(F32) for k in range(9)]
        found = tuple(jnp.zeros((8, lanes), F32) for _ in range(10))
        for l in range(count):

            def conv_row(r, found, l=l, here=here, tap=tap):
                near = [rimmed[l, r + 2 - a, here.start // lanes] for a in range(3)]
                parts = [sum(tap[3 * a + e] * near[a] for a in range(3)) for e in range(3)]
                normed_grad[l, r, :, here] = row_shift(parts[0], -1) + parts[1] + row_shift(parts[2], 1)
                value = normed[l, r, :, here]
                moved = [row_shift(value, 1), value, row_shift(value, -1)]
                added = [found[3 * a + e] + fold_rows(near[a] * moved[e]) for a in range(3) for e in range(3)]
                return tuple(added) + (found[9] + fold_rows(near[1]),)

            found = lax.fori_loop(0, rows, conv_row, found)
        for k in range(10):
            small[k : k + 1, here] = jnp.sum(found[k], axis=0, keepdims=True)
    sums[...] = jnp.zeros_like(sums)
    for l in range(count):
        scaling = 1.0 + modulation[l : l + 1, width : 2 * width]

        def pull_row(r, carry, l=l, scaling=scaling):
            for h in range(0, cols, 16):
                here = slice(h, h + 16)
                unit, inverse = layer_unit(latents[l, r + 2, here].astype(F32))
                grad = normed_grad[l, r, here]
                sums[l, 0] += fold_rows(grad)
                sums[l, 1] += fold_rows(grad * unit)
                pulled = middle_grad[l, r, here] + unit_pull(unit, inverse, grad * scaling)
                latents_grad[l, r, here] = pulled.astype(BF16)
            return carry

        lax.fori_loop(0, rows, pull_row, 0)


def finish(place, parts, latents_rim, modulation, taps, middle_grad):
    count, rows, cols, width = middle_grad.shape
    return call_whole(
        finish_body,
        "finish",
        (place, *parts, latents_rim, modulation, taps, middle_grad),
        [(middle_grad.shape, BF16), ((count, 2, 8, width), F32), ((16, width), F32)],
        [(chunked(count, rows + 2, cols, width), F32), (middle_grad.shape, F32), (middle_grad.shape, F32)],
    )


def exchange(parts):
    count = lax.axis_size(GRP)
    moved = [lax.ppermute(parts[s], GRP, [(i, i ^ s) for i in range(count)]) for s in range(1, count)]
    return (parts[0], *moved)


def on_device(
    latents,
    cotangent,
    timesteps,
    labels,
    time_weight,
    time_bias,
    label_table,
    ada_weight,
    ada_bias,
    conv_a,
    conv_a_bias,
    qkv_weight,
    qv_bias,
    proj_weight,
    proj_bias,
    fc1_weight,
    fc1_bias,
    conv_f,
    conv_f_bias,
    fc2_weight,
    fc2_bias,
):
    count, rows, cols, width = latents.shape
    hidden_width = fc1_weight.shape[1]
    devices = lax.axis_size(BATCH) * lax.axis_size(GRP)
    slot = lax.axis_index(BATCH) * lax.axis_size(GRP) + lax.axis_index(GRP)

    latents_rim = with_edges(latents, 2)
    cotangent_rim = with_edges(cotangent, 1)
    strip = lax.axis_index(GRP)
    inside = jnp.stack([strip > 0, strip < lax.axis_size(GRP) - 1])
    flags = inside.astype(F32)
    place = jnp.concatenate([strip[None], inside.astype(jnp.int32)])

    frequency_rows = sinusoid(timesteps, time_weight.shape[0])
    condition = exact_dot(frequency_rows, time_weight) + time_bias.astype(F32)
    picked = jnp.concatenate(
        [lax.dynamic_slice_in_dim(label_table, labels[i], 1, axis=0) for i in range(count)], axis=0
    )
    condition = condition + picked.astype(F32)
    active = condition * jax.nn.sigmoid(condition)
    modulation = exact_dot(active, ada_weight) + ada_bias.astype(F32)
    pieces = [modulation[:, None, None, i * width : (i + 1) * width] for i in range(6)]
    offset_one, scaling_one, gate_one, offset_two, scaling_two, gate_two = pieces

    mixed = exchange(stem(place, latents_rim, modulation, conv_a, conv_a_bias))
    qkv_bias = jnp.concatenate([qv_bias[0:1], jnp.zeros_like(qv_bias[0:1]), qv_bias[1:2]], axis=1)
    *sent, projected, log_totals = attend(place, mixed, qkv_weight, qkv_bias)
    normed_rim, attended, branch_one = middle_part(
        place, exchange(sent), latents_rim, modulation, proj_weight, proj_bias
    )

    branch_two_rim = (gate_two * cotangent_rim.astype(F32)).astype(BF16)
    branch_two, normed_two_grad, fc1_grad, fc2_grad, ff_small = feed_forward(
        flags, normed_rim, branch_two_rim, fc1_weight, fc1_bias, conv_f, conv_f_bias, fc2_weight
    )
    fc1_sum = scatter_sum(fc1_grad.reshape(devices, -1, width), False)
    fc2_sum = scatter_sum(fc2_grad.reshape(devices, -1, hidden_width), True)

    output, middle_grad, proj_grad, turn_sums, turn_bias, *sent = turn(
        place,
        branch_two.reshape(latents.shape),
        normed_two_grad.reshape(latents.shape),
        branch_one,
        attended,
        latents_rim,
        cotangent,
        modulation,
        fc2_bias,
        proj_weight,
    )
    turn_sums = jnp.sum(turn_sums, axis=2)
    turn_bias = jnp.sum(turn_bias, axis=1)

    def slots(vectors):
        return vectors.reshape(len(vectors), devices, -1).transpose(1, 0, 2).reshape(devices, -1)

    small = jnp.concatenate([slots(ff_small[:11]), slots(turn_bias)], axis=1).astype(BF16)
    small_length = small.shape[1]
    small_rows = -(-small_length // width)
    small = jnp.pad(small, ((0, 0), (0, small_rows * width - small_length))).reshape(devices, small_rows, width)
    beside = scatter_sum(jnp.concatenate([proj_grad.reshape(devices, -1, width), small], axis=1), False)
    proj_sum = beside[:-small_rows]
    small_sum = beside[-small_rows:].reshape(-1)
    wide_length = 11 * (hidden_width // devices)
    wide_sum = small_sum[:wide_length].reshape(11, -1)
    narrow_sum = small_sum[wide_length:small_length].reshape(2, -1)

    qkv_grad, qv_sums, *sent = attend_back(place, exchange(sent), mixed, projected, log_totals, qkv_weight)
    qkv_sum = scatter_sum(qkv_grad.reshape(devices, -1, width), True)
    latents_grad, finish_sums, conv_a_small = finish(
        place, exchange(sent), latents_rim, modulation, conv_a, middle_grad
    )
    finish_sums = jnp.sum(finish_sums, axis=2)

    late = jnp.concatenate([conv_a_small[:10], jnp.sum(qv_sums, axis=1)], axis=0)
    modulation_grad = jnp.concatenate([finish_sums, turn_sums], axis=1).reshape(count, -1)
    per_latent = jnp.concatenate(
        [condition, frequency_rows, jnp.broadcast_to(labels.astype(F32)[:, None], (count, 128))], axis=1
    )
    every_grad, late_sum = gather_batch(*all_sum_grp(modulation_grad, late))
    every_side = gather_batch(per_latent, None)[0]
    every_condition = every_side[:, :width]
    every_frequency = every_side[:, width:-128]
    every_label = every_side[:, -128].astype(jnp.int32)
    late_sum = lax.dynamic_slice_in_dim(late_sum, slot * (width // devices), width // devices, axis=1)
    sigmoid = jax.nn.sigmoid(every_condition)
    every_active = every_condition * sigmoid
    narrow_width = width // devices
    ada_width = 6 * width // devices
    ada_part = lax.dynamic_slice_in_dim(every_grad, slot * ada_width, ada_width, axis=1)
    ada_grad = lax.dot_general(
        every_active, ada_part, (((0,), (0,)), ((), ())), precision=HIGHEST, preferred_element_type=F32
    )
    ada_bias_grad = jnp.sum(ada_part, axis=0)[None, :]
    ada_rows = lax.dynamic_slice_in_dim(ada_weight, slot * narrow_width, narrow_width, axis=0)
    active_grad = lax.dot_general(
        every_grad, ada_rows.astype(F32), (((1,), (1,)), ((), ())), precision=HIGHEST
    )
    slope_silu = lax.dynamic_slice_in_dim(
        sigmoid * (1.0 + every_condition * (1.0 - sigmoid)), slot * narrow_width, narrow_width, axis=1
    )
    condition_grad = active_grad * slope_silu
    onehot = (every_label[:, None] == jnp.arange(label_table.shape[0], dtype=jnp.int32)[None, :]).astype(F32)
    table_grad = lax.dot_general(onehot, condition_grad, (((0,), (0,)), ((), ())), precision=HIGHEST)
    time_grad = lax.dot_general(
        every_frequency, condition_grad, (((0,), (0,)), ((), ())), precision=HIGHEST
    )
    time_bias_grad = jnp.sum(condition_grad, axis=0)[None, :]

    return (
        output,
        latents_grad,
        time_grad,
        time_bias_grad,
        table_grad,
        ada_grad,
        ada_bias_grad,
        late_sum[0:9],
        late_sum[9:10],
        qkv_sum.T,
        late_sum[10:12],
        proj_sum.T,
        narrow_sum[0:1],
        fc1_sum.T,
        wide_sum[10:11],
        wide_sum[0:9],
        wide_sum[9:10],
        fc2_sum.T,
        narrow_sum[1:2],
    )


def solution(mesh):
    columns = P(None, (BATCH, GRP))
    return jax.shard_map(
        on_device,
        mesh=mesh,
        in_specs=(P(BATCH, GRP, None, None), P(BATCH, GRP, None, None), P(BATCH), P(BATCH)) + (P(),) * 17,
        out_specs=(P(BATCH, GRP, None, None), P(BATCH, GRP, None, None)) + (columns,) * 17,
        check_vma=False,
    )
```

```python
import math

import jax
import jax.numpy as jnp
from jax import lax
from jax.experimental import pallas as pl
from jax.experimental.pallas import tpu as pltpu
from jax.sharding import PartitionSpec as P


HEAD = 64
BATCH, GRP = "batch", "grp"
HIGHEST = lax.Precision.HIGHEST
F32 = jnp.float32
BF16 = jnp.bfloat16
GELU_C = math.sqrt(2.0 / math.pi)


def swap_bit(value, axis, bit):
    count = lax.axis_size(axis)
    return lax.ppermute(value, axis, [(i, i ^ (1 << bit)) for i in range(count)])


def to_pairs(block):
    strip = lax.axis_index(GRP)
    odd = strip & 1
    arrived = []
    for k in range(2):
        piece = lax.dynamic_slice_in_dim(block, k ^ odd, 1, axis=0)
        arrived.append(lax.ppermute(piece, (BATCH, GRP), pair_moves(k)))
    swapped = odd == 1
    upper = jnp.where(swapped, arrived[1], arrived[0])
    lower = jnp.where(swapped, arrived[0], arrived[1])
    return jnp.concatenate([upper, lower], axis=1)


def pair_moves(k, back=False):
    strips = lax.axis_size(GRP)
    moves = []
    for b in range(lax.axis_size(BATCH)):
        for z in range(strips):
            to = (2 * (b // 2) + (z >> 1)) * strips + 2 * (b & 1) + (k ^ (z & 1))
            moves.append((to, b * strips + z) if back else (b * strips + z, to))
    return moves


def from_pairs(block):
    rows = block.shape[1] // 2
    odd = lax.axis_index(GRP) & 1
    arrived = []
    for k in range(2):
        piece = lax.dynamic_slice_in_dim(block, (k ^ odd) * rows, rows, axis=1)
        arrived.append(lax.ppermute(piece, (BATCH, GRP), pair_moves(k, True)))
    swapped = odd == 1
    first = jnp.where(swapped, arrived[1], arrived[0])
    second = jnp.where(swapped, arrived[0], arrived[1])
    return jnp.concatenate([first, second], axis=0)


def with_edges(block, width):
    rows = block.shape[1]
    lower = (lax.axis_index(BATCH) & 1) == 1
    edge = jnp.where(lower, block[:, :width], block[:, rows - width :])
    other = swap_bit(edge, BATCH, 0)
    zero = jnp.zeros_like(other)
    return jnp.concatenate([jnp.where(lower, other, zero), block, jnp.where(lower, zero, other)], axis=1)


def halve(here, away, axis, bit):
    arrived = swap_bit(away, axis, bit)
    return here.astype(F32) + arrived.astype(F32)


def halve_dim(block, place, axis, bit):
    mine = (lax.axis_index(axis) >> bit) & 1
    away = lax.dynamic_index_in_dim(block, 1 - mine, place, keepdims=False)
    here = lax.dynamic_index_in_dim(block, mine, place, keepdims=False)
    return halve(here, away, axis, bit)


def scatter_rest(block, swapped):
    high = list(range(1, lax.axis_size(BATCH).bit_length() - 1))
    left = high[::-1]
    _, rows, width = block.shape
    block = block.reshape((2,) * len(high) + (rows, width))
    for bit in high[::-1] if swapped else high:
        block = halve_dim(block.astype(BF16), left.index(bit), BATCH, bit)
        left.remove(bit)
    bits = lax.axis_size(GRP).bit_length() - 1
    block = block.reshape((2,) * bits + (-1, width))
    for bit in range(bits):
        block = halve_dim(block.astype(BF16), bits - 1 - bit, GRP, bit)
    return block


def scatter_sum(block, swapped):
    pairs = lax.axis_size(BATCH) // 2
    width = block.shape[-1]
    block = halve_dim(block.reshape(pairs, 2, -1, width), 1, BATCH, 0)
    return scatter_rest(block, swapped)


def gather_sum(rows, pair_rows, summed):
    bits = [(BATCH, bit) for bit in range(1, lax.axis_size(BATCH).bit_length() - 1)]
    bits += [(GRP, bit) for bit in range(lax.axis_size(GRP).bit_length() - 1)]
    length = pair_rows.shape[0]
    both = jnp.concatenate([pair_rows, summed], axis=0)
    other = swap_bit(both, BATCH, 0)
    both = both + other
    rows = jnp.concatenate([both[:length], rows], axis=0)
    summed = both[length:]
    for axis, bit in bits:
        sent = jnp.concatenate([summed, rows], axis=0)
        other = swap_bit(sent, axis, bit)
        summed = summed + other[: len(summed)]
        rows = jnp.concatenate([rows, other[len(summed) :]], axis=0)
    return rows, summed


def exact_dot(left, right):
    high = lax.reduce_precision(left, 8, 7)
    rest = left - high
    middle = lax.reduce_precision(rest, 8, 7)
    low = rest - middle
    rows = jnp.concatenate([high, middle, low], axis=0).astype(BF16)
    out = jnp.dot(rows, right, preferred_element_type=F32)
    count = left.shape[0]
    return out[:count] + (out[count : 2 * count] + out[2 * count :])


def sinusoid(timestep, length):
    halfway = length // 2
    frequency = jnp.exp(-math.log(10000.0) * jnp.arange(halfway, dtype=F32) / halfway)
    angles = timestep.astype(F32)[:, None] * frequency[None, :]
    return jnp.concatenate([jnp.cos(angles), jnp.sin(angles)], axis=1)


def unit_pull(unit, inverse, grad):
    first = jnp.mean(grad, axis=-1, keepdims=True)
    second = jnp.mean(grad * unit, axis=-1, keepdims=True)
    return inverse * (grad - first - unit * second)


def row_shift(values, step):
    cols = values.shape[0]
    place = lax.broadcasted_iota(jnp.int32, values.shape, 0)
    rolled = pltpu.roll(values, step % cols, 0)
    return jnp.where(place == (0 if step == 1 else cols - 1), 0.0, rolled)


def fold_rows(values):
    total = values[0:8]
    for start in range(8, values.shape[0], 8):
        total = total + values[start : start + 8]
    return total


def feed_forward_body(
    place, normed, upstream, fc1, fc1_bias, taps, conv_bias, fc2,
    branch_out, normed_grad_out, fc1_here, fc1_away, fc2_here, fc2_away, small_out,
    hidden, lifted, activated, convolved_grad, hidden_grad, fc1_grad, fc2_grad,
):
    count, rim_rows, cols, width = normed.shape
    rows = rim_rows - 4
    tile = fc1.shape[1]
    lanes = 128
    raw = jnp.dot(
        normed[...].reshape(count * rim_rows * cols, width), fc1[...], preferred_element_type=F32
    ) + fc1_bias[...].astype(F32)
    hidden[...] = raw.astype(BF16).astype(F32).reshape(count, rim_rows, cols, tile)
    hidden[:, 0:2] = hidden[:, 0:2] * place[1].astype(F32)
    hidden[:, rows + 2 :] = hidden[:, rows + 2 :] * place[2].astype(F32)
    lifted[...] = lax.dot_general(
        upstream[...].reshape(count * (rows + 2) * cols, width),
        fc2[...],
        (((1,), (1,)), ((), ())),
        preferred_element_type=F32,
    ).reshape(count, rows + 2, cols, tile)
    for start in range(0, tile, lanes):
        here = slice(start, start + lanes)
        tap = [taps[k : k + 1, here].astype(F32) for k in range(9)]
        bias = conv_bias[:, here].astype(F32)

        def forward_row(l, r, sums):
            near = [hidden[l, r + a, :, here] for a in range(3)]
            parts = [sum(tap[3 * a + e] * near[a] for a in range(3)) for e in range(3)]
            value = row_shift(parts[0], 1) + parts[1] + row_shift(parts[2], -1) + bias
            square = value * value
            bent = jnp.tanh(value * (GELU_C + GELU_C * 0.044715 * square))
            half = 0.5 * (1.0 + bent)
            activated[l, r, :, here] = (value * half).astype(BF16)
            slope = half + value * half * (1.0 - bent) * (GELU_C + 3.0 * 0.044715 * GELU_C * square)
            grad = (lifted[l, r, :, here] * slope).astype(BF16).astype(F32)
            convolved_grad[l, r, :, here] = grad
            if sums is None:
                return None
            moved = [row_shift(grad, -1), grad, row_shift(grad, 1)]
            added = [sums[3 * a + e] + fold_rows(near[a] * moved[e]) for a in range(3) for e in range(3)]
            return tuple(added) + (sums[9] + fold_rows(grad),)

        sums = tuple(jnp.zeros((8, lanes), F32) for _ in range(10))
        bias_sum = jnp.zeros((8, lanes), F32)
        for l in range(count):
            forward_row(l, 0, None)
            forward_row(l, rows + 1, None)
            sums = lax.fori_loop(1, rows + 1, lambda r, sums, l=l: forward_row(l, r, sums), sums)

            def backward_row(r, bias_sum, l=l):
                near = [convolved_grad[l, r + 2 - a, :, here] for a in range(3)]
                parts = [sum(tap[3 * a + e] * near[a] for a in range(3)) for e in range(3)]
                value = row_shift(parts[0], -1) + parts[1] + row_shift(parts[2], 1)
                rounded = value.astype(BF16)
                hidden_grad[l, r, :, here] = rounded
                return bias_sum + fold_rows(rounded.astype(F32))

            bias_sum = lax.fori_loop(0, rows, backward_row, bias_sum)
        for k in range(10):
            small_out[k : k + 1, here] = jnp.sum(sums[k], axis=0, keepdims=True)
        small_out[10:11, here] = jnp.sum(bias_sum, axis=0, keepdims=True)
    tokens = count * rows * cols
    active = activated[:, 1 : rows + 1].reshape(tokens, tile)
    back = hidden_grad[...].reshape(tokens, tile)
    inner = normed[:, 2 : rows + 2].reshape(tokens, width)
    above = upstream[:, 1 : rows + 1].reshape(tokens, width)

    @pl.when(pl.program_id(0) == 0)
    def _():
        branch_out[...] = jnp.zeros_like(branch_out)
        normed_grad_out[...] = jnp.zeros_like(normed_grad_out)

    branch_out[...] += jnp.dot(active, fc2[...], preferred_element_type=F32)
    normed_grad_out[...] += lax.dot_general(
        back, fc1[...], (((1,), (1,)), ((), ())), preferred_element_type=F32
    )
    me = place[0]
    fc1_grad[...] = lax.dot_general(
        back, inner, (((0,), (0,)), ((), ())), preferred_element_type=F32
    ).astype(BF16).reshape(fc1_grad.shape)
    for j in range(fc1_grad.shape[0]):
        fc1_here[0, j] = fc1_grad[j, me]
        fc1_away[0, j] = fc1_grad[j, 1 - me]
    fc2_grad[...] = lax.dot_general(
        above, active, (((0,), (0,)), ((), ())), preferred_element_type=F32
    ).reshape(fc2_grad.shape)
    for j in range(fc2_grad.shape[0]):
        fc2_here[j] = fc2_grad[j, me].astype(BF16)
        fc2_away[j] = fc2_grad[j, 1 - me].astype(BF16)


def feed_forward(place, normed, upstream, fc1, fc1_bias, taps, conv_bias, fc2):
    count, rim_rows, cols, width = normed.shape
    rows = rim_rows - 4
    tokens = count * rows * cols
    units = fc1.shape[1]
    tile = 768
    steps = units // tile
    batch = lax.axis_size(BATCH)
    fc1_block = (1, batch // 2 // steps, units // batch, width)
    fc2_block = (batch // 2, width // batch, tile)
    return pl.pallas_call(
        feed_forward_body,
        grid=(steps,),
        in_specs=[
            pl.BlockSpec(memory_space=pltpu.SMEM),
            pl.BlockSpec(normed.shape, lambda i: (0, 0, 0, 0)),
            pl.BlockSpec(upstream.shape, lambda i: (0, 0, 0, 0)),
            pl.BlockSpec((width, tile), lambda i: (0, i)),
            pl.BlockSpec((1, tile), lambda i: (0, i)),
            pl.BlockSpec((9, tile), lambda i: (0, i)),
            pl.BlockSpec((1, tile), lambda i: (0, i)),
            pl.BlockSpec((tile, width), lambda i: (i, 0)),
        ],
        out_specs=[
            pl.BlockSpec((tokens, width), lambda i: (0, 0)),
            pl.BlockSpec((tokens, width), lambda i: (0, 0)),
            pl.BlockSpec(fc1_block, lambda i: (i, 0, 0, 0)),
            pl.BlockSpec(fc1_block, lambda i: (i, 0, 0, 0)),
            pl.BlockSpec(fc2_block, lambda i: (0, 0, i)),
            pl.BlockSpec(fc2_block, lambda i: (0, 0, i)),
            pl.BlockSpec((16, tile), lambda i: (0, i)),
        ],
        out_shape=[
            jax.ShapeDtypeStruct((tokens, width), F32),
            jax.ShapeDtypeStruct((tokens, width), F32),
            jax.ShapeDtypeStruct((steps,) + fc1_block[1:], BF16),
            jax.ShapeDtypeStruct((steps,) + fc1_block[1:], BF16),
            jax.ShapeDtypeStruct(fc2_block[:2] + (units,), BF16),
            jax.ShapeDtypeStruct(fc2_block[:2] + (units,), BF16),
            jax.ShapeDtypeStruct((16, units), F32),
        ],
        scratch_shapes=[
            pltpu.VMEM((count, rim_rows, cols, tile), F32),
            pltpu.VMEM((count, rows + 2, cols, tile), F32),
            pltpu.VMEM((count, rows + 2, cols, tile), BF16),
            pltpu.VMEM((count, rows + 2, cols, tile), F32),
            pltpu.VMEM((count, rows, cols, tile), BF16),
            pltpu.VMEM((fc1_block[1], 2) + fc1_block[2:], BF16),
            pltpu.VMEM((batch // 2, 2, width // batch, tile), F32),
        ],
        compiler_params=pltpu.CompilerParams(
            dimension_semantics=("arbitrary",), vmem_limit_bytes=48 * 1024 * 1024
        ),
        name="feed_forward",
    )(place, normed, upstream, fc1, fc1_bias, taps, conv_bias, fc2)


def layer_unit(values):
    centre = jnp.mean(values, axis=-1, keepdims=True)
    centred = values - centre
    inverse = lax.rsqrt(jnp.mean(centred * centred, axis=-1, keepdims=True) + 1e-06)
    return centred * inverse, inverse


def chunked(count, rows, cols, width):
    return (count, rows, width // 128, cols, 128)


def half_rows(start):
    return pl.ds(start, 16, stride=2)


def pack_strips(values, outs, me):
    _, rows, chunks, _, lanes = values.shape

    def one(i, carry):
        for s, out in enumerate(outs):
            row = 2 * i + (me ^ s)
            for q in range(2):
                for c in range(chunks):
                    out[q, i, :, c * lanes : (c + 1) * lanes] = values[0, row, c, half_rows(q), :].astype(BF16)
        return carry

    lax.fori_loop(0, rows // 2, one, 0)


def unpack_strips(parts, values, me, first):
    halves = parts[0].shape[1]
    chunks, _, lanes = values.shape[2:]

    def one(i, carry):
        for s, part in enumerate(parts):
            row = 2 * i + (me ^ s ^ first)
            for q in range(2):
                full = part[q, i].astype(F32)
                for c in range(chunks):
                    values[0, row, c, half_rows(q), :] = full[:, c * lanes : (c + 1) * lanes]
        return carry

    lax.fori_loop(0, halves, one, 0)


def stem_body(place, latents, modulation, taps, conv_bias, out0, out1, normed, mixed):
    count, rim_rows, cols, width = normed.shape
    rows = rim_rows - 2
    lanes = 128
    for l in range(count):
        offset = modulation[l : l + 1, 0:width]
        scaling = 1.0 + modulation[l : l + 1, width : 2 * width]

        def norm_row(r, carry, l=l, offset=offset, scaling=scaling):
            for h in range(0, cols, 16):
                unit, _ = layer_unit(latents[l, r + 1, h : h + 16].astype(F32))
                normed[l, r, h : h + 16] = (unit * scaling + offset).astype(BF16).astype(F32)
            return carry

        lax.fori_loop(0, rim_rows, norm_row, 0)
        normed[l, 0] = normed[l, 0] * place[1].astype(F32)
        normed[l, rows + 1] = normed[l, rows + 1] * place[2].astype(F32)
    for start in range(0, width, lanes):
        here = slice(start, start + lanes)
        tap = [taps[k : k + 1, here].astype(F32) for k in range(9)]
        bias = conv_bias[:, here].astype(F32)
        for l in range(count):

            def conv_row(r, carry, l=l, here=here, tap=tap, bias=bias):
                near = [normed[l, r + a, :, here] for a in range(3)]
                parts = [sum(tap[3 * a + e] * near[a] for a in range(3)) for e in range(3)]
                total = row_shift(parts[0], 1) + parts[1] + row_shift(parts[2], -1) + bias
                mixed[l, r, here.start // lanes] = total
                return carry

            lax.fori_loop(0, rows, conv_row, 0)
    pack_strips(mixed, (out0, out1), place[0])


WHOLE = pl.BlockSpec(memory_space=pltpu.VMEM)
SCALARS = pl.BlockSpec(memory_space=pltpu.SMEM)


def call_whole(body, inputs, outputs, scratch):
    return pl.pallas_call(
        body,
        in_specs=[SCALARS] + [WHOLE] * (len(inputs) - 1),
        out_specs=[WHOLE] * len(outputs),
        out_shape=[jax.ShapeDtypeStruct(shape, kind) for shape, kind in outputs],
        scratch_shapes=[pltpu.VMEM(shape, kind) for shape, kind in scratch],
        compiler_params=pltpu.CompilerParams(vmem_limit_bytes=56 * 1024 * 1024),
    )(*inputs)


def stem(place, latents_rim, modulation, taps, conv_bias):
    count, rim_rows, cols, width = latents_rim.shape
    rows = rim_rows - 4
    return call_whole(
        stem_body,
        (place, latents_rim, modulation, taps, conv_bias),
        [((2, rows // 2, cols // 2, width), BF16)] * 2,
        [((count, rows + 2, cols, width), F32), (chunked(count, rows, cols, width), F32)],
    )


def head_mask(lanes, h):
    lane = lax.broadcasted_iota(jnp.int32, (1, lanes), 1)
    return (lane >= h * HEAD) & (lane < (h + 1) * HEAD)


def attend_body(place, part0, part1, weight, bias, out0, out1, projected, log_totals, gathered, attended):
    parts = (part0, part1)
    count, halves, cols, width = part0.shape
    block = halves * cols
    tokens = len(parts) * block
    me = place[0]
    for l in range(count):
        for s, part in enumerate(parts):
            gathered[l, s * block : (s + 1) * block] = part[l].reshape(block, width)
    raw = jnp.dot(gathered[...].reshape(count * tokens, width), weight[...], preferred_element_type=F32)
    projected[...] = (raw + bias[...].astype(F32)).astype(BF16).reshape(count, tokens, 3 * width)
    log_totals[...] = jnp.zeros_like(log_totals)
    lanes = 2 * HEAD
    lane = lax.broadcasted_iota(jnp.int32, (1, lanes), 1)
    for l in range(count):

        def pair(n, carry, l=l):
            start = pl.multiple_of(n * lanes, lanes)
            query = projected[l, :, pl.ds(start, lanes)].astype(F32) * HEAD ** (-0.5)
            key = projected[l, :, pl.ds(pl.multiple_of(width + n * lanes, lanes), lanes)]
            value = projected[l, :, pl.ds(pl.multiple_of(2 * width + n * lanes, lanes), lanes)]
            total_rows = log_totals[l]
            mixed = []
            for h in range(2):
                masked = jnp.where(head_mask(lanes, h), query, 0.0).astype(BF16)
                scores = lax.dot_general(masked, key, (((1,), (1,)), ((), ())), preferred_element_type=F32)
                highest = jnp.max(scores, axis=-1, keepdims=True)
                raised = jnp.exp(scores - highest)
                totals = jnp.sum(raised, axis=-1, keepdims=True)
                weights = (raised * (1.0 / totals)).astype(BF16)
                mixed.append(jnp.dot(weights, value, preferred_element_type=F32))
                total_rows = jnp.where(lane == 2 * n + h, highest + jnp.log(totals), total_rows)
            log_totals[l] = total_rows
            both = jnp.where(head_mask(lanes, 0), mixed[0], mixed[1]).astype(BF16)
            attended[l, :, :, pl.ds(start, lanes)] = both.reshape(len(parts) * halves, cols, lanes)
            return carry

        lax.fori_loop(0, width // lanes, pair, 0)
    send_rows(attended, (out0, out1), me, halves, 1, 0)


def send_rows(values, outs, me, halves, before, shift):
    count, total = values.shape[:2]
    for s, out in enumerate(outs):
        strip = me ^ s
        for k in range(out.shape[1]):
            row = strip * halves - before + shift + k
            inside = ((row >= 0) & (row < total)).astype(F32)
            kept = jnp.clip(row, 0, total - 1)
            source = (me ^ (kept // halves)) * halves + kept % halves
            for l in range(count):
                out[l, k] = (values[l, source].astype(F32) * inside).astype(BF16)


def attend(place, parts, weight, bias):
    count, halves, cols, width = parts[0].shape
    tokens = len(parts) * halves * cols
    return call_whole(
        attend_body,
        (place, *parts, weight, bias),
        [((count, halves + 2, cols, width), BF16)] * 2
        + [((count, tokens, 3 * width), BF16), ((count, tokens, 2 * HEAD), F32)],
        [((count, tokens, width), BF16), ((count, len(parts) * halves, cols, width), BF16)],
    )


def middle_body(place, part0, part1, latents, modulation, weight, bias, normed, attended, branch, spread, rimmed, raw):
    count, rim_rows, cols, width = latents.shape
    rows = rim_rows - 4
    unpack_strips((part0, part1), spread, place[0], 0)
    for c in range(width // 128):
        rimmed[:, :, :, c * 128 : (c + 1) * 128] = spread[:, :, c].astype(BF16)
    attended[...] = rimmed[:, 2 : rows + 2]
    every = rimmed[...].reshape(count * rim_rows * cols, width)
    dotted = jnp.dot(every, weight[...], preferred_element_type=F32) + bias[...].astype(F32)
    raw[...] = dotted.reshape(count, rim_rows, cols, width)
    branch[...] = raw[:, 2 : rows + 2]
    for l in range(count):
        gate = modulation[l : l + 1, 2 * width : 3 * width]
        offset = modulation[l : l + 1, 3 * width : 4 * width]
        scaling = 1.0 + modulation[l : l + 1, 4 * width : 5 * width]

        def norm_row(r, carry, l=l, gate=gate, offset=offset, scaling=scaling):
            for h in range(0, cols, 16):
                middle = latents[l, r, h : h + 16].astype(F32) + gate * raw[l, r, h : h + 16]
                unit, _ = layer_unit(middle)
                normed[l, r, h : h + 16] = (unit * scaling + offset).astype(BF16)
            return carry

        lax.fori_loop(0, rim_rows, norm_row, 0)


def middle_part(place, parts, latents_rim, modulation, weight, bias):
    count, rim_rows, cols, width = latents_rim.shape
    rows = rim_rows - 4
    return call_whole(
        middle_body,
        (place, *parts, latents_rim, modulation, weight, bias),
        [
            (latents_rim.shape, BF16),
            ((count, rows, cols, width), BF16),
            ((count, rows, cols, width), F32),
        ],
        [(chunked(*latents_rim.shape), F32), (latents_rim.shape, BF16), (latents_rim.shape, F32)],
    )


def turn_body(
    place, branch_two, normed_grad, branch_one, attended, latents, cotangent, modulation, fc2_bias, weight,
    output, middle_grad, weight_grad, sums, bias_sums, out0, out1, branch_grad, spread,
):
    count, rows, cols, width = cotangent.shape
    bias_sums[...] = jnp.zeros_like(bias_sums)
    sums[...] = jnp.zeros_like(sums)
    for l in range(count):
        gate_one, _, scaling, gate_two = (
            modulation[l : l + 1, k * width : (k + 1) * width] for k in range(2, 6)
        )
        scaling = 1.0 + scaling

        def one_row(r, carry, l=l, gate_one=gate_one, scaling=scaling, gate_two=gate_two):
            for h in range(0, cols, 16):
                here = slice(h, h + 16)
                first = branch_one[l, r, here]
                second = branch_two[l, r, here] + fc2_bias[...].astype(F32)
                upstream = cotangent[l, r, here].astype(F32)
                middle = latents[l, r + 2, here].astype(F32) + gate_one * first
                output[l, r, here] = (middle + gate_two * second).astype(BF16)
                unit, inverse = layer_unit(middle)
                grad = normed_grad[l, r, here]
                pulled = upstream + unit_pull(unit, inverse, grad * scaling)
                middle_grad[l, r, here] = pulled
                rounded = (gate_one * pulled).astype(BF16)
                branch_grad[l, r, here] = rounded
                sums[l, 0] += fold_rows(pulled * first)
                sums[l, 1] += fold_rows(grad)
                sums[l, 2] += fold_rows(grad * unit)
                sums[l, 3] += fold_rows(upstream * second)
                bias_sums[0] += fold_rows(rounded.astype(F32))
                bias_sums[1] += fold_rows((gate_two * upstream).astype(BF16).astype(F32))
            return carry

        lax.fori_loop(0, rows, one_row, 0)
    tokens = count * rows * cols
    back = branch_grad[...].reshape(tokens, width)
    weight_grad[...] = lax.dot_general(
        back, attended[...].reshape(tokens, width), (((0,), (0,)), ((), ())), preferred_element_type=F32
    ).astype(BF16)
    raw = lax.dot_general(back, weight[...], (((1,), (1,)), ((), ())), preferred_element_type=F32)
    for c in range(width // 128):
        spread[:, :, c] = raw[:, c * 128 : (c + 1) * 128].reshape(count, rows, cols, 128)
    pack_strips(spread, (out0, out1), place[0])


def turn(place, branch_two, normed_grad, branch_one, attended, latents_rim, cotangent, modulation, fc2_bias, weight):
    count, rows, cols, width = cotangent.shape
    return call_whole(
        turn_body,
        (place, branch_two, normed_grad, branch_one, attended, latents_rim, cotangent, modulation, fc2_bias, weight),
        [
            (cotangent.shape, BF16),
            (cotangent.shape, F32),
            ((width, width), BF16),
            ((count, 4, 8, width), F32),
            ((2, 8, width), F32),
        ]
        + [((2, rows // 2, cols // 2, width), BF16)] * 2,
        [(cotangent.shape, BF16), (chunked(*cotangent.shape), F32)],
    )


def attend_back_body(
    place, up0, up1, part0, part1, projected, log_totals, weight,
    weight_grad, bias_sums, out0, out1, gathered, upstream, grads, spread,
):
    parts = (part0, part1)
    count, halves, cols, width = part0.shape
    block = halves * cols
    tokens = len(parts) * block
    me = place[0]
    for l in range(count):
        for s, (part, up) in enumerate(zip(parts, (up0, up1))):
            gathered[l, s * block : (s + 1) * block] = part[l].reshape(block, width)
            upstream[l, s * block : (s + 1) * block] = up[l].reshape(block, width)
    bias_sums[...] = jnp.zeros_like(bias_sums)
    lanes = 2 * HEAD
    lane = lax.broadcasted_iota(jnp.int32, (1, lanes), 1)
    turned = (((0,), (0,)), ((), ()))
    inner = (((1,), (1,)), ((), ()))
    for l in range(count):

        def pair(n, carry, l=l):
            here = [pl.ds(pl.multiple_of(k * width + n * lanes, lanes), lanes) for k in range(3)]
            query = projected[l, :, here[0]]
            key = projected[l, :, here[1]]
            value = projected[l, :, here[2]]
            up = upstream[l, :, here[0]]
            query_full = query.astype(F32) * HEAD ** (-0.5)
            up_full = up.astype(F32)
            found = []
            for h in range(2):
                mask = head_mask(lanes, h)
                total = jnp.sum(jnp.where(lane == 2 * n + h, log_totals[l], 0.0), axis=-1, keepdims=True)
                masked = jnp.where(mask, query_full, 0.0).astype(BF16)
                scores = lax.dot_general(masked, key, inner, preferred_element_type=F32)
                weights = jnp.exp(scores - total)
                value_grad = lax.dot_general(weights.astype(BF16), up, turned, preferred_element_type=F32)
                weight_side = lax.dot_general(
                    jnp.where(mask, up_full, 0.0).astype(BF16), value, inner, preferred_element_type=F32
                )
                weighted = jnp.sum(weights * weight_side, axis=-1, keepdims=True)
                score_grad = (weights * (weight_side - weighted)).astype(BF16)
                query_grad = jnp.dot(score_grad, key, preferred_element_type=F32) * HEAD ** (-0.5)
                key_grad = lax.dot_general(score_grad, query, turned, preferred_element_type=F32) * HEAD ** (-0.5)
                found.append((query_grad, key_grad, value_grad))
            mask = head_mask(lanes, 0)
            for k in range(3):
                both = jnp.where(mask, found[0][k], found[1][k]).astype(BF16)
                grads[l, :, here[k]] = both
                if k != 1:
                    bias_sums[k // 2, :, here[0]] += fold_rows(both.astype(F32))
            return carry

        lax.fori_loop(0, width // lanes, pair, 0)
    every = grads[...].reshape(count * tokens, 3 * width)
    weight_grad[...] = lax.dot_general(
        every, gathered[...].reshape(count * tokens, width), turned, preferred_element_type=F32
    ).astype(BF16)
    raw = lax.dot_general(every, weight[...], inner, preferred_element_type=F32)
    spread[...] = raw.astype(BF16).reshape(count, len(parts) * halves, cols, width)
    send_rows(spread, (out0, out1), me, halves, me, 0)


def attend_back(place, ups, parts, projected, log_totals, weight):
    count, halves, cols, width = parts[0].shape
    tokens = len(parts) * halves * cols
    return call_whole(
        attend_back_body,
        (place, *ups, *parts, projected, log_totals, weight),
        [((3 * width, width), BF16), ((2, 8, width), F32)] + [((count, halves + 1, cols, width), BF16)] * 2,
        [
            ((count, tokens, width), BF16),
            ((count, tokens, width), BF16),
            ((count, tokens, 3 * width), BF16),
            ((count, len(parts) * halves, cols, width), BF16),
        ],
    )


def finish_body(
    place, part0, part1, latents, modulation, taps, middle_grad, latents_grad, sums, small,
    rimmed, normed, normed_grad,
):
    count, rows, cols, width = middle_grad.shape
    lanes = 128
    unpack_strips((part0, part1), rimmed, place[0], 1)
    for l in range(count):
        offset = modulation[l : l + 1, 0:width]
        scaling = 1.0 + modulation[l : l + 1, width : 2 * width]

        def norm_row(r, carry, l=l, offset=offset, scaling=scaling):
            for h in range(0, cols, 16):
                unit, _ = layer_unit(latents[l, r + 2, h : h + 16].astype(F32))
                normed[l, r, h : h + 16] = (unit * scaling + offset).astype(BF16).astype(F32)
            return carry

        lax.fori_loop(0, rows, norm_row, 0)
    for start in range(0, width, lanes):
        here = slice(start, start + lanes)
        tap = [taps[k : k + 1, here].astype(F32) for k in range(9)]
        found = tuple(jnp.zeros((8, lanes), F32) for _ in range(10))
        for l in range(count):

            def conv_row(r, found, l=l, here=here, tap=tap):
                near = [rimmed[l, r + 2 - a, here.start // lanes] for a in range(3)]
                parts = [sum(tap[3 * a + e] * near[a] for a in range(3)) for e in range(3)]
                normed_grad[l, r, :, here] = row_shift(parts[0], -1) + parts[1] + row_shift(parts[2], 1)
                value = normed[l, r, :, here]
                moved = [row_shift(value, 1), value, row_shift(value, -1)]
                added = [found[3 * a + e] + fold_rows(near[a] * moved[e]) for a in range(3) for e in range(3)]
                return tuple(added) + (found[9] + fold_rows(near[1]),)

            found = lax.fori_loop(0, rows, conv_row, found)
        for k in range(10):
            small[k : k + 1, here] = jnp.sum(found[k], axis=0, keepdims=True)
    sums[...] = jnp.zeros_like(sums)
    for l in range(count):
        scaling = 1.0 + modulation[l : l + 1, width : 2 * width]

        def pull_row(r, carry, l=l, scaling=scaling):
            for h in range(0, cols, 16):
                here = slice(h, h + 16)
                unit, inverse = layer_unit(latents[l, r + 2, here].astype(F32))
                grad = normed_grad[l, r, here]
                sums[l, 0] += fold_rows(grad)
                sums[l, 1] += fold_rows(grad * unit)
                pulled = middle_grad[l, r, here] + unit_pull(unit, inverse, grad * scaling)
                latents_grad[l, r, here] = pulled.astype(BF16)
            return carry

        lax.fori_loop(0, rows, pull_row, 0)


def finish(place, parts, latents_rim, modulation, taps, middle_grad):
    count, rows, cols, width = middle_grad.shape
    return call_whole(
        finish_body,
        (place, *parts, latents_rim, modulation, taps, middle_grad),
        [(middle_grad.shape, BF16), ((count, 2, 8, width), F32), ((16, width), F32)],
        [(chunked(count, rows + 2, cols, width), F32), (middle_grad.shape, F32), (middle_grad.shape, F32)],
    )


def exchange(parts):
    return parts[0], swap_bit(parts[1], BATCH, 0)


def on_device(
    latents,
    cotangent,
    timesteps,
    labels,
    time_weight,
    time_bias,
    label_table,
    ada_weight,
    ada_bias,
    conv_a,
    conv_a_bias,
    qkv_weight,
    qv_bias,
    proj_weight,
    proj_bias,
    fc1_weight,
    fc1_bias,
    conv_f,
    conv_f_bias,
    fc2_weight,
    fc2_bias,
):
    width = latents.shape[3]
    hidden_width = fc1_weight.shape[1]
    devices = lax.axis_size(BATCH) * lax.axis_size(GRP)
    slot = lax.axis_index(BATCH) * lax.axis_size(GRP) + lax.axis_index(GRP)

    strip = lax.axis_index(GRP)
    half = lax.axis_index(BATCH) & 1
    inside = jnp.stack([half == 1, half == 0])
    place = jnp.concatenate([half[None], inside.astype(jnp.int32)])
    numbers = jnp.stack([timesteps.astype(F32), labels.astype(F32)])
    other = swap_bit(numbers, BATCH, 0)
    numbers = jnp.where(half == strip >> 1, numbers, other)
    numbers = jnp.where((strip & 1) == 0, numbers[:, 0], numbers[:, 1])
    latents_rim = with_edges(to_pairs(latents), 2)
    cotangent = to_pairs(cotangent)
    cotangent_rim = with_edges(cotangent, 1)

    frequency_rows = sinusoid(numbers[:1], time_weight.shape[0])
    condition = exact_dot(frequency_rows, time_weight) + time_bias.astype(F32)
    picked = lax.dynamic_slice_in_dim(label_table, numbers[1].astype(jnp.int32), 1, axis=0)
    condition = condition + picked.astype(F32)
    active = condition * jax.nn.sigmoid(condition)
    modulation = exact_dot(active, ada_weight) + ada_bias.astype(F32)
    gate_two = modulation[:, None, None, 5 * width :]

    mixed = exchange(stem(place, latents_rim, modulation, conv_a, conv_a_bias))
    qkv_bias = jnp.concatenate([qv_bias[0:1], jnp.zeros_like(qv_bias[0:1]), qv_bias[1:2]], axis=1)
    *sent, projected, log_totals = attend(place, mixed, qkv_weight, qkv_bias)
    normed_rim, attended, branch_one = middle_part(
        place, exchange(sent), latents_rim, modulation, proj_weight, proj_bias
    )

    branch_two_rim = (gate_two * cotangent_rim.astype(F32)).astype(BF16)
    branch_two, normed_two_grad, fc1_here, fc1_away, fc2_here, fc2_away, ff_small = feed_forward(
        place, normed_rim, branch_two_rim, fc1_weight, fc1_bias, conv_f, conv_f_bias, fc2_weight
    )
    pairs = lax.axis_size(BATCH) // 2
    fc1_sum = halve(fc1_here, fc1_away, BATCH, 0).reshape(pairs, -1, width)
    fc2_sum = halve(fc2_here, fc2_away, BATCH, 0)
    fc1_sum = scatter_rest(fc1_sum, False)
    fc2_sum = scatter_rest(fc2_sum, True)

    output, middle_grad, proj_grad, turn_sums, turn_bias, *sent = turn(
        place,
        branch_two.reshape(cotangent.shape),
        normed_two_grad.reshape(cotangent.shape),
        branch_one,
        attended,
        latents_rim,
        cotangent,
        modulation,
        fc2_bias,
        proj_weight,
    )
    output = from_pairs(output)
    turn_sums = jnp.sum(turn_sums, axis=2)
    turn_bias = jnp.sum(turn_bias, axis=1)

    def slots(vectors):
        return vectors.reshape(len(vectors), devices, -1).transpose(1, 0, 2).reshape(devices, -1)

    small = jnp.concatenate([slots(ff_small[:11]), slots(turn_bias)], axis=1).astype(BF16)
    small_length = small.shape[1]
    small_rows = -(-small_length // width)
    small = jnp.pad(small, ((0, 0), (0, small_rows * width - small_length))).reshape(devices, small_rows, width)
    beside = scatter_sum(
        jnp.concatenate([proj_grad.reshape(devices, -1, width), small], axis=1).reshape(-1, width), False
    )
    proj_sum = beside[:-small_rows]
    small_sum = beside[-small_rows:].reshape(-1)
    wide_length = 11 * (hidden_width // devices)
    wide_sum = small_sum[:wide_length].reshape(11, -1)
    narrow_sum = small_sum[wide_length:small_length].reshape(2, -1)

    qkv_grad, qv_sums, *sent = attend_back(place, exchange(sent), mixed, projected, log_totals, qkv_weight)
    qkv_sum = scatter_sum(qkv_grad, True)
    latents_grad, finish_sums, conv_a_small = finish(
        place, exchange(sent), latents_rim, modulation, conv_a, middle_grad
    )
    latents_grad = from_pairs(latents_grad)
    finish_sums = jnp.sum(finish_sums, axis=2)

    late = jnp.concatenate([conv_a_small[:10], jnp.sum(qv_sums, axis=1)], axis=0)
    modulation_grad = jnp.concatenate([finish_sums, turn_sums], axis=1)[0]
    side = jnp.concatenate(
        [condition, jnp.pad(frequency_rows, ((0, 0), (0, width - frequency_rows.shape[1] - 1))), numbers[1:][None]],
        axis=1,
    )
    every, late_sum = gather_sum(side.reshape(2, width), modulation_grad, late)
    every = every.reshape(-1, 8, width)
    every_grad = every[:, :6].reshape(-1, 6 * width)
    every_condition = every[:, 6]
    every_frequency = every[:, 7, : frequency_rows.shape[1]]
    every_label = every[:, 7, -1].astype(jnp.int32)
    late_sum = lax.dynamic_slice_in_dim(late_sum, slot * (width // devices), width // devices, axis=1)
    sigmoid = jax.nn.sigmoid(every_condition)
    every_active = every_condition * sigmoid
    narrow_width = width // devices
    ada_width = 6 * width // devices
    ada_part = lax.dynamic_slice_in_dim(every_grad, slot * ada_width, ada_width, axis=1)
    ada_grad = lax.dot_general(
        every_active, ada_part, (((0,), (0,)), ((), ())), precision=HIGHEST, preferred_element_type=F32
    )
    ada_bias_grad = jnp.sum(ada_part, axis=0)[None, :]
    ada_rows = lax.dynamic_slice_in_dim(ada_weight, slot * narrow_width, narrow_width, axis=0)
    active_grad = lax.dot_general(
        every_grad, ada_rows.astype(F32), (((1,), (1,)), ((), ())), precision=HIGHEST
    )
    slope_silu = lax.dynamic_slice_in_dim(
        sigmoid * (1.0 + every_condition * (1.0 - sigmoid)), slot * narrow_width, narrow_width, axis=1
    )
    condition_grad = active_grad * slope_silu
    onehot = (every_label[:, None] == jnp.arange(label_table.shape[0], dtype=jnp.int32)[None, :]).astype(F32)
    table_grad = lax.dot_general(onehot, condition_grad, (((0,), (0,)), ((), ())), precision=HIGHEST)
    time_grad = lax.dot_general(
        every_frequency, condition_grad, (((0,), (0,)), ((), ())), precision=HIGHEST
    )
    time_bias_grad = jnp.sum(condition_grad, axis=0)[None, :]

    return (
        output,
        latents_grad,
        time_grad,
        time_bias_grad,
        table_grad,
        ada_grad,
        ada_bias_grad,
        late_sum[0:9],
        late_sum[9:10],
        qkv_sum.T,
        late_sum[10:12],
        proj_sum.T,
        narrow_sum[0:1],
        fc1_sum.T,
        wide_sum[10:11],
        wide_sum[0:9],
        wide_sum[9:10],
        fc2_sum.T,
        narrow_sum[1:2],
    )


def solution(mesh):
    columns = P(None, (BATCH, GRP))
    return jax.shard_map(
        on_device,
        mesh=mesh,
        in_specs=(P(BATCH, GRP, None, None), P(BATCH, GRP, None, None), P(BATCH), P(BATCH)) + (P(),) * 17,
        out_specs=(P(BATCH, GRP, None, None), P(BATCH, GRP, None, None)) + (columns,) * 17,
        check_vma=False,
    )
```

```python
from functools import partial
import math

import jax
import jax.numpy as jnp
from jax import lax
from jax.experimental import pallas as pl
from jax.experimental.pallas import tpu as pltpu
from jax.sharding import PartitionSpec as P


HEAD = 64
BATCH, GRP = "batch", "grp"
HIGHEST = lax.Precision.HIGHEST
F32 = jnp.float32
BF16 = jnp.bfloat16
GELU_C = math.sqrt(2.0 / math.pi)


def swap_bit(value, axis, bit):
    count = lax.axis_size(axis)
    return lax.ppermute(value, axis, [(i, i ^ (1 << bit)) for i in range(count)])


def to_pairs(block):
    strip = lax.axis_index(GRP)
    odd = strip & 1
    arrived = []
    for k in range(2):
        piece = lax.dynamic_slice_in_dim(block, k ^ odd, 1, axis=0)
        arrived.append(lax.ppermute(piece, (BATCH, GRP), pair_moves(k)))
    swapped = odd == 1
    upper = jnp.where(swapped, arrived[1], arrived[0])
    lower = jnp.where(swapped, arrived[0], arrived[1])
    return jnp.concatenate([upper, lower], axis=1)


def pair_moves(k, back=False):
    strips = lax.axis_size(GRP)
    moves = []
    for b in range(lax.axis_size(BATCH)):
        for z in range(strips):
            to = (2 * (b // 2) + (z >> 1)) * strips + 2 * (b & 1) + (k ^ (z & 1))
            moves.append((to, b * strips + z) if back else (b * strips + z, to))
    return moves


def from_pairs(block):
    rows = block.shape[1] // 2
    odd = lax.axis_index(GRP) & 1
    arrived = []
    for k in range(2):
        piece = lax.dynamic_slice_in_dim(block, (k ^ odd) * rows, rows, axis=1)
        arrived.append(lax.ppermute(piece, (BATCH, GRP), pair_moves(k, True)))
    swapped = odd == 1
    first = jnp.where(swapped, arrived[1], arrived[0])
    second = jnp.where(swapped, arrived[0], arrived[1])
    return jnp.concatenate([first, second], axis=0)


def with_edges(block, width):
    rows = block.shape[1]
    lower = (lax.axis_index(BATCH) & 1) == 1
    edge = jnp.where(lower, block[:, :width], block[:, rows - width :])
    other = swap_bit(edge, BATCH, 0)
    zero = jnp.zeros_like(other)
    return jnp.concatenate([jnp.where(lower, other, zero), block, jnp.where(lower, zero, other)], axis=1)


def halve(here, away, axis, bit):
    arrived = swap_bit(away, axis, bit)
    return here.astype(F32) + arrived.astype(F32)


def halve_dim(block, place, axis, bit):
    mine = (lax.axis_index(axis) >> bit) & 1
    away = lax.dynamic_index_in_dim(block, 1 - mine, place, keepdims=False)
    here = lax.dynamic_index_in_dim(block, mine, place, keepdims=False)
    return halve(here, away, axis, bit)


def scatter_rest(block, swapped):
    high = list(range(1, lax.axis_size(BATCH).bit_length() - 1))
    left = high[::-1]
    _, rows, width = block.shape
    block = block.reshape((2,) * len(high) + (rows, width))
    for bit in high[::-1] if swapped else high:
        block = halve_dim(block.astype(BF16), left.index(bit), BATCH, bit)
        left.remove(bit)
    bits = lax.axis_size(GRP).bit_length() - 1
    block = block.reshape((2,) * bits + (-1, width))
    for bit in range(bits):
        block = halve_dim(block.astype(BF16), bits - 1 - bit, GRP, bit)
    return block


def gather_sum(rows, pair_rows, summed):
    length = pair_rows.shape[0]
    bits = [(GRP, bit) for bit in range(lax.axis_size(GRP).bit_length() - 1)]
    bits += [(BATCH, bit) for bit in range(1, lax.axis_size(BATCH).bit_length() - 1)]
    length = pair_rows.shape[0]
    both = jnp.concatenate([pair_rows, summed], axis=0)
    other = swap_bit(both, BATCH, 0)
    both = both + other
    rows = both[:length] + rows
    summed = both[length:]
    for axis, bit in bits:
        sent = jnp.concatenate([summed, rows], axis=0)
        other = swap_bit(sent, axis, bit)
        summed = summed + other[: len(summed)]
        rows = jnp.concatenate([rows, other[len(summed) :]], axis=0)
    return rows, summed


def exact_dot(left, right):
    high = lax.reduce_precision(left, 8, 7)
    rest = left - high
    middle = lax.reduce_precision(rest, 8, 7)
    low = rest - middle
    rows = jnp.concatenate([high, middle, low], axis=0).astype(BF16)
    out = jnp.dot(rows, right, preferred_element_type=F32)
    count = left.shape[0]
    return out[:count] + (out[count : 2 * count] + out[2 * count :])


def sinusoid(timestep, length):
    halfway = length // 2
    frequency = jnp.exp(-math.log(10000.0) * jnp.arange(halfway, dtype=F32) / halfway)
    angles = timestep.astype(F32)[:, None] * frequency[None, :]
    return jnp.concatenate([jnp.cos(angles), jnp.sin(angles)], axis=1)


def unit_pull(unit, inverse, grad):
    first = jnp.mean(grad, axis=-1, keepdims=True)
    second = jnp.mean(grad * unit, axis=-1, keepdims=True)
    return inverse * (grad - first - unit * second)


def row_shift(values, step):
    cols = values.shape[0]
    place = lax.broadcasted_iota(jnp.int32, values.shape, 0)
    rolled = pltpu.roll(values, step % cols, 0)
    return jnp.where(place == (0 if step == 1 else cols - 1), 0.0, rolled)


def fold_rows(values):
    total = values[0:8]
    for start in range(8, values.shape[0], 8):
        total = total + values[start : start + 8]
    return total


def feed_forward_body(
    place, normed, upstream, fc1, fc1_bias, taps, conv_bias, fc2,
    branch_out, normed_grad_out, fc1_here, fc1_away, fc2_here, fc2_away, small_out,
    hidden, lifted, activated, convolved_grad, hidden_grad, fc1_grad, fc2_grad,
):
    count, rim_rows, cols, width = normed.shape
    rows = rim_rows - 4
    tile = fc1.shape[1]
    lanes = 128
    raw = jnp.dot(
        normed[...].reshape(count * rim_rows * cols, width), fc1[...], preferred_element_type=F32
    ) + fc1_bias[...].astype(F32)
    hidden[...] = raw.astype(BF16).astype(F32).reshape(count, rim_rows, cols, tile)
    hidden[:, 0:2] = hidden[:, 0:2] * place[1].astype(F32)
    hidden[:, rows + 2 :] = hidden[:, rows + 2 :] * place[2].astype(F32)
    lifted[...] = lax.dot_general(
        upstream[...].reshape(count * (rows + 2) * cols, width),
        fc2[...],
        (((1,), (1,)), ((), ())),
        preferred_element_type=F32,
    ).reshape(count, rows + 2, cols, tile)
    for start in range(0, tile, lanes):
        here = slice(start, start + lanes)
        tap = [taps[k : k + 1, here].astype(F32) for k in range(9)]
        bias = conv_bias[:, here].astype(F32)

        def forward_row(l, r, sums):
            near = [hidden[l, r + a, :, here] for a in range(3)]
            parts = [sum(tap[3 * a + e] * near[a] for a in range(3)) for e in range(3)]
            value = row_shift(parts[0], 1) + parts[1] + row_shift(parts[2], -1) + bias
            square = value * value
            bent = jnp.tanh(value * (GELU_C + GELU_C * 0.044715 * square))
            half = 0.5 * (1.0 + bent)
            activated[l, r, :, here] = (value * half).astype(BF16)
            slope = half + value * half * (1.0 - bent) * (GELU_C + 3.0 * 0.044715 * GELU_C * square)
            grad = (lifted[l, r, :, here] * slope).astype(BF16).astype(F32)
            convolved_grad[l, r, :, here] = grad
            if sums is None:
                return None
            moved = [row_shift(grad, -1), grad, row_shift(grad, 1)]
            added = [sums[3 * a + e] + fold_rows(near[a] * moved[e]) for a in range(3) for e in range(3)]
            return tuple(added) + (sums[9] + fold_rows(grad),)

        sums = tuple(jnp.zeros((8, lanes), F32) for _ in range(10))
        bias_sum = jnp.zeros((8, lanes), F32)
        for l in range(count):
            forward_row(l, 0, None)
            forward_row(l, rows + 1, None)
            sums = lax.fori_loop(1, rows + 1, lambda r, sums, l=l: forward_row(l, r, sums), sums)

            def backward_row(r, bias_sum, l=l):
                near = [convolved_grad[l, r + 2 - a, :, here] for a in range(3)]
                parts = [sum(tap[3 * a + e] * near[a] for a in range(3)) for e in range(3)]
                value = row_shift(parts[0], -1) + parts[1] + row_shift(parts[2], 1)
                rounded = value.astype(BF16)
                hidden_grad[l, r, :, here] = rounded
                return bias_sum + fold_rows(rounded.astype(F32))

            bias_sum = lax.fori_loop(0, rows, backward_row, bias_sum)
        for k in range(10):
            small_out[k : k + 1, here] = jnp.sum(sums[k], axis=0, keepdims=True)
        small_out[10:11, here] = jnp.sum(bias_sum, axis=0, keepdims=True)
    tokens = count * rows * cols
    active = activated[:, 1 : rows + 1].reshape(tokens, tile)
    back = hidden_grad[...].reshape(tokens, tile)
    inner = normed[:, 2 : rows + 2].reshape(tokens, width)
    above = upstream[:, 1 : rows + 1].reshape(tokens, width)

    @pl.when(pl.program_id(0) == 0)
    def _():
        branch_out[...] = jnp.zeros_like(branch_out)
        normed_grad_out[...] = jnp.zeros_like(normed_grad_out)

    branch_out[...] += jnp.dot(active, fc2[...], preferred_element_type=F32)
    normed_grad_out[...] += lax.dot_general(
        back, fc1[...], (((1,), (1,)), ((), ())), preferred_element_type=F32
    )
    me = place[0]
    fc1_grad[...] = lax.dot_general(
        back, inner, (((0,), (0,)), ((), ())), preferred_element_type=F32
    ).astype(BF16).reshape(fc1_grad.shape)
    for j in range(fc1_grad.shape[0]):
        fc1_here[0, j] = fc1_grad[j, me]
        fc1_away[0, j] = fc1_grad[j, 1 - me]
    fc2_grad[...] = lax.dot_general(
        above, active, (((0,), (0,)), ((), ())), preferred_element_type=F32
    ).reshape(fc2_grad.shape)
    for j in range(fc2_grad.shape[0]):
        fc2_here[j] = fc2_grad[j, me].astype(BF16)
        fc2_away[j] = fc2_grad[j, 1 - me].astype(BF16)


def feed_forward(place, normed, upstream, fc1, fc1_bias, taps, conv_bias, fc2):
    count, rim_rows, cols, width = normed.shape
    rows = rim_rows - 4
    tokens = count * rows * cols
    units = fc1.shape[1]
    tile = 768
    steps = units // tile
    batch = lax.axis_size(BATCH)
    fc1_block = (1, batch // 2 // steps, units // batch, width)
    fc2_block = (batch // 2, width // batch, tile)
    return pl.pallas_call(
        feed_forward_body,
        grid=(steps,),
        in_specs=[
            pl.BlockSpec(memory_space=pltpu.SMEM),
            pl.BlockSpec(normed.shape, lambda i: (0, 0, 0, 0)),
            pl.BlockSpec(upstream.shape, lambda i: (0, 0, 0, 0)),
            pl.BlockSpec((width, tile), lambda i: (0, i)),
            pl.BlockSpec((1, tile), lambda i: (0, i)),
            pl.BlockSpec((9, tile), lambda i: (0, i)),
            pl.BlockSpec((1, tile), lambda i: (0, i)),
            pl.BlockSpec((tile, width), lambda i: (i, 0)),
        ],
        out_specs=[
            pl.BlockSpec((tokens, width), lambda i: (0, 0)),
            pl.BlockSpec((tokens, width), lambda i: (0, 0)),
            pl.BlockSpec(fc1_block, lambda i: (i, 0, 0, 0)),
            pl.BlockSpec(fc1_block, lambda i: (i, 0, 0, 0)),
            pl.BlockSpec(fc2_block, lambda i: (0, 0, i)),
            pl.BlockSpec(fc2_block, lambda i: (0, 0, i)),
            pl.BlockSpec((16, tile), lambda i: (0, i)),
        ],
        out_shape=[
            jax.ShapeDtypeStruct((tokens, width), F32),
            jax.ShapeDtypeStruct((tokens, width), F32),
            jax.ShapeDtypeStruct((steps,) + fc1_block[1:], BF16),
            jax.ShapeDtypeStruct((steps,) + fc1_block[1:], BF16),
            jax.ShapeDtypeStruct(fc2_block[:2] + (units,), BF16),
            jax.ShapeDtypeStruct(fc2_block[:2] + (units,), BF16),
            jax.ShapeDtypeStruct((16, units), F32),
        ],
        scratch_shapes=[
            pltpu.VMEM((count, rim_rows, cols, tile), F32),
            pltpu.VMEM((count, rows + 2, cols, tile), F32),
            pltpu.VMEM((count, rows + 2, cols, tile), BF16),
            pltpu.VMEM((count, rows + 2, cols, tile), F32),
            pltpu.VMEM((count, rows, cols, tile), BF16),
            pltpu.VMEM((fc1_block[1], 2) + fc1_block[2:], BF16),
            pltpu.VMEM((batch // 2, 2, width // batch, tile), F32),
        ],
        compiler_params=pltpu.CompilerParams(
            dimension_semantics=("arbitrary",), vmem_limit_bytes=48 * 1024 * 1024
        ),
        name="feed_forward",
    )(place, normed, upstream, fc1, fc1_bias, taps, conv_bias, fc2)


def layer_unit(values):
    centre = jnp.mean(values, axis=-1, keepdims=True)
    centred = values - centre
    inverse = lax.rsqrt(jnp.mean(centred * centred, axis=-1, keepdims=True) + 1e-06)
    return centred * inverse, inverse


def chunked(count, rows, cols, width):
    return (count, rows, width // 128, cols, 128)


def half_rows(start):
    return pl.ds(start, 16, stride=2)


def pack_strips(values, outs, me):
    _, rows, chunks, _, lanes = values.shape

    def one(i, carry):
        for s, out in enumerate(outs):
            row = 2 * i + (me ^ s)
            for q in range(2):
                for c in range(chunks):
                    out[q, i, :, c * lanes : (c + 1) * lanes] = values[0, row, c, half_rows(q), :].astype(BF16)
        return carry

    lax.fori_loop(0, rows // 2, one, 0)


def unpack_strips(parts, values, me, first):
    halves = parts[0].shape[1]
    chunks, _, lanes = values.shape[2:]

    def one(i, carry):
        for s, part in enumerate(parts):
            row = 2 * i + (me ^ s ^ first)
            for q in range(2):
                full = part[q, i].astype(F32)
                for c in range(chunks):
                    values[0, row, c, half_rows(q), :] = full[:, c * lanes : (c + 1) * lanes]
        return carry

    lax.fori_loop(0, halves, one, 0)


def stem_body(place, latents, modulation, taps, conv_bias, out0, out1, normed, mixed):
    count, rim_rows, cols, width = normed.shape
    rows = rim_rows - 2
    lanes = 128
    for l in range(count):
        offset = modulation[l : l + 1, 0:width]
        scaling = 1.0 + modulation[l : l + 1, width : 2 * width]

        def norm_row(r, carry, l=l, offset=offset, scaling=scaling):
            for h in range(0, cols, 16):
                unit, _ = layer_unit(latents[l, r + 1, h : h + 16].astype(F32))
                normed[l, r, h : h + 16] = (unit * scaling + offset).astype(BF16).astype(F32)
            return carry

        lax.fori_loop(0, rim_rows, norm_row, 0)
        normed[l, 0] = normed[l, 0] * place[1].astype(F32)
        normed[l, rows + 1] = normed[l, rows + 1] * place[2].astype(F32)
    for start in range(0, width, lanes):
        here = slice(start, start + lanes)
        tap = [taps[k : k + 1, here].astype(F32) for k in range(9)]
        bias = conv_bias[:, here].astype(F32)
        for l in range(count):

            def conv_row(r, carry, l=l, here=here, tap=tap, bias=bias):
                near = [normed[l, r + a, :, here] for a in range(3)]
                parts = [sum(tap[3 * a + e] * near[a] for a in range(3)) for e in range(3)]
                total = row_shift(parts[0], 1) + parts[1] + row_shift(parts[2], -1) + bias
                mixed[l, r, here.start // lanes] = total
                return carry

            lax.fori_loop(0, rows, conv_row, 0)
    pack_strips(mixed, (out0, out1), place[0])


WHOLE = pl.BlockSpec(memory_space=pltpu.VMEM)
SCALARS = pl.BlockSpec(memory_space=pltpu.SMEM)


def call_whole(body, inputs, outputs, scratch):
    return pl.pallas_call(
        body,
        in_specs=[SCALARS] + [WHOLE] * (len(inputs) - 1),
        out_specs=[WHOLE] * len(outputs),
        out_shape=[jax.ShapeDtypeStruct(shape, kind) for shape, kind in outputs],
        scratch_shapes=[pltpu.VMEM(shape, kind) for shape, kind in scratch],
        compiler_params=pltpu.CompilerParams(vmem_limit_bytes=56 * 1024 * 1024),
    )(*inputs)


def stem(place, latents_rim, modulation, taps, conv_bias):
    count, rim_rows, cols, width = latents_rim.shape
    rows = rim_rows - 4
    return call_whole(
        stem_body,
        (place, latents_rim, modulation, taps, conv_bias),
        [((2, rows // 2, cols // 2, width), BF16)] * 2,
        [((count, rows + 2, cols, width), F32), (chunked(count, rows, cols, width), F32)],
    )


def head_mask(lanes, h):
    lane = lax.broadcasted_iota(jnp.int32, (1, lanes), 1)
    return (lane >= h * HEAD) & (lane < (h + 1) * HEAD)


def attend_body(place, part0, part1, weight, bias, out0, out1, projected, log_totals, gathered, attended):
    parts = (part0, part1)
    count, halves, cols, width = part0.shape
    block = halves * cols
    tokens = len(parts) * block
    me = place[0]
    for l in range(count):
        for s, part in enumerate(parts):
            gathered[l, s * block : (s + 1) * block] = part[l].reshape(block, width)
    raw = jnp.dot(gathered[...].reshape(count * tokens, width), weight[...], preferred_element_type=F32)
    projected[...] = (raw + bias[...].astype(F32)).astype(BF16).reshape(count, tokens, 3 * width)
    log_totals[...] = jnp.zeros_like(log_totals)
    lanes = 2 * HEAD
    lane = lax.broadcasted_iota(jnp.int32, (1, lanes), 1)
    for l in range(count):

        def pair(n, carry, l=l):
            start = pl.multiple_of(n * lanes, lanes)
            query = projected[l, :, pl.ds(start, lanes)].astype(F32) * HEAD ** (-0.5)
            key = projected[l, :, pl.ds(pl.multiple_of(width + n * lanes, lanes), lanes)]
            value = projected[l, :, pl.ds(pl.multiple_of(2 * width + n * lanes, lanes), lanes)]
            total_rows = log_totals[l]
            mixed = []
            for h in range(2):
                masked = jnp.where(head_mask(lanes, h), query, 0.0).astype(BF16)
                scores = lax.dot_general(masked, key, (((1,), (1,)), ((), ())), preferred_element_type=F32)
                highest = jnp.max(scores, axis=-1, keepdims=True)
                raised = jnp.exp(scores - highest)
                totals = jnp.sum(raised, axis=-1, keepdims=True)
                weights = (raised * (1.0 / totals)).astype(BF16)
                mixed.append(jnp.dot(weights, value, preferred_element_type=F32))
                total_rows = jnp.where(lane == 2 * n + h, highest + jnp.log(totals), total_rows)
            log_totals[l] = total_rows
            both = jnp.where(head_mask(lanes, 0), mixed[0], mixed[1]).astype(BF16)
            attended[l, :, :, pl.ds(start, lanes)] = both.reshape(len(parts) * halves, cols, lanes)
            return carry

        lax.fori_loop(0, width // lanes, pair, 0, unroll=2)
    send_rows(attended, (out0, out1), me, halves, 1, 0)


def send_rows(values, outs, me, halves, before, shift):
    count, total = values.shape[:2]
    for s, out in enumerate(outs):
        strip = me ^ s
        for k in range(out.shape[1]):
            row = strip * halves - before + shift + k
            inside = ((row >= 0) & (row < total)).astype(F32)
            kept = jnp.clip(row, 0, total - 1)
            source = (me ^ (kept // halves)) * halves + kept % halves
            for l in range(count):
                out[l, k] = (values[l, source].astype(F32) * inside).astype(BF16)


def attend(place, parts, weight, bias):
    count, halves, cols, width = parts[0].shape
    tokens = len(parts) * halves * cols
    return call_whole(
        attend_body,
        (place, *parts, weight, bias),
        [((count, halves + 2, cols, width), BF16)] * 2
        + [((count, tokens, 3 * width), BF16), ((count, tokens, 2 * HEAD), F32)],
        [((count, tokens, width), BF16), ((count, len(parts) * halves, cols, width), BF16)],
    )


def middle_body(place, part0, part1, latents, modulation, weight, bias, normed, attended, branch, spread, rimmed, raw):
    count, rim_rows, cols, width = latents.shape
    rows = rim_rows - 4
    unpack_strips((part0, part1), spread, place[0], 0)
    for c in range(width // 128):
        rimmed[:, :, :, c * 128 : (c + 1) * 128] = spread[:, :, c].astype(BF16)
    attended[...] = rimmed[:, 2 : rows + 2]
    every = rimmed[...].reshape(count * rim_rows * cols, width)
    dotted = jnp.dot(every, weight[...], preferred_element_type=F32) + bias[...].astype(F32)
    raw[...] = dotted.reshape(count, rim_rows, cols, width)
    branch[...] = raw[:, 2 : rows + 2]
    for l in range(count):
        gate = modulation[l : l + 1, 2 * width : 3 * width]
        offset = modulation[l : l + 1, 3 * width : 4 * width]
        scaling = 1.0 + modulation[l : l + 1, 4 * width : 5 * width]

        def norm_row(r, carry, l=l, gate=gate, offset=offset, scaling=scaling):
            for h in range(0, cols, 16):
                middle = latents[l, r, h : h + 16].astype(F32) + gate * raw[l, r, h : h + 16]
                unit, _ = layer_unit(middle)
                normed[l, r, h : h + 16] = (unit * scaling + offset).astype(BF16)
            return carry

        lax.fori_loop(0, rim_rows, norm_row, 0)


def middle_part(place, parts, latents_rim, modulation, weight, bias):
    count, rim_rows, cols, width = latents_rim.shape
    rows = rim_rows - 4
    return call_whole(
        middle_body,
        (place, *parts, latents_rim, modulation, weight, bias),
        [
            (latents_rim.shape, BF16),
            ((count, rows, cols, width), BF16),
            ((count, rows, cols, width), F32),
        ],
        [(chunked(*latents_rim.shape), F32), (latents_rim.shape, BF16), (latents_rim.shape, F32)],
    )


def turn_body(
    place, branch_two, normed_grad, branch_one, attended, latents, cotangent, modulation, fc2_bias, weight,
    output, middle_grad, weight_grad, sums, bias_sums, out0, out1, branch_grad, spread,
):
    count, rows, cols, width = cotangent.shape
    bias_sums[...] = jnp.zeros_like(bias_sums)
    sums[...] = jnp.zeros_like(sums)
    for l in range(count):
        gate_one, _, scaling, gate_two = (
            modulation[l : l + 1, k * width : (k + 1) * width] for k in range(2, 6)
        )
        scaling = 1.0 + scaling

        def one_row(r, carry, l=l, gate_one=gate_one, scaling=scaling, gate_two=gate_two):
            for h in range(0, cols, 16):
                here = slice(h, h + 16)
                first = branch_one[l, r, here]
                second = branch_two[l, r, here] + fc2_bias[...].astype(F32)
                upstream = cotangent[l, r, here].astype(F32)
                middle = latents[l, r + 2, here].astype(F32) + gate_one * first
                output[l, r, here] = (middle + gate_two * second).astype(BF16)
                unit, inverse = layer_unit(middle)
                grad = normed_grad[l, r, here]
                pulled = upstream + unit_pull(unit, inverse, grad * scaling)
                middle_grad[l, r, here] = pulled
                rounded = (gate_one * pulled).astype(BF16)
                branch_grad[l, r, here] = rounded
                sums[l, 0] += fold_rows(pulled * first)
                sums[l, 1] += fold_rows(grad)
                sums[l, 2] += fold_rows(grad * unit)
                sums[l, 3] += fold_rows(upstream * second)
                bias_sums[0] += fold_rows(rounded.astype(F32))
                bias_sums[1] += fold_rows((gate_two * upstream).astype(BF16).astype(F32))
            return carry

        lax.fori_loop(0, rows, one_row, 0)
    tokens = count * rows * cols
    back = branch_grad[...].reshape(tokens, width)
    weight_grad[...] = lax.dot_general(
        back, attended[...].reshape(tokens, width), (((0,), (0,)), ((), ())), preferred_element_type=F32
    ).astype(BF16)
    raw = lax.dot_general(back, weight[...], (((1,), (1,)), ((), ())), preferred_element_type=F32)
    for c in range(width // 128):
        spread[:, :, c] = raw[:, c * 128 : (c + 1) * 128].reshape(count, rows, cols, 128)
    pack_strips(spread, (out0, out1), place[0])


def turn(place, branch_two, normed_grad, branch_one, attended, latents_rim, cotangent, modulation, fc2_bias, weight):
    count, rows, cols, width = cotangent.shape
    return call_whole(
        turn_body,
        (place, branch_two, normed_grad, branch_one, attended, latents_rim, cotangent, modulation, fc2_bias, weight),
        [
            (cotangent.shape, BF16),
            (cotangent.shape, F32),
            ((width, width), BF16),
            ((count, 4, 8, width), F32),
            ((2, 8, width), F32),
        ]
        + [((2, rows // 2, cols // 2, width), BF16)] * 2,
        [(cotangent.shape, BF16), (chunked(*cotangent.shape), F32)],
    )


def attend_back_body(
    place, up0, up1, part0, part1, projected, log_totals, weight,
    weight_here, weight_away, bias_sums, out0, out1, gathered, upstream, grads, spread, weight_grad,
):
    parts = (part0, part1)
    count, halves, cols, width = part0.shape
    block = halves * cols
    tokens = len(parts) * block
    me = place[0]
    for l in range(count):
        for s, (part, up) in enumerate(zip(parts, (up0, up1))):
            gathered[l, s * block : (s + 1) * block] = part[l].reshape(block, width)
            upstream[l, s * block : (s + 1) * block] = up[l].reshape(block, width)
    bias_sums[...] = jnp.zeros_like(bias_sums)
    lanes = 2 * HEAD
    lane = lax.broadcasted_iota(jnp.int32, (1, lanes), 1)
    turned = (((0,), (0,)), ((), ()))
    inner = (((1,), (1,)), ((), ()))
    for l in range(count):

        def pair(n, carry, l=l):
            here = [pl.ds(pl.multiple_of(k * width + n * lanes, lanes), lanes) for k in range(3)]
            query = projected[l, :, here[0]]
            key = projected[l, :, here[1]]
            value = projected[l, :, here[2]]
            up = upstream[l, :, here[0]]
            query_full = query.astype(F32) * HEAD ** (-0.5)
            up_full = up.astype(F32)
            found = []
            for h in range(2):
                mask = head_mask(lanes, h)
                total = jnp.sum(jnp.where(lane == 2 * n + h, log_totals[l], 0.0), axis=-1, keepdims=True)
                masked = jnp.where(mask, query_full, 0.0).astype(BF16)
                scores = lax.dot_general(masked, key, inner, preferred_element_type=F32)
                weights = jnp.exp(scores - total)
                value_grad = lax.dot_general(weights.astype(BF16), up, turned, preferred_element_type=F32)
                weight_side = lax.dot_general(
                    jnp.where(mask, up_full, 0.0).astype(BF16), value, inner, preferred_element_type=F32
                )
                weighted = jnp.sum(weights * weight_side, axis=-1, keepdims=True)
                score_grad = (weights * (weight_side - weighted)).astype(BF16)
                query_grad = jnp.dot(score_grad, key, preferred_element_type=F32) * HEAD ** (-0.5)
                key_grad = lax.dot_general(score_grad, query, turned, preferred_element_type=F32) * HEAD ** (-0.5)
                found.append((query_grad, key_grad, value_grad))
            mask = head_mask(lanes, 0)
            for k in range(3):
                both = jnp.where(mask, found[0][k], found[1][k]).astype(BF16)
                grads[l, :, here[k]] = both
                if k != 1:
                    bias_sums[k // 2, :, here[0]] += fold_rows(both.astype(F32))
            return carry

        lax.fori_loop(0, width // lanes, pair, 0, unroll=2)
    every = grads[...].reshape(count * tokens, 3 * width)
    weight_grad[...] = lax.dot_general(
        every, gathered[...].reshape(count * tokens, width), turned, preferred_element_type=F32
    ).reshape(weight_grad.shape)
    for j in range(weight_grad.shape[0]):
        weight_here[j] = weight_grad[j, me].astype(BF16)
        weight_away[j] = weight_grad[j, 1 - me].astype(BF16)
    raw = lax.dot_general(every, weight[...], inner, preferred_element_type=F32)
    spread[...] = raw.astype(BF16).reshape(count, len(parts) * halves, cols, width)
    send_rows(spread, (out0, out1), me, halves, me, 0)


def attend_back(place, ups, parts, projected, log_totals, weight):
    count, halves, cols, width = parts[0].shape
    tokens = len(parts) * halves * cols
    batch = lax.axis_size(BATCH)
    half_grad = (batch // 2, 3 * width // batch, width)
    return call_whole(
        attend_back_body,
        (place, *ups, *parts, projected, log_totals, weight),
        [(half_grad, BF16), (half_grad, BF16), ((2, 8, width), F32)] + [((count, halves + 1, cols, width), BF16)] * 2,
        [
            ((count, tokens, width), BF16),
            ((count, tokens, width), BF16),
            ((count, tokens, 3 * width), BF16),
            ((count, len(parts) * halves, cols, width), BF16),
            ((batch // 2, 2, 3 * width // batch, width), F32),
        ],
    )


def finish_body(
    place, part0, part1, latents, modulation, taps, middle_grad, latents_grad, sums, small,
    rimmed, normed, normed_grad,
):
    count, rows, cols, width = middle_grad.shape
    lanes = 128
    unpack_strips((part0, part1), rimmed, place[0], 1)
    for l in range(count):
        offset = modulation[l : l + 1, 0:width]
        scaling = 1.0 + modulation[l : l + 1, width : 2 * width]

        def norm_row(r, carry, l=l, offset=offset, scaling=scaling):
            for h in range(0, cols, 16):
                unit, _ = layer_unit(latents[l, r + 2, h : h + 16].astype(F32))
                normed[l, r, h : h + 16] = (unit * scaling + offset).astype(BF16).astype(F32)
            return carry

        lax.fori_loop(0, rows, norm_row, 0)
    for start in range(0, width, lanes):
        here = slice(start, start + lanes)
        tap = [taps[k : k + 1, here].astype(F32) for k in range(9)]
        found = tuple(jnp.zeros((8, lanes), F32) for _ in range(10))
        for l in range(count):

            def conv_row(r, found, l=l, here=here, tap=tap):
                near = [rimmed[l, r + 2 - a, here.start // lanes] for a in range(3)]
                parts = [sum(tap[3 * a + e] * near[a] for a in range(3)) for e in range(3)]
                normed_grad[l, r, :, here] = row_shift(parts[0], -1) + parts[1] + row_shift(parts[2], 1)
                value = normed[l, r, :, here]
                moved = [row_shift(value, 1), value, row_shift(value, -1)]
                added = [found[3 * a + e] + fold_rows(near[a] * moved[e]) for a in range(3) for e in range(3)]
                return tuple(added) + (found[9] + fold_rows(near[1]),)

            found = lax.fori_loop(0, rows, conv_row, found)
        for k in range(10):
            small[k : k + 1, here] = jnp.sum(found[k], axis=0, keepdims=True)
    sums[...] = jnp.zeros_like(sums)
    for l in range(count):
        scaling = 1.0 + modulation[l : l + 1, width : 2 * width]

        def pull_row(r, carry, l=l, scaling=scaling):
            for h in range(0, cols, 16):
                here = slice(h, h + 16)
                unit, inverse = layer_unit(latents[l, r + 2, here].astype(F32))
                grad = normed_grad[l, r, here]
                sums[l, 0] += fold_rows(grad)
                sums[l, 1] += fold_rows(grad * unit)
                pulled = middle_grad[l, r, here] + unit_pull(unit, inverse, grad * scaling)
                latents_grad[l, r, here] = pulled.astype(BF16)
            return carry

        lax.fori_loop(0, rows, pull_row, 0)


def finish(place, parts, latents_rim, modulation, taps, middle_grad):
    count, rows, cols, width = middle_grad.shape
    return call_whole(
        finish_body,
        (place, *parts, latents_rim, modulation, taps, middle_grad),
        [(middle_grad.shape, BF16), ((count, 2, 8, width), F32), ((16, width), F32)],
        [(chunked(count, rows + 2, cols, width), F32), (middle_grad.shape, F32), (middle_grad.shape, F32)],
    )


def fold_body(pieces, sources, outputs, *refs):
    mine = refs[0]
    heres, aways = refs[1 : 1 + sources], refs[1 + sources : 1 + 2 * sources]
    kept, sent = refs[1 + 2 * sources :][:outputs], refs[1 + 2 * sources + outputs :][:outputs]
    scratch = list(refs[1 + 2 * sources + 2 * outputs :])
    for source, row, rows, lane, lead, bit, out, out_row, out_lane in pieces:
        here, away = heres[source], aways[source]
        size = rows // (2 * lead)
        lanes, out_lanes = slice(lane, lane + FOLD), slice(out_lane, out_lane + FOLD)
        me = mine[bit]
        if size % 16:
            whole = scratch.pop(0)
            total = here[row : row + rows, lanes].astype(F32) + away[row : row + rows, lanes].astype(F32)
            whole[...] = total.reshape(lead, 2, size, FOLD)
            for side, place in ((kept, me), (sent, 1 - me)):
                picked = whole[:, place].reshape(lead * size, FOLD).astype(BF16)
                side[out][out_row : out_row + lead * size, out_lanes] = picked
            continue
        part = max(p for p in range(16, 97, 16) if size % p == 0)

        def one(n, carry, here=here, away=away, row=row, size=size, part=part, lanes=lanes, out=out,
                out_row=out_row, out_lanes=out_lanes, me=me):
            a, k = n // (size // part), n % (size // part)
            target = pl.ds(pl.multiple_of(out_row + a * size + k * part, 16), part)
            for side, place in ((kept, me), (sent, 1 - me)):
                origin = pl.ds(pl.multiple_of(row + (2 * a + place) * size + k * part, 16), part)
                total = here[origin, lanes].astype(F32) + away[origin, lanes].astype(F32)
                side[out][target, out_lanes] = total.astype(BF16)
            return carry

        lax.fori_loop(0, lead * size // part, one, 0)


FOLD = 768


def fold(pairs, bits, pieces, outs):
    mine = jnp.stack([(lax.axis_index(axis) >> bit) & 1 for axis, bit in bits]).astype(jnp.int32)
    scratch = [(p[4], 2, p[2] // (2 * p[4]), FOLD) for p in pieces if p[2] // (2 * p[4]) % 16]
    found = call_whole(
        partial(fold_body, pieces, len(pairs), len(outs)),
        (mine, *[pair[0] for pair in pairs], *[pair[1] for pair in pairs]),
        [(shape, BF16) for shape in outs] * 2,
        [(shape, F32) for shape in scratch],
    )
    return list(zip(found[: len(outs)], found[len(outs) :]))


def swap(pair, axis, bit):
    return pair[0], swap_bit(pair[1], axis, bit)


def quick_sums():
    return lax.axis_size(BATCH) == 8 and lax.axis_size(GRP) == 4


def exchange(parts):
    return parts[0], swap_bit(parts[1], BATCH, 0)


def on_device(
    latents,
    cotangent,
    timesteps,
    labels,
    time_weight,
    time_bias,
    label_table,
    ada_weight,
    ada_bias,
    conv_a,
    conv_a_bias,
    qkv_weight,
    qv_bias,
    proj_weight,
    proj_bias,
    fc1_weight,
    fc1_bias,
    conv_f,
    conv_f_bias,
    fc2_weight,
    fc2_bias,
):
    width = latents.shape[3]
    hidden_width = fc1_weight.shape[1]
    devices = lax.axis_size(BATCH) * lax.axis_size(GRP)
    slot = lax.axis_index(BATCH) * lax.axis_size(GRP) + lax.axis_index(GRP)

    strip = lax.axis_index(GRP)
    half = lax.axis_index(BATCH) & 1
    inside = jnp.stack([half == 1, half == 0])
    place = jnp.concatenate([half[None], inside.astype(jnp.int32)])
    numbers = jnp.stack([timesteps.astype(F32), labels.astype(F32)])
    other = swap_bit(numbers, BATCH, 0)
    numbers = jnp.where(half == strip >> 1, numbers, other)
    numbers = jnp.where((strip & 1) == 0, numbers[:, 0], numbers[:, 1])
    latents_rim = with_edges(to_pairs(latents), 2)
    cotangent = to_pairs(cotangent)
    cotangent_rim = with_edges(cotangent, 1)

    frequency_rows = sinusoid(numbers[:1], time_weight.shape[0])
    condition = exact_dot(frequency_rows, time_weight) + time_bias.astype(F32)
    picked = lax.dynamic_slice_in_dim(label_table, numbers[1].astype(jnp.int32), 1, axis=0)
    condition = condition + picked.astype(F32)
    active = condition * jax.nn.sigmoid(condition)
    modulation = exact_dot(active, ada_weight) + ada_bias.astype(F32)
    gate_two = modulation[:, None, None, 5 * width :]

    mixed = exchange(stem(place, latents_rim, modulation, conv_a, conv_a_bias))
    qkv_bias = jnp.concatenate([qv_bias[0:1], jnp.zeros_like(qv_bias[0:1]), qv_bias[1:2]], axis=1)
    *sent, projected, log_totals = attend(place, mixed, qkv_weight, qkv_bias)
    normed_rim, attended, branch_one = middle_part(
        place, exchange(sent), latents_rim, modulation, proj_weight, proj_bias
    )

    branch_two_rim = (gate_two * cotangent_rim.astype(F32)).astype(BF16)
    branch_two, normed_two_grad, fc1_here, fc1_away, fc2_here, fc2_away, ff_small = feed_forward(
        place, normed_rim, branch_two_rim, fc1_weight, fc1_bias, conv_f, conv_f_bias, fc2_weight
    )
    pairs = lax.axis_size(BATCH) // 2
    quick = quick_sums()
    fc1_pair = (fc1_here.reshape(-1, width), fc1_away.reshape(-1, width))
    fc2_pair = (fc2_here.reshape(-1, hidden_width), fc2_away.reshape(-1, hidden_width))
    fc1_pair = swap(fc1_pair, BATCH, 0)
    fc2_pair = swap(fc2_pair, BATCH, 0)
    lanes = range(0, hidden_width, width)
    near, far, by_x, by_y = (GRP, 0), (GRP, 1), (BATCH, 1), (BATCH, 2)
    if quick:
        fc1_rows, fc2_rows = fc1_pair[0].shape[0], fc2_pair[0].shape[0]
        fc1_pair, fc2_pair = fold(
            [fc1_pair, fc2_pair],
            [by_x, near],
            [(0, 0, fc1_rows, 0, 2, 0, 0, 0, 0)] + [(1, 0, fc2_rows, c, 8, 1, 1, 0, c) for c in lanes],
            [(fc1_rows // 2, width), (fc2_rows // 2, hidden_width)],
        )
        fc1_pair = swap(fc1_pair, *by_x)
        fc2_pair = swap(fc2_pair, *near)
    else:
        fc1_sum, fc2_sum = (
            scatter_rest((pair[0].astype(F32) + pair[1].astype(F32)).reshape(pairs, -1, pair[0].shape[1]), flip)
            for pair, flip in ((fc1_pair, False), (fc2_pair, True))
        )

    output, middle_grad, proj_grad, turn_sums, turn_bias, *sent = turn(
        place,
        branch_two.reshape(cotangent.shape),
        normed_two_grad.reshape(cotangent.shape),
        branch_one,
        attended,
        latents_rim,
        cotangent,
        modulation,
        fc2_bias,
        proj_weight,
    )
    output = from_pairs(output)
    turn_sums = jnp.sum(turn_sums, axis=2)
    turn_bias = jnp.sum(turn_bias, axis=1)

    def slots(vectors):
        return vectors.reshape(len(vectors), devices, -1).transpose(1, 0, 2).reshape(devices, -1)

    small = jnp.concatenate([slots(ff_small[:11]), slots(turn_bias)], axis=1).astype(BF16)
    small_length = small.shape[1]
    small_lanes = -(-small_length // 8)
    small = jnp.pad(small, ((0, 0), (0, small_lanes * 8 - small_length))).reshape(devices, 8, small_lanes)
    small = jnp.pad(small, ((0, 0), (0, 0), (0, width - small_lanes)))
    beside = jnp.concatenate([proj_grad.reshape(devices, -1, width), small], axis=1).reshape(pairs, 2, -1, width)
    beside_pair = tuple(
        lax.dynamic_index_in_dim(beside, side, 1, keepdims=False).reshape(-1, width) for side in (half, 1 - half)
    )
    beside_pair = swap(beside_pair, BATCH, 0)

    qkv_here, qkv_away, qv_sums, *sent = attend_back(
        place, exchange(sent), mixed, projected, log_totals, qkv_weight
    )
    qkv_pair = swap((qkv_here.reshape(-1, width), qkv_away.reshape(-1, width)), BATCH, 0)
    if quick:
        beside_rows, qkv_rows = beside_pair[0].shape[0], qkv_pair[0].shape[0]
        fc1_pair, fc2_pair, beside_pair = fold(
            [fc1_pair, fc2_pair, beside_pair],
            [by_y, far, by_x],
            [(0, 0, fc1_rows // 2, 0, 1, 0, 0, 0, 0)]
            + [(1, 0, fc2_rows // 2, c, 4, 1, 1, 0, c) for c in lanes]
            + [(2, 0, beside_rows, 0, 2, 2, 2, 0, 0)],
            [(fc1_rows // 4, width), (fc2_rows // 4, hidden_width), (beside_rows // 2, width)],
        )
        fc1_pair = swap(fc1_pair, *by_y)
        fc2_pair = swap(fc2_pair, *far)
        beside_pair = swap(beside_pair, *by_x)
        (qkv_pair,) = fold([qkv_pair], [by_x], [(0, 0, qkv_rows, 0, 2, 0, 0, 0, 0)], [(qkv_rows // 2, width)])
        qkv_pair = swap(qkv_pair, *by_x)
    else:
        beside, qkv_sum = (
            scatter_rest((pair[0].astype(F32) + pair[1].astype(F32)).reshape(pairs, -1, width), flip)
            for pair, flip in ((beside_pair, False), (qkv_pair, True))
        )
    latents_grad, finish_sums, conv_a_small = finish(
        place, exchange(sent), latents_rim, modulation, conv_a, middle_grad
    )
    latents_grad = from_pairs(latents_grad)
    if quick:
        fc1_rows, fc2_rows, beside_rows, qkv_rows = fc1_rows // 4, fc2_rows // 4, beside_rows // 2, qkv_rows // 2
        fc1_pair, fc2_pair = fold(
            [fc1_pair, fc2_pair],
            [near, by_x],
            [(0, 0, fc1_rows, 0, 2, 0, 0, 0, 0)]
            + [(1, 0, fc2_rows, c, 2, 1, 1, k * (fc2_rows // 2), 0) for k, c in enumerate(lanes)],
            [(fc1_rows // 2, width), (len(lanes) * fc2_rows // 2, width)],
        )
        fc1_pair = swap(fc1_pair, *near)
        fc2_pair = swap(fc2_pair, *by_x)
        (attention_pair,) = fold(
            [beside_pair, qkv_pair],
            [by_y],
            [(0, 0, beside_rows, 0, 1, 0, 0, 0, 0), (1, 0, qkv_rows, 0, 1, 0, 0, beside_rows // 2, 0)],
            [((beside_rows + qkv_rows) // 2, width)],
        )
        attention_pair = swap(attention_pair, *by_y)
        fc1_rows, fc2_rows = fc1_rows // 2, len(lanes) * fc2_rows // 2
        beside_rows, qkv_rows = beside_rows // 2, qkv_rows // 2
        fc1_pair, fc2_pair, attention_pair = fold(
            [fc1_pair, fc2_pair, attention_pair],
            [far, by_y, near],
            [
                (0, 0, fc1_rows, 0, 1, 0, 0, 0, 0),
                (1, 0, fc2_rows, 0, len(lanes), 1, 1, 0, 0),
                (2, 0, beside_rows, 0, 2, 2, 2, 0, 0),
                (2, beside_rows, qkv_rows, 0, 2, 2, 2, beside_rows // 2, 0),
            ],
            [(fc1_rows // 2, width), (fc2_rows // 2, width), ((beside_rows + qkv_rows) // 2, width)],
        )
        fc1_pair = swap(fc1_pair, *far)
        fc2_pair = swap(fc2_pair, *by_y)
        attention_pair = swap(attention_pair, *near)
        beside_rows, qkv_rows = beside_rows // 2, qkv_rows // 2
        (attention_pair,) = fold(
            [attention_pair],
            [far],
            [(0, 0, beside_rows, 0, 1, 0, 0, 0, 0), (0, beside_rows, qkv_rows, 0, 1, 0, 0, beside_rows // 2, 0)],
            [((beside_rows + qkv_rows) // 2, width)],
        )
        attention_pair = swap(attention_pair, *far)
        fc1_sum, fc2_sum, attention_sum = (
            pair[0].astype(F32) + pair[1].astype(F32) for pair in (fc1_pair, fc2_pair, attention_pair)
        )
        fc2_sum = fc2_sum.reshape(len(lanes), -1, width).transpose(1, 0, 2).reshape(-1, hidden_width)
        beside, qkv_sum = attention_sum[: beside_rows // 2], attention_sum[beside_rows // 2 :]
    proj_sum = beside[:-8]
    small_sum = beside[-8:, :small_lanes].reshape(-1)
    wide_length = 11 * (hidden_width // devices)
    wide_sum = small_sum[:wide_length].reshape(11, -1)
    narrow_sum = small_sum[wide_length:small_length].reshape(2, -1)
    finish_sums = jnp.sum(finish_sums, axis=2)

    late = jnp.concatenate([conv_a_small[:10], jnp.sum(qv_sums, axis=1), jnp.zeros((4, width), F32)], axis=0)
    modulation_grad = jnp.concatenate([finish_sums[0], turn_sums[0], jnp.zeros((2, width), F32)], axis=0)
    side = jnp.concatenate(
        [condition, jnp.pad(frequency_rows, ((0, 0), (0, width - frequency_rows.shape[1] - 1))), numbers[1:][None]],
        axis=1,
    )
    every, late_sum = gather_sum(jnp.pad(side.reshape(2, width), ((6, 0), (0, 0))), modulation_grad, late)
    every = every.reshape(-1, 8, width)
    every_grad = every[:, :6].reshape(-1, 6 * width)
    every_condition = every[:, 6]
    every_frequency = every[:, 7, : frequency_rows.shape[1]]
    every_label = every[:, 7, -1].astype(jnp.int32)
    late_sum = lax.dynamic_slice_in_dim(late_sum, slot * (width // devices), width // devices, axis=1)
    sigmoid = jax.nn.sigmoid(every_condition)
    every_active = every_condition * sigmoid
    narrow_width = width // devices
    ada_width = 6 * width // devices
    ada_part = lax.dynamic_slice_in_dim(every_grad, slot * ada_width, ada_width, axis=1)
    ada_grad = lax.dot_general(
        every_active, ada_part, (((0,), (0,)), ((), ())), precision=HIGHEST, preferred_element_type=F32
    )
    ada_bias_grad = jnp.sum(ada_part, axis=0)[None, :]
    ada_rows = lax.dynamic_slice_in_dim(ada_weight, slot * narrow_width, narrow_width, axis=0)
    active_grad = lax.dot_general(
        every_grad, ada_rows.astype(F32), (((1,), (1,)), ((), ())), precision=HIGHEST
    )
    slope_silu = lax.dynamic_slice_in_dim(
        sigmoid * (1.0 + every_condition * (1.0 - sigmoid)), slot * narrow_width, narrow_width, axis=1
    )
    condition_grad = active_grad * slope_silu
    onehot = (every_label[:, None] == jnp.arange(label_table.shape[0], dtype=jnp.int32)[None, :]).astype(F32)
    table_grad = lax.dot_general(onehot, condition_grad, (((0,), (0,)), ((), ())), precision=HIGHEST)
    time_grad = lax.dot_general(
        every_frequency, condition_grad, (((0,), (0,)), ((), ())), precision=HIGHEST
    )
    time_bias_grad = jnp.sum(condition_grad, axis=0)[None, :]

    return (
        output,
        latents_grad,
        time_grad,
        time_bias_grad,
        table_grad,
        ada_grad,
        ada_bias_grad,
        late_sum[0:9],
        late_sum[9:10],
        qkv_sum.T,
        late_sum[10:12],
        proj_sum.T,
        narrow_sum[0:1],
        fc1_sum.T,
        wide_sum[10:11],
        wide_sum[0:9],
        wide_sum[9:10],
        fc2_sum.T,
        narrow_sum[1:2],
    )


def solution(mesh):
    columns = P(None, (BATCH, GRP))
    return jax.shard_map(
        on_device,
        mesh=mesh,
        in_specs=(P(BATCH, GRP, None, None), P(BATCH, GRP, None, None), P(BATCH), P(BATCH)) + (P(),) * 17,
        out_specs=(P(BATCH, GRP, None, None), P(BATCH, GRP, None, None)) + (columns,) * 17,
        check_vma=False,
    )
```

```python
from functools import partial
import math

import jax
import jax.numpy as jnp
from jax import lax
from jax.experimental import pallas as pl
from jax.experimental.pallas import tpu as pltpu
from jax.sharding import PartitionSpec as P


HEAD = 64
BATCH, GRP = "batch", "grp"
HIGHEST = lax.Precision.HIGHEST
F32 = jnp.float32
BF16 = jnp.bfloat16
GELU_C = math.sqrt(2.0 / math.pi)


def swap_bit(value, axis, bit):
    count = lax.axis_size(axis)
    return lax.ppermute(value, axis, [(i, i ^ (1 << bit)) for i in range(count)])


def to_pairs(block):
    strip = lax.axis_index(GRP)
    odd = strip & 1
    arrived = []
    for k in range(2):
        piece = lax.dynamic_slice_in_dim(block, k ^ odd, 1, axis=0)
        arrived.append(lax.ppermute(piece, (BATCH, GRP), pair_moves(k)))
    swapped = odd == 1
    upper = jnp.where(swapped, arrived[1], arrived[0])
    lower = jnp.where(swapped, arrived[0], arrived[1])
    return jnp.concatenate([upper, lower], axis=1)


def pair_moves(k, back=False):
    strips = lax.axis_size(GRP)
    moves = []
    for b in range(lax.axis_size(BATCH)):
        for z in range(strips):
            to = (2 * (b // 2) + (z >> 1)) * strips + 2 * (b & 1) + (k ^ (z & 1))
            moves.append((to, b * strips + z) if back else (b * strips + z, to))
    return moves


def from_pairs(block):
    rows = block.shape[1] // 2
    odd = lax.axis_index(GRP) & 1
    arrived = []
    for k in range(2):
        piece = lax.dynamic_slice_in_dim(block, (k ^ odd) * rows, rows, axis=1)
        arrived.append(lax.ppermute(piece, (BATCH, GRP), pair_moves(k, True)))
    swapped = odd == 1
    first = jnp.where(swapped, arrived[1], arrived[0])
    second = jnp.where(swapped, arrived[0], arrived[1])
    return jnp.concatenate([first, second], axis=0)


def with_edges(block, width):
    rows = block.shape[1]
    lower = (lax.axis_index(BATCH) & 1) == 1
    edge = jnp.where(lower, block[:, :width], block[:, rows - width :])
    other = swap_bit(edge, BATCH, 0)
    zero = jnp.zeros_like(other)
    return jnp.concatenate([jnp.where(lower, other, zero), block, jnp.where(lower, zero, other)], axis=1)


def halve(here, away, axis, bit):
    arrived = swap_bit(away, axis, bit)
    return here.astype(F32) + arrived.astype(F32)


def halve_dim(block, place, axis, bit):
    mine = (lax.axis_index(axis) >> bit) & 1
    away = lax.dynamic_index_in_dim(block, 1 - mine, place, keepdims=False)
    here = lax.dynamic_index_in_dim(block, mine, place, keepdims=False)
    return halve(here, away, axis, bit)


def scatter_rest(block, swapped):
    high = list(range(1, lax.axis_size(BATCH).bit_length() - 1))
    left = high[::-1]
    _, rows, width = block.shape
    block = block.reshape((2,) * len(high) + (rows, width))
    for bit in high[::-1] if swapped else high:
        block = halve_dim(block.astype(BF16), left.index(bit), BATCH, bit)
        left.remove(bit)
    bits = lax.axis_size(GRP).bit_length() - 1
    block = block.reshape((2,) * bits + (-1, width))
    for bit in range(bits):
        block = halve_dim(block.astype(BF16), bits - 1 - bit, GRP, bit)
    return block


def gather_sum(rows, pair_rows, summed):
    length = pair_rows.shape[0]
    bits = [(GRP, bit) for bit in range(lax.axis_size(GRP).bit_length() - 1)]
    bits += [(BATCH, bit) for bit in range(1, lax.axis_size(BATCH).bit_length() - 1)]
    length = pair_rows.shape[0]
    both = jnp.concatenate([pair_rows, summed], axis=0)
    other = swap_bit(both, BATCH, 0)
    both = both + other
    rows = both[:length] + rows
    summed = both[length:]
    for axis, bit in bits:
        sent = jnp.concatenate([summed, rows], axis=0)
        other = swap_bit(sent, axis, bit)
        summed = summed + other[: len(summed)]
        rows = jnp.concatenate([rows, other[len(summed) :]], axis=0)
    return rows, summed


def exact_dot(left, right):
    high = lax.reduce_precision(left, 8, 7)
    rest = left - high
    middle = lax.reduce_precision(rest, 8, 7)
    low = rest - middle
    rows = jnp.concatenate([high, middle, low], axis=0).astype(BF16)
    out = jnp.dot(rows, right, preferred_element_type=F32)
    count = left.shape[0]
    return out[:count] + (out[count : 2 * count] + out[2 * count :])


def sinusoid(timestep, length):
    halfway = length // 2
    frequency = jnp.exp(-math.log(10000.0) * jnp.arange(halfway, dtype=F32) / halfway)
    angles = timestep.astype(F32)[:, None] * frequency[None, :]
    return jnp.concatenate([jnp.cos(angles), jnp.sin(angles)], axis=1)


def unit_pull(unit, inverse, grad):
    first = jnp.mean(grad, axis=-1, keepdims=True)
    second = jnp.mean(grad * unit, axis=-1, keepdims=True)
    return inverse * (grad - first - unit * second)


def row_shift(values, step):
    cols = values.shape[0]
    place = lax.broadcasted_iota(jnp.int32, values.shape, 0)
    rolled = pltpu.roll(values, step % cols, 0)
    return jnp.where(place == (0 if step == 1 else cols - 1), 0.0, rolled)


def fold_rows(values):
    total = values[0:8]
    for start in range(8, values.shape[0], 8):
        total = total + values[start : start + 8]
    return total


def feed_forward_body(
    place, normed, upstream, fc1, fc1_bias, taps, conv_bias, fc2,
    branch_out, normed_grad_out, fc1_here, fc1_away, fc2_here, fc2_away, small_out,
    hidden, lifted, activated, convolved_grad, hidden_grad, fc1_grad, fc2_grad,
):
    count, rim_rows, cols, width = normed.shape
    rows = rim_rows - 4
    tile = fc1.shape[1]
    lanes = 128
    raw = jnp.dot(
        normed[...].reshape(count * rim_rows * cols, width), fc1[...], preferred_element_type=F32
    ) + fc1_bias[...].astype(F32)
    hidden[...] = raw.astype(BF16).astype(F32).reshape(count, rim_rows, cols, tile)
    hidden[:, 0:2] = hidden[:, 0:2] * place[1].astype(F32)
    hidden[:, rows + 2 :] = hidden[:, rows + 2 :] * place[2].astype(F32)
    lifted[...] = lax.dot_general(
        upstream[...].reshape(count * (rows + 2) * cols, width),
        fc2[...],
        (((1,), (1,)), ((), ())),
        preferred_element_type=F32,
    ).reshape(count, rows + 2, cols, tile)
    for start in range(0, tile, lanes):
        here = slice(start, start + lanes)
        tap = [taps[k : k + 1, here].astype(F32) for k in range(9)]
        bias = conv_bias[:, here].astype(F32)

        def forward_row(l, r, sums):
            near = [hidden[l, r + a, :, here] for a in range(3)]
            parts = [sum(tap[3 * a + e] * near[a] for a in range(3)) for e in range(3)]
            value = row_shift(parts[0], 1) + parts[1] + row_shift(parts[2], -1) + bias
            square = value * value
            bent = jnp.tanh(value * (GELU_C + GELU_C * 0.044715 * square))
            half = 0.5 * (1.0 + bent)
            activated[l, r, :, here] = (value * half).astype(BF16)
            slope = half + value * half * (1.0 - bent) * (GELU_C + 3.0 * 0.044715 * GELU_C * square)
            grad = (lifted[l, r, :, here] * slope).astype(BF16).astype(F32)
            convolved_grad[l, r, :, here] = grad
            if sums is None:
                return None
            moved = [row_shift(grad, -1), grad, row_shift(grad, 1)]
            added = [sums[3 * a + e] + fold_rows(near[a] * moved[e]) for a in range(3) for e in range(3)]
            return tuple(added) + (sums[9] + fold_rows(grad),)

        sums = tuple(jnp.zeros((8, lanes), F32) for _ in range(10))
        bias_sum = jnp.zeros((8, lanes), F32)
        for l in range(count):
            forward_row(l, 0, None)
            forward_row(l, rows + 1, None)
            sums = lax.fori_loop(1, rows + 1, lambda r, sums, l=l: forward_row(l, r, sums), sums, unroll=2)

            def backward_row(r, bias_sum, l=l):
                near = [convolved_grad[l, r + 2 - a, :, here] for a in range(3)]
                parts = [sum(tap[3 * a + e] * near[a] for a in range(3)) for e in range(3)]
                value = row_shift(parts[0], -1) + parts[1] + row_shift(parts[2], 1)
                rounded = value.astype(BF16)
                hidden_grad[l, r, :, here] = rounded
                return bias_sum + fold_rows(rounded.astype(F32))

            bias_sum = lax.fori_loop(0, rows, backward_row, bias_sum, unroll=2)
        for k in range(10):
            small_out[k : k + 1, here] = jnp.sum(sums[k], axis=0, keepdims=True)
        small_out[10:11, here] = jnp.sum(bias_sum, axis=0, keepdims=True)
    tokens = count * rows * cols
    active = activated[:, 1 : rows + 1].reshape(tokens, tile)
    back = hidden_grad[...].reshape(tokens, tile)
    inner = normed[:, 2 : rows + 2].reshape(tokens, width)
    above = upstream[:, 1 : rows + 1].reshape(tokens, width)

    @pl.when(pl.program_id(0) == 0)
    def _():
        branch_out[...] = jnp.zeros_like(branch_out)
        normed_grad_out[...] = jnp.zeros_like(normed_grad_out)

    branch_out[...] += jnp.dot(active, fc2[...], preferred_element_type=F32)
    normed_grad_out[...] += lax.dot_general(
        back, fc1[...], (((1,), (1,)), ((), ())), preferred_element_type=F32
    )
    me = place[0]
    fc1_grad[...] = lax.dot_general(
        back, inner, (((0,), (0,)), ((), ())), preferred_element_type=F32
    ).astype(BF16).reshape(fc1_grad.shape)
    for j in range(fc1_grad.shape[0]):
        fc1_here[0, j] = fc1_grad[j, me]
        fc1_away[0, j] = fc1_grad[j, 1 - me]
    fc2_grad[...] = lax.dot_general(
        above, active, (((0,), (0,)), ((), ())), preferred_element_type=F32
    ).reshape(fc2_grad.shape)
    for j in range(fc2_grad.shape[0]):
        fc2_here[j] = fc2_grad[j, me].astype(BF16)
        fc2_away[j] = fc2_grad[j, 1 - me].astype(BF16)


def feed_forward(place, normed, upstream, fc1, fc1_bias, taps, conv_bias, fc2):
    count, rim_rows, cols, width = normed.shape
    rows = rim_rows - 4
    tokens = count * rows * cols
    units = fc1.shape[1]
    tile = 768
    steps = units // tile
    batch = lax.axis_size(BATCH)
    fc1_block = (1, batch // 2 // steps, units // batch, width)
    fc2_block = (batch // 2, width // batch, tile)
    return pl.pallas_call(
        feed_forward_body,
        grid=(steps,),
        in_specs=[
            pl.BlockSpec(memory_space=pltpu.SMEM),
            pl.BlockSpec(normed.shape, lambda i: (0, 0, 0, 0)),
            pl.BlockSpec(upstream.shape, lambda i: (0, 0, 0, 0)),
            pl.BlockSpec((width, tile), lambda i: (0, i)),
            pl.BlockSpec((1, tile), lambda i: (0, i)),
            pl.BlockSpec((9, tile), lambda i: (0, i)),
            pl.BlockSpec((1, tile), lambda i: (0, i)),
            pl.BlockSpec((tile, width), lambda i: (i, 0)),
        ],
        out_specs=[
            pl.BlockSpec((tokens, width), lambda i: (0, 0)),
            pl.BlockSpec((tokens, width), lambda i: (0, 0)),
            pl.BlockSpec(fc1_block, lambda i: (i, 0, 0, 0)),
            pl.BlockSpec(fc1_block, lambda i: (i, 0, 0, 0)),
            pl.BlockSpec(fc2_block, lambda i: (0, 0, i)),
            pl.BlockSpec(fc2_block, lambda i: (0, 0, i)),
            pl.BlockSpec((16, tile), lambda i: (0, i)),
        ],
        out_shape=[
            jax.ShapeDtypeStruct((tokens, width), F32),
            jax.ShapeDtypeStruct((tokens, width), F32),
            jax.ShapeDtypeStruct((steps,) + fc1_block[1:], BF16),
            jax.ShapeDtypeStruct((steps,) + fc1_block[1:], BF16),
            jax.ShapeDtypeStruct(fc2_block[:2] + (units,), BF16),
            jax.ShapeDtypeStruct(fc2_block[:2] + (units,), BF16),
            jax.ShapeDtypeStruct((16, units), F32),
        ],
        scratch_shapes=[
            pltpu.VMEM((count, rim_rows, cols, tile), F32),
            pltpu.VMEM((count, rows + 2, cols, tile), F32),
            pltpu.VMEM((count, rows + 2, cols, tile), BF16),
            pltpu.VMEM((count, rows + 2, cols, tile), F32),
            pltpu.VMEM((count, rows, cols, tile), BF16),
            pltpu.VMEM((fc1_block[1], 2) + fc1_block[2:], BF16),
            pltpu.VMEM((batch // 2, 2, width // batch, tile), F32),
        ],
        compiler_params=pltpu.CompilerParams(
            dimension_semantics=("arbitrary",), vmem_limit_bytes=48 * 1024 * 1024
        ),
        name="feed_forward",
    )(place, normed, upstream, fc1, fc1_bias, taps, conv_bias, fc2)


def layer_unit(values):
    centre = jnp.mean(values, axis=-1, keepdims=True)
    centred = values - centre
    inverse = lax.rsqrt(jnp.mean(centred * centred, axis=-1, keepdims=True) + 1e-06)
    return centred * inverse, inverse


def chunked(count, rows, cols, width):
    return (count, rows, width // 128, cols, 128)


def half_rows(start):
    return pl.ds(start, 16, stride=2)


def pack_strips(values, outs, me):
    _, rows, chunks, _, lanes = values.shape

    def one(i, carry):
        for s, out in enumerate(outs):
            row = 2 * i + (me ^ s)
            for q in range(2):
                for c in range(chunks):
                    out[q, i, :, c * lanes : (c + 1) * lanes] = values[0, row, c, half_rows(q), :].astype(BF16)
        return carry

    lax.fori_loop(0, rows // 2, one, 0)


def unpack_strips(parts, values, me, first):
    halves = parts[0].shape[1]
    chunks, _, lanes = values.shape[2:]

    def one(i, carry):
        for s, part in enumerate(parts):
            row = 2 * i + (me ^ s ^ first)
            for q in range(2):
                full = part[q, i].astype(F32)
                for c in range(chunks):
                    values[0, row, c, half_rows(q), :] = full[:, c * lanes : (c + 1) * lanes]
        return carry

    lax.fori_loop(0, halves, one, 0)


def stem_body(place, latents, modulation, taps, conv_bias, out0, out1, normed, mixed):
    count, rim_rows, cols, width = normed.shape
    rows = rim_rows - 2
    lanes = 128
    for l in range(count):
        offset = modulation[l : l + 1, 0:width]
        scaling = 1.0 + modulation[l : l + 1, width : 2 * width]

        def norm_row(r, carry, l=l, offset=offset, scaling=scaling):
            for h in range(0, cols, 16):
                unit, _ = layer_unit(latents[l, r + 1, h : h + 16].astype(F32))
                normed[l, r, h : h + 16] = (unit * scaling + offset).astype(BF16).astype(F32)
            return carry

        lax.fori_loop(0, rim_rows, norm_row, 0, unroll=2)
        normed[l, 0] = normed[l, 0] * place[1].astype(F32)
        normed[l, rows + 1] = normed[l, rows + 1] * place[2].astype(F32)
    for start in range(0, width, lanes):
        here = slice(start, start + lanes)
        tap = [taps[k : k + 1, here].astype(F32) for k in range(9)]
        bias = conv_bias[:, here].astype(F32)
        for l in range(count):

            def conv_row(r, carry, l=l, here=here, tap=tap, bias=bias):
                near = [normed[l, r + a, :, here] for a in range(3)]
                parts = [sum(tap[3 * a + e] * near[a] for a in range(3)) for e in range(3)]
                total = row_shift(parts[0], 1) + parts[1] + row_shift(parts[2], -1) + bias
                mixed[l, r, here.start // lanes] = total
                return carry

            lax.fori_loop(0, rows, conv_row, 0, unroll=2)
    pack_strips(mixed, (out0, out1), place[0])


WHOLE = pl.BlockSpec(memory_space=pltpu.VMEM)
SCALARS = pl.BlockSpec(memory_space=pltpu.SMEM)


def call_whole(body, inputs, outputs, scratch):
    return pl.pallas_call(
        body,
        in_specs=[SCALARS] + [WHOLE] * (len(inputs) - 1),
        out_specs=[WHOLE] * len(outputs),
        out_shape=[jax.ShapeDtypeStruct(shape, kind) for shape, kind in outputs],
        scratch_shapes=[pltpu.VMEM(shape, kind) for shape, kind in scratch],
        compiler_params=pltpu.CompilerParams(vmem_limit_bytes=56 * 1024 * 1024),
    )(*inputs)


def stem(place, latents_rim, modulation, taps, conv_bias):
    count, rim_rows, cols, width = latents_rim.shape
    rows = rim_rows - 4
    return call_whole(
        stem_body,
        (place, latents_rim, modulation, taps, conv_bias),
        [((2, rows // 2, cols // 2, width), BF16)] * 2,
        [((count, rows + 2, cols, width), F32), (chunked(count, rows, cols, width), F32)],
    )


def head_mask(lanes, h):
    lane = lax.broadcasted_iota(jnp.int32, (1, lanes), 1)
    return (lane >= h * HEAD) & (lane < (h + 1) * HEAD)


def attend_body(place, part0, part1, weight, bias, out0, out1, projected, log_totals, gathered, attended):
    parts = (part0, part1)
    count, halves, cols, width = part0.shape
    block = halves * cols
    tokens = len(parts) * block
    me = place[0]
    for l in range(count):
        for s, part in enumerate(parts):
            gathered[l, s * block : (s + 1) * block] = part[l].reshape(block, width)
    raw = jnp.dot(gathered[...].reshape(count * tokens, width), weight[...], preferred_element_type=F32)
    projected[...] = (raw + bias[...].astype(F32)).astype(BF16).reshape(count, tokens, 3 * width)
    log_totals[...] = jnp.zeros_like(log_totals)
    lanes = 2 * HEAD
    lane = lax.broadcasted_iota(jnp.int32, (1, lanes), 1)
    for l in range(count):

        def pair(n, carry, l=l):
            start = pl.multiple_of(n * lanes, lanes)
            query = projected[l, :, pl.ds(start, lanes)].astype(F32) * HEAD ** (-0.5)
            key = projected[l, :, pl.ds(pl.multiple_of(width + n * lanes, lanes), lanes)]
            value = projected[l, :, pl.ds(pl.multiple_of(2 * width + n * lanes, lanes), lanes)]
            total_rows = log_totals[l]
            mixed = []
            for h in range(2):
                masked = jnp.where(head_mask(lanes, h), query, 0.0).astype(BF16)
                scores = lax.dot_general(masked, key, (((1,), (1,)), ((), ())), preferred_element_type=F32)
                highest = jnp.max(scores, axis=-1, keepdims=True)
                raised = jnp.exp(scores - highest)
                totals = jnp.sum(raised, axis=-1, keepdims=True)
                weights = (raised * (1.0 / totals)).astype(BF16)
                mixed.append(jnp.dot(weights, value, preferred_element_type=F32))
                total_rows = jnp.where(lane == 2 * n + h, highest + jnp.log(totals), total_rows)
            log_totals[l] = total_rows
            both = jnp.where(head_mask(lanes, 0), mixed[0], mixed[1]).astype(BF16)
            attended[l, :, :, pl.ds(start, lanes)] = both.reshape(len(parts) * halves, cols, lanes)
            return carry

        lax.fori_loop(0, width // lanes, pair, 0, unroll=3)
    send_rows(attended, (out0, out1), me, halves, 1, 0)


def send_rows(values, outs, me, halves, before, shift):
    count, total = values.shape[:2]
    for s, out in enumerate(outs):
        strip = me ^ s
        for k in range(out.shape[1]):
            row = strip * halves - before + shift + k
            inside = ((row >= 0) & (row < total)).astype(F32)
            kept = jnp.clip(row, 0, total - 1)
            source = (me ^ (kept // halves)) * halves + kept % halves
            for l in range(count):
                out[l, k] = (values[l, source].astype(F32) * inside).astype(BF16)


def attend(place, parts, weight, bias):
    count, halves, cols, width = parts[0].shape
    tokens = len(parts) * halves * cols
    return call_whole(
        attend_body,
        (place, *parts, weight, bias),
        [((count, halves + 2, cols, width), BF16)] * 2
        + [((count, tokens, 3 * width), BF16), ((count, tokens, 2 * HEAD), F32)],
        [((count, tokens, width), BF16), ((count, len(parts) * halves, cols, width), BF16)],
    )


def middle_body(place, part0, part1, latents, modulation, weight, bias, normed, attended, branch, spread, rimmed, raw):
    count, rim_rows, cols, width = latents.shape
    rows = rim_rows - 4
    unpack_strips((part0, part1), spread, place[0], 0)
    for c in range(width // 128):
        rimmed[:, :, :, c * 128 : (c + 1) * 128] = spread[:, :, c].astype(BF16)
    attended[...] = rimmed[:, 2 : rows + 2]
    every = rimmed[...].reshape(count * rim_rows * cols, width)
    dotted = jnp.dot(every, weight[...], preferred_element_type=F32) + bias[...].astype(F32)
    raw[...] = dotted.reshape(count, rim_rows, cols, width)
    branch[...] = raw[:, 2 : rows + 2]
    for l in range(count):
        gate = modulation[l : l + 1, 2 * width : 3 * width]
        offset = modulation[l : l + 1, 3 * width : 4 * width]
        scaling = 1.0 + modulation[l : l + 1, 4 * width : 5 * width]

        def norm_row(r, carry, l=l, gate=gate, offset=offset, scaling=scaling):
            for h in range(0, cols, 16):
                middle = latents[l, r, h : h + 16].astype(F32) + gate * raw[l, r, h : h + 16]
                unit, _ = layer_unit(middle)
                normed[l, r, h : h + 16] = (unit * scaling + offset).astype(BF16)
            return carry

        lax.fori_loop(0, rim_rows, norm_row, 0, unroll=2)


def middle_part(place, parts, latents_rim, modulation, weight, bias):
    count, rim_rows, cols, width = latents_rim.shape
    rows = rim_rows - 4
    return call_whole(
        middle_body,
        (place, *parts, latents_rim, modulation, weight, bias),
        [
            (latents_rim.shape, BF16),
            ((count, rows, cols, width), BF16),
            ((count, rows, cols, width), F32),
        ],
        [(chunked(*latents_rim.shape), F32), (latents_rim.shape, BF16), (latents_rim.shape, F32)],
    )


def turn_body(
    place, branch_two, normed_grad, branch_one, attended, latents, cotangent, modulation, fc2_bias, weight,
    output, middle_grad, weight_grad, sums, bias_sums, out0, out1, branch_grad, spread,
):
    count, rows, cols, width = cotangent.shape
    bias_sums[...] = jnp.zeros_like(bias_sums)
    sums[...] = jnp.zeros_like(sums)
    for l in range(count):
        gate_one, _, scaling, gate_two = (
            modulation[l : l + 1, k * width : (k + 1) * width] for k in range(2, 6)
        )
        scaling = 1.0 + scaling

        def one_row(r, carry, l=l, gate_one=gate_one, scaling=scaling, gate_two=gate_two):
            for h in range(0, cols, 16):
                here = slice(h, h + 16)
                first = branch_one[l, r, here]
                second = branch_two[l, r, here] + fc2_bias[...].astype(F32)
                upstream = cotangent[l, r, here].astype(F32)
                middle = latents[l, r + 2, here].astype(F32) + gate_one * first
                output[l, r, here] = (middle + gate_two * second).astype(BF16)
                unit, inverse = layer_unit(middle)
                grad = normed_grad[l, r, here]
                pulled = upstream + unit_pull(unit, inverse, grad * scaling)
                middle_grad[l, r, here] = pulled
                rounded = (gate_one * pulled).astype(BF16)
                branch_grad[l, r, here] = rounded
                sums[l, 0] += fold_rows(pulled * first)
                sums[l, 1] += fold_rows(grad)
                sums[l, 2] += fold_rows(grad * unit)
                sums[l, 3] += fold_rows(upstream * second)
                bias_sums[0] += fold_rows(rounded.astype(F32))
                bias_sums[1] += fold_rows((gate_two * upstream).astype(BF16).astype(F32))
            return carry

        lax.fori_loop(0, rows, one_row, 0, unroll=2)
    tokens = count * rows * cols
    back = branch_grad[...].reshape(tokens, width)
    weight_grad[...] = lax.dot_general(
        back, attended[...].reshape(tokens, width), (((0,), (0,)), ((), ())), preferred_element_type=F32
    ).astype(BF16)
    raw = lax.dot_general(back, weight[...], (((1,), (1,)), ((), ())), preferred_element_type=F32)
    for c in range(width // 128):
        spread[:, :, c] = raw[:, c * 128 : (c + 1) * 128].reshape(count, rows, cols, 128)
    pack_strips(spread, (out0, out1), place[0])


def turn(place, branch_two, normed_grad, branch_one, attended, latents_rim, cotangent, modulation, fc2_bias, weight):
    count, rows, cols, width = cotangent.shape
    return call_whole(
        turn_body,
        (place, branch_two, normed_grad, branch_one, attended, latents_rim, cotangent, modulation, fc2_bias, weight),
        [
            (cotangent.shape, BF16),
            (cotangent.shape, F32),
            ((width, width), BF16),
            ((count, 4, 8, width), F32),
            ((2, 8, width), F32),
        ]
        + [((2, rows // 2, cols // 2, width), BF16)] * 2,
        [(cotangent.shape, BF16), (chunked(*cotangent.shape), F32)],
    )


def attend_back_body(
    place, up0, up1, part0, part1, projected, log_totals, weight,
    weight_here, weight_away, bias_sums, out0, out1, gathered, upstream, grads, spread, weight_grad,
):
    parts = (part0, part1)
    count, halves, cols, width = part0.shape
    block = halves * cols
    tokens = len(parts) * block
    me = place[0]
    for l in range(count):
        for s, (part, up) in enumerate(zip(parts, (up0, up1))):
            gathered[l, s * block : (s + 1) * block] = part[l].reshape(block, width)
            upstream[l, s * block : (s + 1) * block] = up[l].reshape(block, width)
    bias_sums[...] = jnp.zeros_like(bias_sums)
    lanes = 2 * HEAD
    lane = lax.broadcasted_iota(jnp.int32, (1, lanes), 1)
    turned = (((0,), (0,)), ((), ()))
    inner = (((1,), (1,)), ((), ()))
    for l in range(count):

        def pair(n, carry, l=l):
            here = [pl.ds(pl.multiple_of(k * width + n * lanes, lanes), lanes) for k in range(3)]
            query = projected[l, :, here[0]]
            key = projected[l, :, here[1]]
            value = projected[l, :, here[2]]
            up = upstream[l, :, here[0]]
            query_full = query.astype(F32) * HEAD ** (-0.5)
            up_full = up.astype(F32)
            found = []
            for h in range(2):
                mask = head_mask(lanes, h)
                total = jnp.sum(jnp.where(lane == 2 * n + h, log_totals[l], 0.0), axis=-1, keepdims=True)
                masked = jnp.where(mask, query_full, 0.0).astype(BF16)
                scores = lax.dot_general(masked, key, inner, preferred_element_type=F32)
                weights = jnp.exp(scores - total)
                value_grad = lax.dot_general(weights.astype(BF16), up, turned, preferred_element_type=F32)
                weight_side = lax.dot_general(
                    jnp.where(mask, up_full, 0.0).astype(BF16), value, inner, preferred_element_type=F32
                )
                weighted = jnp.sum(weights * weight_side, axis=-1, keepdims=True)
                score_grad = (weights * (weight_side - weighted)).astype(BF16)
                query_grad = jnp.dot(score_grad, key, preferred_element_type=F32) * HEAD ** (-0.5)
                key_grad = lax.dot_general(score_grad, query, turned, preferred_element_type=F32) * HEAD ** (-0.5)
                found.append((query_grad, key_grad, value_grad))
            mask = head_mask(lanes, 0)
            for k in range(3):
                both = jnp.where(mask, found[0][k], found[1][k]).astype(BF16)
                grads[l, :, here[k]] = both
                if k != 1:
                    bias_sums[k // 2, :, here[0]] += fold_rows(both.astype(F32))
            return carry

        lax.fori_loop(0, width // lanes, pair, 0, unroll=3)
    every = grads[...].reshape(count * tokens, 3 * width)
    weight_grad[...] = lax.dot_general(
        every, gathered[...].reshape(count * tokens, width), turned, preferred_element_type=F32
    ).reshape(weight_grad.shape)
    for j in range(weight_grad.shape[0]):
        weight_here[j] = weight_grad[j, me].astype(BF16)
        weight_away[j] = weight_grad[j, 1 - me].astype(BF16)
    raw = lax.dot_general(every, weight[...], inner, preferred_element_type=F32)
    spread[...] = raw.astype(BF16).reshape(count, len(parts) * halves, cols, width)
    send_rows(spread, (out0, out1), me, halves, me, 0)


def attend_back(place, ups, parts, projected, log_totals, weight):
    count, halves, cols, width = parts[0].shape
    tokens = len(parts) * halves * cols
    batch = lax.axis_size(BATCH)
    half_grad = (batch // 2, 3 * width // batch, width)
    return call_whole(
        attend_back_body,
        (place, *ups, *parts, projected, log_totals, weight),
        [(half_grad, BF16), (half_grad, BF16), ((2, 8, width), F32)] + [((count, halves + 1, cols, width), BF16)] * 2,
        [
            ((count, tokens, width), BF16),
            ((count, tokens, width), BF16),
            ((count, tokens, 3 * width), BF16),
            ((count, len(parts) * halves, cols, width), BF16),
            ((batch // 2, 2, 3 * width // batch, width), F32),
        ],
    )


def finish_body(
    place, part0, part1, latents, modulation, taps, middle_grad, latents_grad, sums, small,
    rimmed, normed, normed_grad,
):
    count, rows, cols, width = middle_grad.shape
    lanes = 128
    unpack_strips((part0, part1), rimmed, place[0], 1)
    for l in range(count):
        offset = modulation[l : l + 1, 0:width]
        scaling = 1.0 + modulation[l : l + 1, width : 2 * width]

        def norm_row(r, carry, l=l, offset=offset, scaling=scaling):
            for h in range(0, cols, 16):
                unit, _ = layer_unit(latents[l, r + 2, h : h + 16].astype(F32))
                normed[l, r, h : h + 16] = (unit * scaling + offset).astype(BF16).astype(F32)
            return carry

        lax.fori_loop(0, rows, norm_row, 0, unroll=2)
    for start in range(0, width, lanes):
        here = slice(start, start + lanes)
        tap = [taps[k : k + 1, here].astype(F32) for k in range(9)]
        found = tuple(jnp.zeros((8, lanes), F32) for _ in range(10))
        for l in range(count):

            def conv_row(r, found, l=l, here=here, tap=tap):
                near = [rimmed[l, r + 2 - a, here.start // lanes] for a in range(3)]
                parts = [sum(tap[3 * a + e] * near[a] for a in range(3)) for e in range(3)]
                normed_grad[l, r, :, here] = row_shift(parts[0], -1) + parts[1] + row_shift(parts[2], 1)
                value = normed[l, r, :, here]
                moved = [row_shift(value, 1), value, row_shift(value, -1)]
                added = [found[3 * a + e] + fold_rows(near[a] * moved[e]) for a in range(3) for e in range(3)]
                return tuple(added) + (found[9] + fold_rows(near[1]),)

            found = lax.fori_loop(0, rows, conv_row, found, unroll=2)
        for k in range(10):
            small[k : k + 1, here] = jnp.sum(found[k], axis=0, keepdims=True)
    sums[...] = jnp.zeros_like(sums)
    for l in range(count):
        scaling = 1.0 + modulation[l : l + 1, width : 2 * width]

        def pull_row(r, carry, l=l, scaling=scaling):
            for h in range(0, cols, 16):
                here = slice(h, h + 16)
                unit, inverse = layer_unit(latents[l, r + 2, here].astype(F32))
                grad = normed_grad[l, r, here]
                sums[l, 0] += fold_rows(grad)
                sums[l, 1] += fold_rows(grad * unit)
                pulled = middle_grad[l, r, here] + unit_pull(unit, inverse, grad * scaling)
                latents_grad[l, r, here] = pulled.astype(BF16)
            return carry

        lax.fori_loop(0, rows, pull_row, 0, unroll=2)


def finish(place, parts, latents_rim, modulation, taps, middle_grad):
    count, rows, cols, width = middle_grad.shape
    return call_whole(
        finish_body,
        (place, *parts, latents_rim, modulation, taps, middle_grad),
        [(middle_grad.shape, BF16), ((count, 2, 8, width), F32), ((16, width), F32)],
        [(chunked(count, rows + 2, cols, width), F32), (middle_grad.shape, F32), (middle_grad.shape, F32)],
    )


def fold_body(pieces, sources, outputs, *refs):
    mine = refs[0]
    heres, aways = refs[1 : 1 + sources], refs[1 + sources : 1 + 2 * sources]
    kept, sent = refs[1 + 2 * sources :][:outputs], refs[1 + 2 * sources + outputs :][:outputs]
    scratch = list(refs[1 + 2 * sources + 2 * outputs :])
    for source, row, rows, lane, lead, bit, out, out_row, out_lane in pieces:
        here, away = heres[source], aways[source]
        size = rows // (2 * lead)
        lanes, out_lanes = slice(lane, lane + FOLD), slice(out_lane, out_lane + FOLD)
        me = mine[bit]
        if size % 16:
            whole = scratch.pop(0)
            total = here[row : row + rows, lanes].astype(F32) + away[row : row + rows, lanes].astype(F32)
            whole[...] = total.reshape(lead, 2, size, FOLD)
            for side, place in ((kept, me), (sent, 1 - me)):
                picked = whole[:, place].reshape(lead * size, FOLD).astype(BF16)
                side[out][out_row : out_row + lead * size, out_lanes] = picked
            continue
        part = max(p for p in range(16, 97, 16) if size % p == 0)

        def one(n, carry, here=here, away=away, row=row, size=size, part=part, lanes=lanes, out=out,
                out_row=out_row, out_lanes=out_lanes, me=me):
            a, k = n // (size // part), n % (size // part)
            target = pl.ds(pl.multiple_of(out_row + a * size + k * part, 16), part)
            for side, place in ((kept, me), (sent, 1 - me)):
                origin = pl.ds(pl.multiple_of(row + (2 * a + place) * size + k * part, 16), part)
                total = here[origin, lanes].astype(F32) + away[origin, lanes].astype(F32)
                side[out][target, out_lanes] = total.astype(BF16)
            return carry

        lax.fori_loop(0, lead * size // part, one, 0)


FOLD = 768


def fold(pairs, bits, pieces, outs):
    mine = jnp.stack([(lax.axis_index(axis) >> bit) & 1 for axis, bit in bits]).astype(jnp.int32)
    scratch = [(p[4], 2, p[2] // (2 * p[4]), FOLD) for p in pieces if p[2] // (2 * p[4]) % 16]
    found = call_whole(
        partial(fold_body, pieces, len(pairs), len(outs)),
        (mine, *[pair[0] for pair in pairs], *[pair[1] for pair in pairs]),
        [(shape, BF16) for shape in outs] * 2,
        [(shape, F32) for shape in scratch],
    )
    return list(zip(found[: len(outs)], found[len(outs) :]))


def swap(pair, axis, bit):
    return pair[0], swap_bit(pair[1], axis, bit)


def quick_sums():
    return lax.axis_size(BATCH) == 8 and lax.axis_size(GRP) == 4


def exchange(parts):
    return parts[0], swap_bit(parts[1], BATCH, 0)


def on_device(
    latents,
    cotangent,
    timesteps,
    labels,
    time_weight,
    time_bias,
    label_table,
    ada_weight,
    ada_bias,
    conv_a,
    conv_a_bias,
    qkv_weight,
    qv_bias,
    proj_weight,
    proj_bias,
    fc1_weight,
    fc1_bias,
    conv_f,
    conv_f_bias,
    fc2_weight,
    fc2_bias,
):
    width = latents.shape[3]
    hidden_width = fc1_weight.shape[1]
    devices = lax.axis_size(BATCH) * lax.axis_size(GRP)
    slot = lax.axis_index(BATCH) * lax.axis_size(GRP) + lax.axis_index(GRP)

    strip = lax.axis_index(GRP)
    half = lax.axis_index(BATCH) & 1
    inside = jnp.stack([half == 1, half == 0])
    place = jnp.concatenate([half[None], inside.astype(jnp.int32)])
    numbers = jnp.stack([timesteps.astype(F32), labels.astype(F32)])
    other = swap_bit(numbers, BATCH, 0)
    numbers = jnp.where(half == strip >> 1, numbers, other)
    numbers = jnp.where((strip & 1) == 0, numbers[:, 0], numbers[:, 1])
    latents_rim = with_edges(to_pairs(latents), 2)
    cotangent = to_pairs(cotangent)
    cotangent_rim = with_edges(cotangent, 1)

    frequency_rows = sinusoid(numbers[:1], time_weight.shape[0])
    condition = exact_dot(frequency_rows, time_weight) + time_bias.astype(F32)
    picked = lax.dynamic_slice_in_dim(label_table, numbers[1].astype(jnp.int32), 1, axis=0)
    condition = condition + picked.astype(F32)
    active = condition * jax.nn.sigmoid(condition)
    modulation = exact_dot(active, ada_weight) + ada_bias.astype(F32)
    gate_two = modulation[:, None, None, 5 * width :]

    mixed = exchange(stem(place, latents_rim, modulation, conv_a, conv_a_bias))
    qkv_bias = jnp.concatenate([qv_bias[0:1], jnp.zeros_like(qv_bias[0:1]), qv_bias[1:2]], axis=1)
    *sent, projected, log_totals = attend(place, mixed, qkv_weight, qkv_bias)
    normed_rim, attended, branch_one = middle_part(
        place, exchange(sent), latents_rim, modulation, proj_weight, proj_bias
    )

    branch_two_rim = (gate_two * cotangent_rim.astype(F32)).astype(BF16)
    branch_two, normed_two_grad, fc1_here, fc1_away, fc2_here, fc2_away, ff_small = feed_forward(
        place, normed_rim, branch_two_rim, fc1_weight, fc1_bias, conv_f, conv_f_bias, fc2_weight
    )
    pairs = lax.axis_size(BATCH) // 2
    quick = quick_sums()
    fc1_pair = (fc1_here.reshape(-1, width), fc1_away.reshape(-1, width))
    fc2_pair = (fc2_here.reshape(-1, hidden_width), fc2_away.reshape(-1, hidden_width))
    fc1_pair = swap(fc1_pair, BATCH, 0)
    fc2_pair = swap(fc2_pair, BATCH, 0)
    lanes = range(0, hidden_width, width)
    near, far, by_x, by_y = (GRP, 0), (GRP, 1), (BATCH, 1), (BATCH, 2)
    if quick:
        fc1_rows, fc2_rows = fc1_pair[0].shape[0], fc2_pair[0].shape[0]
        fc1_pair, fc2_pair = fold(
            [fc1_pair, fc2_pair],
            [by_x, near],
            [(0, 0, fc1_rows, 0, 2, 0, 0, 0, 0)] + [(1, 0, fc2_rows, c, 8, 1, 1, 0, c) for c in lanes],
            [(fc1_rows // 2, width), (fc2_rows // 2, hidden_width)],
        )
        fc1_pair = swap(fc1_pair, *by_x)
        fc2_pair = swap(fc2_pair, *near)
    else:
        fc1_sum, fc2_sum = (
            scatter_rest((pair[0].astype(F32) + pair[1].astype(F32)).reshape(pairs, -1, pair[0].shape[1]), flip)
            for pair, flip in ((fc1_pair, False), (fc2_pair, True))
        )

    output, middle_grad, proj_grad, turn_sums, turn_bias, *sent = turn(
        place,
        branch_two.reshape(cotangent.shape),
        normed_two_grad.reshape(cotangent.shape),
        branch_one,
        attended,
        latents_rim,
        cotangent,
        modulation,
        fc2_bias,
        proj_weight,
    )
    output = from_pairs(output)
    turn_sums = jnp.sum(turn_sums, axis=2)
    turn_bias = jnp.sum(turn_bias, axis=1)

    def slots(vectors):
        return vectors.reshape(len(vectors), devices, -1).transpose(1, 0, 2).reshape(devices, -1)

    small = jnp.concatenate([slots(ff_small[:11]), slots(turn_bias)], axis=1).astype(BF16)
    small_length = small.shape[1]
    small_lanes = -(-small_length // 8)
    small = jnp.pad(small, ((0, 0), (0, small_lanes * 8 - small_length))).reshape(devices, 8, small_lanes)
    small = jnp.pad(small, ((0, 0), (0, 0), (0, width - small_lanes)))
    beside = jnp.concatenate([proj_grad.reshape(devices, -1, width), small], axis=1).reshape(pairs, 2, -1, width)
    beside_pair = tuple(
        lax.dynamic_index_in_dim(beside, side, 1, keepdims=False).reshape(-1, width) for side in (half, 1 - half)
    )
    beside_pair = swap(beside_pair, BATCH, 0)

    qkv_here, qkv_away, qv_sums, *sent = attend_back(
        place, exchange(sent), mixed, projected, log_totals, qkv_weight
    )
    qkv_pair = swap((qkv_here.reshape(-1, width), qkv_away.reshape(-1, width)), BATCH, 0)
    if quick:
        beside_rows, qkv_rows = beside_pair[0].shape[0], qkv_pair[0].shape[0]
        fc1_pair, fc2_pair, beside_pair = fold(
            [fc1_pair, fc2_pair, beside_pair],
            [by_y, far, by_x],
            [(0, 0, fc1_rows // 2, 0, 1, 0, 0, 0, 0)]
            + [(1, 0, fc2_rows // 2, c, 4, 1, 1, 0, c) for c in lanes]
            + [(2, 0, beside_rows, 0, 2, 2, 2, 0, 0)],
            [(fc1_rows // 4, width), (fc2_rows // 4, hidden_width), (beside_rows // 2, width)],
        )
        fc1_pair = swap(fc1_pair, *by_y)
        fc2_pair = swap(fc2_pair, *far)
        beside_pair = swap(beside_pair, *by_x)
        (qkv_pair,) = fold([qkv_pair], [by_x], [(0, 0, qkv_rows, 0, 2, 0, 0, 0, 0)], [(qkv_rows // 2, width)])
        qkv_pair = swap(qkv_pair, *by_x)
    else:
        beside, qkv_sum = (
            scatter_rest((pair[0].astype(F32) + pair[1].astype(F32)).reshape(pairs, -1, width), flip)
            for pair, flip in ((beside_pair, False), (qkv_pair, True))
        )
    latents_grad, finish_sums, conv_a_small = finish(
        place, exchange(sent), latents_rim, modulation, conv_a, middle_grad
    )
    latents_grad = from_pairs(latents_grad)
    if quick:
        fc1_rows, fc2_rows, beside_rows, qkv_rows = fc1_rows // 4, fc2_rows // 4, beside_rows // 2, qkv_rows // 2
        fc1_pair, fc2_pair = fold(
            [fc1_pair, fc2_pair],
            [near, by_x],
            [(0, 0, fc1_rows, 0, 2, 0, 0, 0, 0)]
            + [(1, 0, fc2_rows, c, 2, 1, 1, k * (fc2_rows // 2), 0) for k, c in enumerate(lanes)],
            [(fc1_rows // 2, width), (len(lanes) * fc2_rows // 2, width)],
        )
        fc1_pair = swap(fc1_pair, *near)
        fc2_pair = swap(fc2_pair, *by_x)
        (attention_pair,) = fold(
            [beside_pair, qkv_pair],
            [by_y],
            [(0, 0, beside_rows, 0, 1, 0, 0, 0, 0), (1, 0, qkv_rows, 0, 1, 0, 0, beside_rows // 2, 0)],
            [((beside_rows + qkv_rows) // 2, width)],
        )
        attention_pair = swap(attention_pair, *by_y)
        fc1_rows, fc2_rows = fc1_rows // 2, len(lanes) * fc2_rows // 2
        beside_rows, qkv_rows = beside_rows // 2, qkv_rows // 2
        fc1_pair, fc2_pair, attention_pair = fold(
            [fc1_pair, fc2_pair, attention_pair],
            [far, by_y, near],
            [
                (0, 0, fc1_rows, 0, 1, 0, 0, 0, 0),
                (1, 0, fc2_rows, 0, len(lanes), 1, 1, 0, 0),
                (2, 0, beside_rows, 0, 2, 2, 2, 0, 0),
                (2, beside_rows, qkv_rows, 0, 2, 2, 2, beside_rows // 2, 0),
            ],
            [(fc1_rows // 2, width), (fc2_rows // 2, width), ((beside_rows + qkv_rows) // 2, width)],
        )
        fc1_pair = swap(fc1_pair, *far)
        fc2_pair = swap(fc2_pair, *by_y)
        attention_pair = swap(attention_pair, *near)
        beside_rows, qkv_rows = beside_rows // 2, qkv_rows // 2
        (attention_pair,) = fold(
            [attention_pair],
            [far],
            [(0, 0, beside_rows, 0, 1, 0, 0, 0, 0), (0, beside_rows, qkv_rows, 0, 1, 0, 0, beside_rows // 2, 0)],
            [((beside_rows + qkv_rows) // 2, width)],
        )
        attention_pair = swap(attention_pair, *far)
        fc1_sum, fc2_sum, attention_sum = (
            pair[0].astype(F32) + pair[1].astype(F32) for pair in (fc1_pair, fc2_pair, attention_pair)
        )
        fc2_sum = fc2_sum.reshape(len(lanes), -1, width).transpose(1, 0, 2).reshape(-1, hidden_width)
        beside, qkv_sum = attention_sum[: beside_rows // 2], attention_sum[beside_rows // 2 :]
    proj_sum = beside[:-8]
    small_sum = beside[-8:, :small_lanes].reshape(-1)
    wide_length = 11 * (hidden_width // devices)
    wide_sum = small_sum[:wide_length].reshape(11, -1)
    narrow_sum = small_sum[wide_length:small_length].reshape(2, -1)
    finish_sums = jnp.sum(finish_sums, axis=2)

    late = jnp.concatenate([conv_a_small[:10], jnp.sum(qv_sums, axis=1), jnp.zeros((4, width), F32)], axis=0)
    modulation_grad = jnp.concatenate([finish_sums[0], turn_sums[0], jnp.zeros((2, width), F32)], axis=0)
    side = jnp.concatenate(
        [condition, jnp.pad(frequency_rows, ((0, 0), (0, width - frequency_rows.shape[1] - 1))), numbers[1:][None]],
        axis=1,
    )
    every, late_sum = gather_sum(jnp.pad(side.reshape(2, width), ((6, 0), (0, 0))), modulation_grad, late)
    every = every.reshape(-1, 8, width)
    every_grad = every[:, :6].reshape(-1, 6 * width)
    every_condition = every[:, 6]
    every_frequency = every[:, 7, : frequency_rows.shape[1]]
    every_label = every[:, 7, -1].astype(jnp.int32)
    late_sum = lax.dynamic_slice_in_dim(late_sum, slot * (width // devices), width // devices, axis=1)
    sigmoid = jax.nn.sigmoid(every_condition)
    every_active = every_condition * sigmoid
    narrow_width = width // devices
    ada_width = 6 * width // devices
    ada_part = lax.dynamic_slice_in_dim(every_grad, slot * ada_width, ada_width, axis=1)
    ada_grad = lax.dot_general(
        every_active, ada_part, (((0,), (0,)), ((), ())), precision=HIGHEST, preferred_element_type=F32
    )
    ada_bias_grad = jnp.sum(ada_part, axis=0)[None, :]
    ada_rows = lax.dynamic_slice_in_dim(ada_weight, slot * narrow_width, narrow_width, axis=0)
    active_grad = lax.dot_general(
        every_grad, ada_rows.astype(F32), (((1,), (1,)), ((), ())), precision=HIGHEST
    )
    slope_silu = lax.dynamic_slice_in_dim(
        sigmoid * (1.0 + every_condition * (1.0 - sigmoid)), slot * narrow_width, narrow_width, axis=1
    )
    condition_grad = active_grad * slope_silu
    onehot = (every_label[:, None] == jnp.arange(label_table.shape[0], dtype=jnp.int32)[None, :]).astype(F32)
    table_grad = lax.dot_general(onehot, condition_grad, (((0,), (0,)), ((), ())), precision=HIGHEST)
    time_grad = lax.dot_general(
        every_frequency, condition_grad, (((0,), (0,)), ((), ())), precision=HIGHEST
    )
    time_bias_grad = jnp.sum(condition_grad, axis=0)[None, :]

    return (
        output,
        latents_grad,
        time_grad,
        time_bias_grad,
        table_grad,
        ada_grad,
        ada_bias_grad,
        late_sum[0:9],
        late_sum[9:10],
        qkv_sum.T,
        late_sum[10:12],
        proj_sum.T,
        narrow_sum[0:1],
        fc1_sum.T,
        wide_sum[10:11],
        wide_sum[0:9],
        wide_sum[9:10],
        fc2_sum.T,
        narrow_sum[1:2],
    )


def solution(mesh):
    columns = P(None, (BATCH, GRP))
    return jax.shard_map(
        on_device,
        mesh=mesh,
        in_specs=(P(BATCH, GRP, None, None), P(BATCH, GRP, None, None), P(BATCH), P(BATCH)) + (P(),) * 17,
        out_specs=(P(BATCH, GRP, None, None), P(BATCH, GRP, None, None)) + (columns,) * 17,
        check_vma=False,
    )
```

```python
from functools import partial
import math

import jax
import jax.numpy as jnp
from jax import lax
from jax.experimental import pallas as pl
from jax.experimental.pallas import tpu as pltpu
from jax.sharding import PartitionSpec as P


HEAD = 64
BATCH, GRP = "batch", "grp"
HIGHEST = lax.Precision.HIGHEST
F32 = jnp.float32
BF16 = jnp.bfloat16
GELU_C = math.sqrt(2.0 / math.pi)


def swap_bit(value, axis, bit):
    count = lax.axis_size(axis)
    return lax.ppermute(value, axis, [(i, i ^ (1 << bit)) for i in range(count)])


def to_pairs(block):
    strip = lax.axis_index(GRP)
    odd = strip & 1
    arrived = []
    for k in range(2):
        piece = lax.dynamic_slice_in_dim(block, k ^ odd, 1, axis=0)
        arrived.append(lax.ppermute(piece, (BATCH, GRP), pair_moves(k)))
    swapped = odd == 1
    upper = jnp.where(swapped, arrived[1], arrived[0])
    lower = jnp.where(swapped, arrived[0], arrived[1])
    return jnp.concatenate([upper, lower], axis=1)


def pair_moves(k, back=False):
    strips = lax.axis_size(GRP)
    moves = []
    for b in range(lax.axis_size(BATCH)):
        for z in range(strips):
            to = (2 * (b // 2) + (z >> 1)) * strips + 2 * (b & 1) + (k ^ (z & 1))
            moves.append((to, b * strips + z) if back else (b * strips + z, to))
    return moves


def from_pairs(block):
    rows = block.shape[1] // 2
    odd = lax.axis_index(GRP) & 1
    arrived = []
    for k in range(2):
        piece = lax.dynamic_slice_in_dim(block, (k ^ odd) * rows, rows, axis=1)
        arrived.append(lax.ppermute(piece, (BATCH, GRP), pair_moves(k, True)))
    swapped = odd == 1
    first = jnp.where(swapped, arrived[1], arrived[0])
    second = jnp.where(swapped, arrived[0], arrived[1])
    return jnp.concatenate([first, second], axis=0)


def with_edges(block, width):
    rows = block.shape[1]
    lower = (lax.axis_index(BATCH) & 1) == 1
    edge = jnp.where(lower, block[:, :width], block[:, rows - width :])
    other = swap_bit(edge, BATCH, 0)
    zero = jnp.zeros_like(other)
    return jnp.concatenate([jnp.where(lower, other, zero), block, jnp.where(lower, zero, other)], axis=1)


def halve(here, away, axis, bit):
    arrived = swap_bit(away, axis, bit)
    return here.astype(F32) + arrived.astype(F32)


def halve_dim(block, place, axis, bit):
    mine = (lax.axis_index(axis) >> bit) & 1
    away = lax.dynamic_index_in_dim(block, 1 - mine, place, keepdims=False)
    here = lax.dynamic_index_in_dim(block, mine, place, keepdims=False)
    return halve(here, away, axis, bit)


def scatter_rest(block, swapped):
    high = list(range(1, lax.axis_size(BATCH).bit_length() - 1))
    left = high[::-1]
    _, rows, width = block.shape
    block = block.reshape((2,) * len(high) + (rows, width))
    for bit in high[::-1] if swapped else high:
        block = halve_dim(block.astype(BF16), left.index(bit), BATCH, bit)
        left.remove(bit)
    bits = lax.axis_size(GRP).bit_length() - 1
    block = block.reshape((2,) * bits + (-1, width))
    for bit in range(bits):
        block = halve_dim(block.astype(BF16), bits - 1 - bit, GRP, bit)
    return block


def gather_sum(rows, pair_rows, summed):
    length = pair_rows.shape[0]
    bits = [(GRP, bit) for bit in range(lax.axis_size(GRP).bit_length() - 1)]
    bits += [(BATCH, bit) for bit in range(1, lax.axis_size(BATCH).bit_length() - 1)]
    length = pair_rows.shape[0]
    both = jnp.concatenate([pair_rows, summed], axis=0)
    other = swap_bit(both, BATCH, 0)
    both = both + other
    rows = both[:length] + rows
    summed = both[length:]
    for axis, bit in bits:
        sent = jnp.concatenate([summed, rows], axis=0)
        other = swap_bit(sent, axis, bit)
        summed = summed + other[: len(summed)]
        rows = jnp.concatenate([rows, other[len(summed) :]], axis=0)
    return rows, summed


def exact_dot(left, right):
    high = lax.reduce_precision(left, 8, 7)
    rest = left - high
    middle = lax.reduce_precision(rest, 8, 7)
    low = rest - middle
    rows = jnp.concatenate([high, middle, low], axis=0).astype(BF16)
    out = jnp.dot(rows, right, preferred_element_type=F32)
    count = left.shape[0]
    return out[:count] + (out[count : 2 * count] + out[2 * count :])


def sinusoid(timestep, length):
    halfway = length // 2
    frequency = jnp.exp(-math.log(10000.0) * jnp.arange(halfway, dtype=F32) / halfway)
    angles = timestep.astype(F32)[:, None] * frequency[None, :]
    return jnp.concatenate([jnp.cos(angles), jnp.sin(angles)], axis=1)


def unit_pull(unit, inverse, grad):
    first = jnp.mean(grad, axis=-1, keepdims=True)
    second = jnp.mean(grad * unit, axis=-1, keepdims=True)
    return inverse * (grad - first - unit * second)


def row_shift(values, step):
    cols = values.shape[0]
    place = lax.broadcasted_iota(jnp.int32, values.shape, 0)
    rolled = pltpu.roll(values, step % cols, 0)
    return jnp.where(place == (0 if step == 1 else cols - 1), 0.0, rolled)


def fold_rows(values):
    total = values[0:8]
    for start in range(8, values.shape[0], 8):
        total = total + values[start : start + 8]
    return total


def feed_forward_body(
    place, normed, upstream, fc1, fc1_bias, taps, conv_bias, fc2,
    branch_out, normed_grad_out, fc1_here, fc1_away, fc2_here, fc2_away, small_out,
    hidden, lifted, activated, convolved_grad, hidden_grad, fc1_grad, fc2_grad,
):
    count, rim_rows, cols, width = normed.shape
    rows = rim_rows - 4
    tile = fc1.shape[1]
    lanes = 128
    raw = jnp.dot(
        normed[...].reshape(count * rim_rows * cols, width), fc1[...], preferred_element_type=F32
    ) + fc1_bias[...].astype(F32)
    hidden[...] = raw.astype(BF16).astype(F32).reshape(count, rim_rows, cols, tile)
    hidden[:, 0:2] = hidden[:, 0:2] * place[1].astype(F32)
    hidden[:, rows + 2 :] = hidden[:, rows + 2 :] * place[2].astype(F32)
    lifted[...] = lax.dot_general(
        upstream[...].reshape(count * (rows + 2) * cols, width),
        fc2[...],
        (((1,), (1,)), ((), ())),
        preferred_element_type=F32,
    ).reshape(count, rows + 2, cols, tile)
    for start in range(0, tile, lanes):
        here = slice(start, start + lanes)
        tap = [taps[k : k + 1, here].astype(F32) for k in range(9)]
        bias = conv_bias[:, here].astype(F32)

        def forward_row(l, r, sums):
            near = [hidden[l, r + a, :, here] for a in range(3)]
            parts = [sum(tap[3 * a + e] * near[a] for a in range(3)) for e in range(3)]
            value = row_shift(parts[0], 1) + parts[1] + row_shift(parts[2], -1) + bias
            square = value * value
            bent = jnp.tanh(value * (GELU_C + GELU_C * 0.044715 * square))
            half = 0.5 * (1.0 + bent)
            activated[l, r, :, here] = (value * half).astype(BF16)
            slope = half + value * half * (1.0 - bent) * (GELU_C + 3.0 * 0.044715 * GELU_C * square)
            grad = (lifted[l, r, :, here] * slope).astype(BF16).astype(F32)
            convolved_grad[l, r, :, here] = grad
            if sums is None:
                return None
            moved = [row_shift(grad, -1), grad, row_shift(grad, 1)]
            added = [sums[3 * a + e] + fold_rows(near[a] * moved[e]) for a in range(3) for e in range(3)]
            return tuple(added) + (sums[9] + fold_rows(grad),)

        sums = tuple(jnp.zeros((8, lanes), F32) for _ in range(10))
        bias_sum = jnp.zeros((8, lanes), F32)
        for l in range(count):
            forward_row(l, 0, None)
            forward_row(l, rows + 1, None)
            sums = lax.fori_loop(1, rows + 1, lambda r, sums, l=l: forward_row(l, r, sums), sums, unroll=2)

            def backward_row(r, bias_sum, l=l):
                near = [convolved_grad[l, r + 2 - a, :, here] for a in range(3)]
                parts = [sum(tap[3 * a + e] * near[a] for a in range(3)) for e in range(3)]
                value = row_shift(parts[0], -1) + parts[1] + row_shift(parts[2], 1)
                rounded = value.astype(BF16)
                hidden_grad[l, r, :, here] = rounded
                return bias_sum + fold_rows(rounded.astype(F32))

            bias_sum = lax.fori_loop(0, rows, backward_row, bias_sum, unroll=4)
        for k in range(10):
            small_out[k : k + 1, here] = jnp.sum(sums[k], axis=0, keepdims=True)
        small_out[10:11, here] = jnp.sum(bias_sum, axis=0, keepdims=True)
    tokens = count * rows * cols
    active = activated[:, 1 : rows + 1].reshape(tokens, tile)
    back = hidden_grad[...].reshape(tokens, tile)
    inner = normed[:, 2 : rows + 2].reshape(tokens, width)
    above = upstream[:, 1 : rows + 1].reshape(tokens, width)

    @pl.when(pl.program_id(0) == 0)
    def _():
        branch_out[...] = jnp.zeros_like(branch_out)
        normed_grad_out[...] = jnp.zeros_like(normed_grad_out)

    branch_out[...] += jnp.dot(active, fc2[...], preferred_element_type=F32)
    normed_grad_out[...] += lax.dot_general(
        back, fc1[...], (((1,), (1,)), ((), ())), preferred_element_type=F32
    )
    me = place[0]
    fc1_grad[...] = lax.dot_general(
        back, inner, (((0,), (0,)), ((), ())), preferred_element_type=F32
    ).astype(BF16).reshape(fc1_grad.shape)
    for j in range(fc1_grad.shape[0]):
        fc1_here[0, j] = fc1_grad[j, me]
        fc1_away[0, j] = fc1_grad[j, 1 - me]
    fc2_grad[...] = lax.dot_general(
        above, active, (((0,), (0,)), ((), ())), preferred_element_type=F32
    ).reshape(fc2_grad.shape)
    for j in range(fc2_grad.shape[0]):
        fc2_here[j] = fc2_grad[j, me].astype(BF16)
        fc2_away[j] = fc2_grad[j, 1 - me].astype(BF16)


def feed_forward(place, normed, upstream, fc1, fc1_bias, taps, conv_bias, fc2):
    count, rim_rows, cols, width = normed.shape
    rows = rim_rows - 4
    tokens = count * rows * cols
    units = fc1.shape[1]
    tile = 768
    steps = units // tile
    batch = lax.axis_size(BATCH)
    fc1_block = (1, batch // 2 // steps, units // batch, width)
    fc2_block = (batch // 2, width // batch, tile)
    return pl.pallas_call(
        feed_forward_body,
        grid=(steps,),
        in_specs=[
            pl.BlockSpec(memory_space=pltpu.SMEM),
            pl.BlockSpec(normed.shape, lambda i: (0, 0, 0, 0)),
            pl.BlockSpec(upstream.shape, lambda i: (0, 0, 0, 0)),
            pl.BlockSpec((width, tile), lambda i: (0, i)),
            pl.BlockSpec((1, tile), lambda i: (0, i)),
            pl.BlockSpec((9, tile), lambda i: (0, i)),
            pl.BlockSpec((1, tile), lambda i: (0, i)),
            pl.BlockSpec((tile, width), lambda i: (i, 0)),
        ],
        out_specs=[
            pl.BlockSpec((tokens, width), lambda i: (0, 0)),
            pl.BlockSpec((tokens, width), lambda i: (0, 0)),
            pl.BlockSpec(fc1_block, lambda i: (i, 0, 0, 0)),
            pl.BlockSpec(fc1_block, lambda i: (i, 0, 0, 0)),
            pl.BlockSpec(fc2_block, lambda i: (0, 0, i)),
            pl.BlockSpec(fc2_block, lambda i: (0, 0, i)),
            pl.BlockSpec((16, tile), lambda i: (0, i)),
        ],
        out_shape=[
            jax.ShapeDtypeStruct((tokens, width), F32),
            jax.ShapeDtypeStruct((tokens, width), F32),
            jax.ShapeDtypeStruct((steps,) + fc1_block[1:], BF16),
            jax.ShapeDtypeStruct((steps,) + fc1_block[1:], BF16),
            jax.ShapeDtypeStruct(fc2_block[:2] + (units,), BF16),
            jax.ShapeDtypeStruct(fc2_block[:2] + (units,), BF16),
            jax.ShapeDtypeStruct((16, units), F32),
        ],
        scratch_shapes=[
            pltpu.VMEM((count, rim_rows, cols, tile), F32),
            pltpu.VMEM((count, rows + 2, cols, tile), F32),
            pltpu.VMEM((count, rows + 2, cols, tile), BF16),
            pltpu.VMEM((count, rows + 2, cols, tile), F32),
            pltpu.VMEM((count, rows, cols, tile), BF16),
            pltpu.VMEM((fc1_block[1], 2) + fc1_block[2:], BF16),
            pltpu.VMEM((batch // 2, 2, width // batch, tile), F32),
        ],
        compiler_params=pltpu.CompilerParams(
            dimension_semantics=("arbitrary",), vmem_limit_bytes=48 * 1024 * 1024
        ),
        name="feed_forward",
    )(place, normed, upstream, fc1, fc1_bias, taps, conv_bias, fc2)


def layer_unit(values):
    centre = jnp.mean(values, axis=-1, keepdims=True)
    centred = values - centre
    inverse = lax.rsqrt(jnp.mean(centred * centred, axis=-1, keepdims=True) + 1e-06)
    return centred * inverse, inverse


def chunked(count, rows, cols, width):
    return (count, rows, width // 128, cols, 128)


def half_rows(start):
    return pl.ds(start, 16, stride=2)


def pack_strips(values, outs, me):
    _, rows, chunks, _, lanes = values.shape

    def one(i, carry):
        for s, out in enumerate(outs):
            row = 2 * i + (me ^ s)
            for q in range(2):
                for c in range(chunks):
                    out[q, i, :, c * lanes : (c + 1) * lanes] = values[0, row, c, half_rows(q), :].astype(BF16)
        return carry

    lax.fori_loop(0, rows // 2, one, 0)


def unpack_strips(parts, values, me, first):
    halves = parts[0].shape[1]
    chunks, _, lanes = values.shape[2:]

    def one(i, carry):
        for s, part in enumerate(parts):
            row = 2 * i + (me ^ s ^ first)
            for q in range(2):
                full = part[q, i].astype(F32)
                for c in range(chunks):
                    values[0, row, c, half_rows(q), :] = full[:, c * lanes : (c + 1) * lanes]
        return carry

    lax.fori_loop(0, halves, one, 0)


def stem_body(place, latents, modulation, taps, conv_bias, out0, out1, normed, mixed):
    count, rim_rows, cols, width = normed.shape
    rows = rim_rows - 2
    lanes = 128
    for l in range(count):
        offset = modulation[l : l + 1, 0:width]
        scaling = 1.0 + modulation[l : l + 1, width : 2 * width]

        def norm_row(r, carry, l=l, offset=offset, scaling=scaling):
            for h in range(0, cols, 16):
                unit, _ = layer_unit(latents[l, r + 1, h : h + 16].astype(F32))
                normed[l, r, h : h + 16] = (unit * scaling + offset).astype(BF16).astype(F32)
            return carry

        lax.fori_loop(0, rim_rows, norm_row, 0, unroll=2)
        normed[l, 0] = normed[l, 0] * place[1].astype(F32)
        normed[l, rows + 1] = normed[l, rows + 1] * place[2].astype(F32)
    for start in range(0, width, lanes):
        here = slice(start, start + lanes)
        tap = [taps[k : k + 1, here].astype(F32) for k in range(9)]
        bias = conv_bias[:, here].astype(F32)
        for l in range(count):

            def conv_row(r, carry, l=l, here=here, tap=tap, bias=bias):
                near = [normed[l, r + a, :, here] for a in range(3)]
                parts = [sum(tap[3 * a + e] * near[a] for a in range(3)) for e in range(3)]
                total = row_shift(parts[0], 1) + parts[1] + row_shift(parts[2], -1) + bias
                mixed[l, r, here.start // lanes] = total
                return carry

            lax.fori_loop(0, rows, conv_row, 0, unroll=4)
    pack_strips(mixed, (out0, out1), place[0])


WHOLE = pl.BlockSpec(memory_space=pltpu.VMEM)
SCALARS = pl.BlockSpec(memory_space=pltpu.SMEM)


def call_whole(body, inputs, outputs, scratch):
    return pl.pallas_call(
        body,
        in_specs=[SCALARS] + [WHOLE] * (len(inputs) - 1),
        out_specs=[WHOLE] * len(outputs),
        out_shape=[jax.ShapeDtypeStruct(shape, kind) for shape, kind in outputs],
        scratch_shapes=[pltpu.VMEM(shape, kind) for shape, kind in scratch],
        compiler_params=pltpu.CompilerParams(vmem_limit_bytes=56 * 1024 * 1024),
    )(*inputs)


def stem(place, latents_rim, modulation, taps, conv_bias):
    count, rim_rows, cols, width = latents_rim.shape
    rows = rim_rows - 4
    return call_whole(
        stem_body,
        (place, latents_rim, modulation, taps, conv_bias),
        [((2, rows // 2, cols // 2, width), BF16)] * 2,
        [((count, rows + 2, cols, width), F32), (chunked(count, rows, cols, width), F32)],
    )


def head_mask(lanes, h):
    lane = lax.broadcasted_iota(jnp.int32, (1, lanes), 1)
    return (lane >= h * HEAD) & (lane < (h + 1) * HEAD)


def attend_body(place, part0, part1, weight, bias, out0, out1, projected, log_totals, gathered, attended):
    parts = (part0, part1)
    count, halves, cols, width = part0.shape
    block = halves * cols
    tokens = len(parts) * block
    me = place[0]
    for l in range(count):
        for s, part in enumerate(parts):
            gathered[l, s * block : (s + 1) * block] = part[l].reshape(block, width)
    raw = jnp.dot(gathered[...].reshape(count * tokens, width), weight[...], preferred_element_type=F32)
    projected[...] = (raw + bias[...].astype(F32)).astype(BF16).reshape(count, tokens, 3 * width)
    log_totals[...] = jnp.zeros_like(log_totals)
    lanes = 2 * HEAD
    lane = lax.broadcasted_iota(jnp.int32, (1, lanes), 1)
    for l in range(count):

        def pair(n, carry, l=l):
            start = pl.multiple_of(n * lanes, lanes)
            query = projected[l, :, pl.ds(start, lanes)].astype(F32) * HEAD ** (-0.5)
            key = projected[l, :, pl.ds(pl.multiple_of(width + n * lanes, lanes), lanes)]
            value = projected[l, :, pl.ds(pl.multiple_of(2 * width + n * lanes, lanes), lanes)]
            total_rows = log_totals[l]
            mixed = []
            for h in range(2):
                masked = jnp.where(head_mask(lanes, h), query, 0.0).astype(BF16)
                scores = lax.dot_general(masked, key, (((1,), (1,)), ((), ())), preferred_element_type=F32)
                highest = jnp.max(scores, axis=-1, keepdims=True)
                raised = jnp.exp(scores - highest)
                totals = jnp.sum(raised, axis=-1, keepdims=True)
                weights = (raised * (1.0 / totals)).astype(BF16)
                mixed.append(jnp.dot(weights, value, preferred_element_type=F32))
                total_rows = jnp.where(lane == 2 * n + h, highest + jnp.log(totals), total_rows)
            log_totals[l] = total_rows
            both = jnp.where(head_mask(lanes, 0), mixed[0], mixed[1]).astype(BF16)
            attended[l, :, :, pl.ds(start, lanes)] = both.reshape(len(parts) * halves, cols, lanes)
            return carry

        lax.fori_loop(0, width // lanes, pair, 0, unroll=3)
    send_rows(attended, (out0, out1), me, halves, 1, 0)


def send_rows(values, outs, me, halves, before, shift):
    count, total = values.shape[:2]
    for s, out in enumerate(outs):
        strip = me ^ s
        for k in range(out.shape[1]):
            row = strip * halves - before + shift + k
            inside = ((row >= 0) & (row < total)).astype(F32)
            kept = jnp.clip(row, 0, total - 1)
            source = (me ^ (kept // halves)) * halves + kept % halves
            for l in range(count):
                out[l, k] = (values[l, source].astype(F32) * inside).astype(BF16)


def attend(place, parts, weight, bias):
    count, halves, cols, width = parts[0].shape
    tokens = len(parts) * halves * cols
    return call_whole(
        attend_body,
        (place, *parts, weight, bias),
        [((count, halves + 2, cols, width), BF16)] * 2
        + [((count, tokens, 3 * width), BF16), ((count, tokens, 2 * HEAD), F32)],
        [((count, tokens, width), BF16), ((count, len(parts) * halves, cols, width), BF16)],
    )


def middle_body(place, part0, part1, latents, modulation, weight, bias, normed, attended, branch, spread, rimmed, raw):
    count, rim_rows, cols, width = latents.shape
    rows = rim_rows - 4
    unpack_strips((part0, part1), spread, place[0], 0)
    for c in range(width // 128):
        rimmed[:, :, :, c * 128 : (c + 1) * 128] = spread[:, :, c].astype(BF16)
    attended[...] = rimmed[:, 2 : rows + 2]
    every = rimmed[...].reshape(count * rim_rows * cols, width)
    dotted = jnp.dot(every, weight[...], preferred_element_type=F32) + bias[...].astype(F32)
    raw[...] = dotted.reshape(count, rim_rows, cols, width)
    branch[...] = raw[:, 2 : rows + 2]
    for l in range(count):
        gate = modulation[l : l + 1, 2 * width : 3 * width]
        offset = modulation[l : l + 1, 3 * width : 4 * width]
        scaling = 1.0 + modulation[l : l + 1, 4 * width : 5 * width]

        def norm_row(r, carry, l=l, gate=gate, offset=offset, scaling=scaling):
            for h in range(0, cols, 16):
                middle = latents[l, r, h : h + 16].astype(F32) + gate * raw[l, r, h : h + 16]
                unit, _ = layer_unit(middle)
                normed[l, r, h : h + 16] = (unit * scaling + offset).astype(BF16)
            return carry

        lax.fori_loop(0, rim_rows, norm_row, 0, unroll=2)


def middle_part(place, parts, latents_rim, modulation, weight, bias):
    count, rim_rows, cols, width = latents_rim.shape
    rows = rim_rows - 4
    return call_whole(
        middle_body,
        (place, *parts, latents_rim, modulation, weight, bias),
        [
            (latents_rim.shape, BF16),
            ((count, rows, cols, width), BF16),
            ((count, rows, cols, width), F32),
        ],
        [(chunked(*latents_rim.shape), F32), (latents_rim.shape, BF16), (latents_rim.shape, F32)],
    )


def turn_body(
    place, branch_two, normed_grad, branch_one, attended, latents, cotangent, modulation, fc2_bias, weight,
    output, middle_grad, weight_grad, sums, bias_sums, out0, out1, branch_grad, spread,
):
    count, rows, cols, width = cotangent.shape
    bias_sums[...] = jnp.zeros_like(bias_sums)
    sums[...] = jnp.zeros_like(sums)
    for l in range(count):
        gate_one, _, scaling, gate_two = (
            modulation[l : l + 1, k * width : (k + 1) * width] for k in range(2, 6)
        )
        scaling = 1.0 + scaling

        def one_row(r, carry, l=l, gate_one=gate_one, scaling=scaling, gate_two=gate_two):
            for h in range(0, cols, 16):
                here = slice(h, h + 16)
                first = branch_one[l, r, here]
                second = branch_two[l, r, here] + fc2_bias[...].astype(F32)
                upstream = cotangent[l, r, here].astype(F32)
                middle = latents[l, r + 2, here].astype(F32) + gate_one * first
                output[l, r, here] = (middle + gate_two * second).astype(BF16)
                unit, inverse = layer_unit(middle)
                grad = normed_grad[l, r, here]
                pulled = upstream + unit_pull(unit, inverse, grad * scaling)
                middle_grad[l, r, here] = pulled
                rounded = (gate_one * pulled).astype(BF16)
                branch_grad[l, r, here] = rounded
                sums[l, 0] += fold_rows(pulled * first)
                sums[l, 1] += fold_rows(grad)
                sums[l, 2] += fold_rows(grad * unit)
                sums[l, 3] += fold_rows(upstream * second)
                bias_sums[0] += fold_rows(rounded.astype(F32))
                bias_sums[1] += fold_rows((gate_two * upstream).astype(BF16).astype(F32))
            return carry

        lax.fori_loop(0, rows, one_row, 0, unroll=2)
    tokens = count * rows * cols
    back = branch_grad[...].reshape(tokens, width)
    weight_grad[...] = lax.dot_general(
        back, attended[...].reshape(tokens, width), (((0,), (0,)), ((), ())), preferred_element_type=F32
    ).astype(BF16)
    raw = lax.dot_general(back, weight[...], (((1,), (1,)), ((), ())), preferred_element_type=F32)
    for c in range(width // 128):
        spread[:, :, c] = raw[:, c * 128 : (c + 1) * 128].reshape(count, rows, cols, 128)
    pack_strips(spread, (out0, out1), place[0])


def turn(place, branch_two, normed_grad, branch_one, attended, latents_rim, cotangent, modulation, fc2_bias, weight):
    count, rows, cols, width = cotangent.shape
    return call_whole(
        turn_body,
        (place, branch_two, normed_grad, branch_one, attended, latents_rim, cotangent, modulation, fc2_bias, weight),
        [
            (cotangent.shape, BF16),
            (cotangent.shape, F32),
            ((width, width), BF16),
            ((count, 4, 8, width), F32),
            ((2, 8, width), F32),
        ]
        + [((2, rows // 2, cols // 2, width), BF16)] * 2,
        [(cotangent.shape, BF16), (chunked(*cotangent.shape), F32)],
    )


def attend_back_body(
    place, up0, up1, part0, part1, projected, log_totals, weight,
    weight_here, weight_away, bias_sums, out0, out1, gathered, upstream, grads, spread, weight_grad,
):
    parts = (part0, part1)
    count, halves, cols, width = part0.shape
    block = halves * cols
    tokens = len(parts) * block
    me = place[0]
    for l in range(count):
        for s, (part, up) in enumerate(zip(parts, (up0, up1))):
            gathered[l, s * block : (s + 1) * block] = part[l].reshape(block, width)
            upstream[l, s * block : (s + 1) * block] = up[l].reshape(block, width)
    bias_sums[...] = jnp.zeros_like(bias_sums)
    lanes = 2 * HEAD
    lane = lax.broadcasted_iota(jnp.int32, (1, lanes), 1)
    turned = (((0,), (0,)), ((), ()))
    inner = (((1,), (1,)), ((), ()))
    for l in range(count):

        def pair(n, carry, l=l):
            here = [pl.ds(pl.multiple_of(k * width + n * lanes, lanes), lanes) for k in range(3)]
            query = projected[l, :, here[0]]
            key = projected[l, :, here[1]]
            value = projected[l, :, here[2]]
            up = upstream[l, :, here[0]]
            query_full = query.astype(F32) * HEAD ** (-0.5)
            up_full = up.astype(F32)
            found = []
            for h in range(2):
                mask = head_mask(lanes, h)
                total = jnp.sum(jnp.where(lane == 2 * n + h, log_totals[l], 0.0), axis=-1, keepdims=True)
                masked = jnp.where(mask, query_full, 0.0).astype(BF16)
                scores = lax.dot_general(masked, key, inner, preferred_element_type=F32)
                weights = jnp.exp(scores - total)
                value_grad = lax.dot_general(weights.astype(BF16), up, turned, preferred_element_type=F32)
                weight_side = lax.dot_general(
                    jnp.where(mask, up_full, 0.0).astype(BF16), value, inner, preferred_element_type=F32
                )
                weighted = jnp.sum(weights * weight_side, axis=-1, keepdims=True)
                score_grad = (weights * (weight_side - weighted)).astype(BF16)
                query_grad = jnp.dot(score_grad, key, preferred_element_type=F32) * HEAD ** (-0.5)
                key_grad = lax.dot_general(score_grad, query, turned, preferred_element_type=F32) * HEAD ** (-0.5)
                found.append((query_grad, key_grad, value_grad))
            mask = head_mask(lanes, 0)
            for k in range(3):
                both = jnp.where(mask, found[0][k], found[1][k]).astype(BF16)
                grads[l, :, here[k]] = both
                if k != 1:
                    bias_sums[k // 2, :, here[0]] += fold_rows(both.astype(F32))
            return carry

        lax.fori_loop(0, width // lanes, pair, 0, unroll=3)
    every = grads[...].reshape(count * tokens, 3 * width)
    weight_grad[...] = lax.dot_general(
        every, gathered[...].reshape(count * tokens, width), turned, preferred_element_type=F32
    ).reshape(weight_grad.shape)
    for j in range(weight_grad.shape[0]):
        weight_here[j] = weight_grad[j, me].astype(BF16)
        weight_away[j] = weight_grad[j, 1 - me].astype(BF16)
    raw = lax.dot_general(every, weight[...], inner, preferred_element_type=F32)
    spread[...] = raw.astype(BF16).reshape(count, len(parts) * halves, cols, width)
    send_rows(spread, (out0, out1), me, halves, me, 0)


def attend_back(place, ups, parts, projected, log_totals, weight):
    count, halves, cols, width = parts[0].shape
    tokens = len(parts) * halves * cols
    batch = lax.axis_size(BATCH)
    half_grad = (batch // 2, 3 * width // batch, width)
    return call_whole(
        attend_back_body,
        (place, *ups, *parts, projected, log_totals, weight),
        [(half_grad, BF16), (half_grad, BF16), ((2, 8, width), F32)] + [((count, halves + 1, cols, width), BF16)] * 2,
        [
            ((count, tokens, width), BF16),
            ((count, tokens, width), BF16),
            ((count, tokens, 3 * width), BF16),
            ((count, len(parts) * halves, cols, width), BF16),
            ((batch // 2, 2, 3 * width // batch, width), F32),
        ],
    )


def finish_body(
    place, part0, part1, latents, modulation, taps, middle_grad, latents_grad, sums, small,
    rimmed, normed, normed_grad,
):
    count, rows, cols, width = middle_grad.shape
    lanes = 128
    unpack_strips((part0, part1), rimmed, place[0], 1)
    for l in range(count):
        offset = modulation[l : l + 1, 0:width]
        scaling = 1.0 + modulation[l : l + 1, width : 2 * width]

        def norm_row(r, carry, l=l, offset=offset, scaling=scaling):
            for h in range(0, cols, 16):
                unit, _ = layer_unit(latents[l, r + 2, h : h + 16].astype(F32))
                normed[l, r, h : h + 16] = (unit * scaling + offset).astype(BF16).astype(F32)
            return carry

        lax.fori_loop(0, rows, norm_row, 0, unroll=2)
    for start in range(0, width, lanes):
        here = slice(start, start + lanes)
        tap = [taps[k : k + 1, here].astype(F32) for k in range(9)]
        found = tuple(jnp.zeros((8, lanes), F32) for _ in range(10))
        for l in range(count):

            def conv_row(r, found, l=l, here=here, tap=tap):
                near = [rimmed[l, r + 2 - a, here.start // lanes] for a in range(3)]
                parts = [sum(tap[3 * a + e] * near[a] for a in range(3)) for e in range(3)]
                normed_grad[l, r, :, here] = row_shift(parts[0], -1) + parts[1] + row_shift(parts[2], 1)
                value = normed[l, r, :, here]
                moved = [row_shift(value, 1), value, row_shift(value, -1)]
                added = [found[3 * a + e] + fold_rows(near[a] * moved[e]) for a in range(3) for e in range(3)]
                return tuple(added) + (found[9] + fold_rows(near[1]),)

            found = lax.fori_loop(0, rows, conv_row, found, unroll=2)
        for k in range(10):
            small[k : k + 1, here] = jnp.sum(found[k], axis=0, keepdims=True)
    sums[...] = jnp.zeros_like(sums)
    for l in range(count):
        scaling = 1.0 + modulation[l : l + 1, width : 2 * width]

        def pull_row(r, carry, l=l, scaling=scaling):
            for h in range(0, cols, 16):
                here = slice(h, h + 16)
                unit, inverse = layer_unit(latents[l, r + 2, here].astype(F32))
                grad = normed_grad[l, r, here]
                sums[l, 0] += fold_rows(grad)
                sums[l, 1] += fold_rows(grad * unit)
                pulled = middle_grad[l, r, here] + unit_pull(unit, inverse, grad * scaling)
                latents_grad[l, r, here] = pulled.astype(BF16)
            return carry

        lax.fori_loop(0, rows, pull_row, 0, unroll=4)


def finish(place, parts, latents_rim, modulation, taps, middle_grad):
    count, rows, cols, width = middle_grad.shape
    return call_whole(
        finish_body,
        (place, *parts, latents_rim, modulation, taps, middle_grad),
        [(middle_grad.shape, BF16), ((count, 2, 8, width), F32), ((16, width), F32)],
        [(chunked(count, rows + 2, cols, width), F32), (middle_grad.shape, F32), (middle_grad.shape, F32)],
    )


def fold_body(pieces, sources, outputs, *refs):
    mine = refs[0]
    heres, aways = refs[1 : 1 + sources], refs[1 + sources : 1 + 2 * sources]
    kept, sent = refs[1 + 2 * sources :][:outputs], refs[1 + 2 * sources + outputs :][:outputs]
    scratch = list(refs[1 + 2 * sources + 2 * outputs :])
    for source, row, rows, lane, lead, bit, out, out_row, out_lane in pieces:
        here, away = heres[source], aways[source]
        size = rows // (2 * lead)
        lanes, out_lanes = slice(lane, lane + FOLD), slice(out_lane, out_lane + FOLD)
        me = mine[bit]
        if size % 16:
            whole = scratch.pop(0)
            total = here[row : row + rows, lanes].astype(F32) + away[row : row + rows, lanes].astype(F32)
            whole[...] = total.reshape(lead, 2, size, FOLD)
            for side, place in ((kept, me), (sent, 1 - me)):
                picked = whole[:, place].reshape(lead * size, FOLD).astype(BF16)
                side[out][out_row : out_row + lead * size, out_lanes] = picked
            continue
        part = max(p for p in range(16, 97, 16) if size % p == 0)

        def one(n, carry, here=here, away=away, row=row, size=size, part=part, lanes=lanes, out=out,
                out_row=out_row, out_lanes=out_lanes, me=me):
            a, k = n // (size // part), n % (size // part)
            target = pl.ds(pl.multiple_of(out_row + a * size + k * part, 16), part)
            for side, place in ((kept, me), (sent, 1 - me)):
                origin = pl.ds(pl.multiple_of(row + (2 * a + place) * size + k * part, 16), part)
                total = here[origin, lanes].astype(F32) + away[origin, lanes].astype(F32)
                side[out][target, out_lanes] = total.astype(BF16)
            return carry

        lax.fori_loop(0, lead * size // part, one, 0)


FOLD = 768


def fold(pairs, bits, pieces, outs):
    mine = jnp.stack([(lax.axis_index(axis) >> bit) & 1 for axis, bit in bits]).astype(jnp.int32)
    scratch = [(p[4], 2, p[2] // (2 * p[4]), FOLD) for p in pieces if p[2] // (2 * p[4]) % 16]
    found = call_whole(
        partial(fold_body, pieces, len(pairs), len(outs)),
        (mine, *[pair[0] for pair in pairs], *[pair[1] for pair in pairs]),
        [(shape, BF16) for shape in outs] * 2,
        [(shape, F32) for shape in scratch],
    )
    return list(zip(found[: len(outs)], found[len(outs) :]))


def swap(pair, axis, bit):
    return pair[0], swap_bit(pair[1], axis, bit)


def quick_sums():
    return lax.axis_size(BATCH) == 8 and lax.axis_size(GRP) == 4


def exchange(parts):
    return parts[0], swap_bit(parts[1], BATCH, 0)


def on_device(
    latents,
    cotangent,
    timesteps,
    labels,
    time_weight,
    time_bias,
    label_table,
    ada_weight,
    ada_bias,
    conv_a,
    conv_a_bias,
    qkv_weight,
    qv_bias,
    proj_weight,
    proj_bias,
    fc1_weight,
    fc1_bias,
    conv_f,
    conv_f_bias,
    fc2_weight,
    fc2_bias,
):
    width = latents.shape[3]
    hidden_width = fc1_weight.shape[1]
    devices = lax.axis_size(BATCH) * lax.axis_size(GRP)
    slot = lax.axis_index(BATCH) * lax.axis_size(GRP) + lax.axis_index(GRP)

    strip = lax.axis_index(GRP)
    half = lax.axis_index(BATCH) & 1
    inside = jnp.stack([half == 1, half == 0])
    place = jnp.concatenate([half[None], inside.astype(jnp.int32)])
    numbers = jnp.stack([timesteps.astype(F32), labels.astype(F32)])
    other = swap_bit(numbers, BATCH, 0)
    numbers = jnp.where(half == strip >> 1, numbers, other)
    numbers = jnp.where((strip & 1) == 0, numbers[:, 0], numbers[:, 1])
    latents_rim = with_edges(to_pairs(latents), 2)
    cotangent = to_pairs(cotangent)
    cotangent_rim = with_edges(cotangent, 1)

    frequency_rows = sinusoid(numbers[:1], time_weight.shape[0])
    condition = exact_dot(frequency_rows, time_weight) + time_bias.astype(F32)
    picked = lax.dynamic_slice_in_dim(label_table, numbers[1].astype(jnp.int32), 1, axis=0)
    condition = condition + picked.astype(F32)
    active = condition * jax.nn.sigmoid(condition)
    modulation = exact_dot(active, ada_weight) + ada_bias.astype(F32)
    gate_two = modulation[:, None, None, 5 * width :]

    mixed = exchange(stem(place, latents_rim, modulation, conv_a, conv_a_bias))
    qkv_bias = jnp.concatenate([qv_bias[0:1], jnp.zeros_like(qv_bias[0:1]), qv_bias[1:2]], axis=1)
    *sent, projected, log_totals = attend(place, mixed, qkv_weight, qkv_bias)
    normed_rim, attended, branch_one = middle_part(
        place, exchange(sent), latents_rim, modulation, proj_weight, proj_bias
    )

    branch_two_rim = (gate_two * cotangent_rim.astype(F32)).astype(BF16)
    branch_two, normed_two_grad, fc1_here, fc1_away, fc2_here, fc2_away, ff_small = feed_forward(
        place, normed_rim, branch_two_rim, fc1_weight, fc1_bias, conv_f, conv_f_bias, fc2_weight
    )
    pairs = lax.axis_size(BATCH) // 2
    quick = quick_sums()
    fc1_pair = (fc1_here.reshape(-1, width), fc1_away.reshape(-1, width))
    fc2_pair = (fc2_here.reshape(-1, hidden_width), fc2_away.reshape(-1, hidden_width))
    fc1_pair = swap(fc1_pair, BATCH, 0)
    fc2_pair = swap(fc2_pair, BATCH, 0)
    lanes = range(0, hidden_width, width)
    near, far, by_x, by_y = (GRP, 0), (GRP, 1), (BATCH, 1), (BATCH, 2)
    if quick:
        fc1_rows, fc2_rows = fc1_pair[0].shape[0], fc2_pair[0].shape[0]
        fc1_pair, fc2_pair = fold(
            [fc1_pair, fc2_pair],
            [by_x, near],
            [(0, 0, fc1_rows, 0, 2, 0, 0, 0, 0)] + [(1, 0, fc2_rows, c, 8, 1, 1, 0, c) for c in lanes],
            [(fc1_rows // 2, width), (fc2_rows // 2, hidden_width)],
        )
        fc1_pair = swap(fc1_pair, *by_x)
        fc2_pair = swap(fc2_pair, *near)
    else:
        fc1_sum, fc2_sum = (
            scatter_rest((pair[0].astype(F32) + pair[1].astype(F32)).reshape(pairs, -1, pair[0].shape[1]), flip)
            for pair, flip in ((fc1_pair, False), (fc2_pair, True))
        )

    output, middle_grad, proj_grad, turn_sums, turn_bias, *sent = turn(
        place,
        branch_two.reshape(cotangent.shape),
        normed_two_grad.reshape(cotangent.shape),
        branch_one,
        attended,
        latents_rim,
        cotangent,
        modulation,
        fc2_bias,
        proj_weight,
    )
    output = from_pairs(output)
    turn_sums = jnp.sum(turn_sums, axis=2)
    turn_bias = jnp.sum(turn_bias, axis=1)

    def slots(vectors):
        return vectors.reshape(len(vectors), devices, -1).transpose(1, 0, 2).reshape(devices, -1)

    small = jnp.concatenate([slots(ff_small[:11]), slots(turn_bias)], axis=1).astype(BF16)
    small_length = small.shape[1]
    small_lanes = -(-small_length // 8)
    small = jnp.pad(small, ((0, 0), (0, small_lanes * 8 - small_length))).reshape(devices, 8, small_lanes)
    small = jnp.pad(small, ((0, 0), (0, 0), (0, width - small_lanes)))
    beside = jnp.concatenate([proj_grad.reshape(devices, -1, width), small], axis=1).reshape(pairs, 2, -1, width)
    beside_pair = tuple(
        lax.dynamic_index_in_dim(beside, side, 1, keepdims=False).reshape(-1, width) for side in (half, 1 - half)
    )
    beside_pair = swap(beside_pair, BATCH, 0)

    qkv_here, qkv_away, qv_sums, *sent = attend_back(
        place, exchange(sent), mixed, projected, log_totals, qkv_weight
    )
    qkv_pair = swap((qkv_here.reshape(-1, width), qkv_away.reshape(-1, width)), BATCH, 0)
    if quick:
        beside_rows, qkv_rows = beside_pair[0].shape[0], qkv_pair[0].shape[0]
        fc1_pair, fc2_pair, beside_pair = fold(
            [fc1_pair, fc2_pair, beside_pair],
            [by_y, far, by_x],
            [(0, 0, fc1_rows // 2, 0, 1, 0, 0, 0, 0)]
            + [(1, 0, fc2_rows // 2, c, 4, 1, 1, 0, c) for c in lanes]
            + [(2, 0, beside_rows, 0, 2, 2, 2, 0, 0)],
            [(fc1_rows // 4, width), (fc2_rows // 4, hidden_width), (beside_rows // 2, width)],
        )
        fc1_pair = swap(fc1_pair, *by_y)
        fc2_pair = swap(fc2_pair, *far)
        beside_pair = swap(beside_pair, *by_x)
        (qkv_pair,) = fold([qkv_pair], [by_x], [(0, 0, qkv_rows, 0, 2, 0, 0, 0, 0)], [(qkv_rows // 2, width)])
        qkv_pair = swap(qkv_pair, *by_x)
    else:
        beside, qkv_sum = (
            scatter_rest((pair[0].astype(F32) + pair[1].astype(F32)).reshape(pairs, -1, width), flip)
            for pair, flip in ((beside_pair, False), (qkv_pair, True))
        )
    latents_grad, finish_sums, conv_a_small = finish(
        place, exchange(sent), latents_rim, modulation, conv_a, middle_grad
    )
    latents_grad = from_pairs(latents_grad)
    if quick:
        fc1_rows, fc2_rows, beside_rows, qkv_rows = fc1_rows // 4, fc2_rows // 4, beside_rows // 2, qkv_rows // 2
        fc1_pair, fc2_pair = fold(
            [fc1_pair, fc2_pair],
            [near, by_x],
            [(0, 0, fc1_rows, 0, 2, 0, 0, 0, 0)]
            + [(1, 0, fc2_rows, c, 2, 1, 1, k * (fc2_rows // 2), 0) for k, c in enumerate(lanes)],
            [(fc1_rows // 2, width), (len(lanes) * fc2_rows // 2, width)],
        )
        fc1_pair = swap(fc1_pair, *near)
        fc2_pair = swap(fc2_pair, *by_x)
        (attention_pair,) = fold(
            [beside_pair, qkv_pair],
            [by_y],
            [(0, 0, beside_rows, 0, 1, 0, 0, 0, 0), (1, 0, qkv_rows, 0, 1, 0, 0, beside_rows // 2, 0)],
            [((beside_rows + qkv_rows) // 2, width)],
        )
        attention_pair = swap(attention_pair, *by_y)
        fc1_rows, fc2_rows = fc1_rows // 2, len(lanes) * fc2_rows // 2
        beside_rows, qkv_rows = beside_rows // 2, qkv_rows // 2
        fc1_pair, fc2_pair, attention_pair = fold(
            [fc1_pair, fc2_pair, attention_pair],
            [far, by_y, near],
            [
                (0, 0, fc1_rows, 0, 1, 0, 0, 0, 0),
                (1, 0, fc2_rows, 0, len(lanes), 1, 1, 0, 0),
                (2, 0, beside_rows, 0, 2, 2, 2, 0, 0),
                (2, beside_rows, qkv_rows, 0, 2, 2, 2, beside_rows // 2, 0),
            ],
            [(fc1_rows // 2, width), (fc2_rows // 2, width), ((beside_rows + qkv_rows) // 2, width)],
        )
        fc1_pair = swap(fc1_pair, *far)
        fc2_pair = swap(fc2_pair, *by_y)
        attention_pair = swap(attention_pair, *near)
        beside_rows, qkv_rows = beside_rows // 2, qkv_rows // 2
        (attention_pair,) = fold(
            [attention_pair],
            [far],
            [(0, 0, beside_rows, 0, 1, 0, 0, 0, 0), (0, beside_rows, qkv_rows, 0, 1, 0, 0, beside_rows // 2, 0)],
            [((beside_rows + qkv_rows) // 2, width)],
        )
        attention_pair = swap(attention_pair, *far)
        fc1_sum, fc2_sum, attention_sum = (
            pair[0].astype(F32) + pair[1].astype(F32) for pair in (fc1_pair, fc2_pair, attention_pair)
        )
        fc2_sum = fc2_sum.reshape(len(lanes), -1, width).transpose(1, 0, 2).reshape(-1, hidden_width)
        beside, qkv_sum = attention_sum[: beside_rows // 2], attention_sum[beside_rows // 2 :]
    proj_sum = beside[:-8]
    small_sum = beside[-8:, :small_lanes].reshape(-1)
    wide_length = 11 * (hidden_width // devices)
    wide_sum = small_sum[:wide_length].reshape(11, -1)
    narrow_sum = small_sum[wide_length:small_length].reshape(2, -1)
    finish_sums = jnp.sum(finish_sums, axis=2)

    late = jnp.concatenate([conv_a_small[:10], jnp.sum(qv_sums, axis=1), jnp.zeros((4, width), F32)], axis=0)
    modulation_grad = jnp.concatenate([finish_sums[0], turn_sums[0], jnp.zeros((2, width), F32)], axis=0)
    side = jnp.concatenate(
        [condition, jnp.pad(frequency_rows, ((0, 0), (0, width - frequency_rows.shape[1] - 1))), numbers[1:][None]],
        axis=1,
    )
    every, late_sum = gather_sum(jnp.pad(side.reshape(2, width), ((6, 0), (0, 0))), modulation_grad, late)
    every = every.reshape(-1, 8, width)
    every_grad = every[:, :6].reshape(-1, 6 * width)
    every_condition = every[:, 6]
    every_frequency = every[:, 7, : frequency_rows.shape[1]]
    every_label = every[:, 7, -1].astype(jnp.int32)
    late_sum = lax.dynamic_slice_in_dim(late_sum, slot * (width // devices), width // devices, axis=1)
    sigmoid = jax.nn.sigmoid(every_condition)
    every_active = every_condition * sigmoid
    narrow_width = width // devices
    ada_width = 6 * width // devices
    ada_part = lax.dynamic_slice_in_dim(every_grad, slot * ada_width, ada_width, axis=1)
    ada_grad = lax.dot_general(
        every_active, ada_part, (((0,), (0,)), ((), ())), precision=HIGHEST, preferred_element_type=F32
    )
    ada_bias_grad = jnp.sum(ada_part, axis=0)[None, :]
    ada_rows = lax.dynamic_slice_in_dim(ada_weight, slot * narrow_width, narrow_width, axis=0)
    active_grad = lax.dot_general(
        every_grad, ada_rows.astype(F32), (((1,), (1,)), ((), ())), precision=HIGHEST
    )
    slope_silu = lax.dynamic_slice_in_dim(
        sigmoid * (1.0 + every_condition * (1.0 - sigmoid)), slot * narrow_width, narrow_width, axis=1
    )
    condition_grad = active_grad * slope_silu
    onehot = (every_label[:, None] == jnp.arange(label_table.shape[0], dtype=jnp.int32)[None, :]).astype(F32)
    table_grad = lax.dot_general(onehot, condition_grad, (((0,), (0,)), ((), ())), precision=HIGHEST)
    time_grad = lax.dot_general(
        every_frequency, condition_grad, (((0,), (0,)), ((), ())), precision=HIGHEST
    )
    time_bias_grad = jnp.sum(condition_grad, axis=0)[None, :]

    return (
        output,
        latents_grad,
        time_grad,
        time_bias_grad,
        table_grad,
        ada_grad,
        ada_bias_grad,
        late_sum[0:9],
        late_sum[9:10],
        qkv_sum.T,
        late_sum[10:12],
        proj_sum.T,
        narrow_sum[0:1],
        fc1_sum.T,
        wide_sum[10:11],
        wide_sum[0:9],
        wide_sum[9:10],
        fc2_sum.T,
        narrow_sum[1:2],
    )


def solution(mesh):
    columns = P(None, (BATCH, GRP))
    return jax.shard_map(
        on_device,
        mesh=mesh,
        in_specs=(P(BATCH, GRP, None, None), P(BATCH, GRP, None, None), P(BATCH), P(BATCH)) + (P(),) * 17,
        out_specs=(P(BATCH, GRP, None, None), P(BATCH, GRP, None, None)) + (columns,) * 17,
        check_vma=False,
    )
```
